32 devices in a mesh: dp: 8 (over z, x), tp: 4 (over y, core).
Axes of the slice: x: 2, y: 2, z: 4, core: 2. Of those that a mesh axis runs over, the one named last changes fastest.
Arguments:
- tokens: bfloat16 [8, 4096, 512], P('dp', 'tp'), may hold values from -6 to 6
- segment_ids: int32 [8, 4096], P('dp', 'tp'), may hold values from 0 to 15, never falling along the last dimension, each value on 1 to 2048 neighbouring positions
- grad_out: bfloat16 [8, 4096, 512], P('dp', 'tp'), may hold values from -6 to 6
- w_query: bfloat16 [512, 512], replicated, may hold values from -0.25 to 0.25
- w_key: bfloat16 [512, 512], replicated, may hold values from -0.25 to 0.25
- w_value: bfloat16 [512, 512], replicated, may hold values from -0.25 to 0.25
- w_out: bfloat16 [512, 512], replicated, may hold values from -1 to 1
- w_up: bfloat16 [512, 2048], P(None, 'tp'), may hold values from -0.25 to 0.25
- w_down: bfloat16 [2048, 512], P('tp'), may hold values from -0.125 to 0.125
- gain_attn: float32 [512], replicated, may hold values from 0.5 to 1.5
- gain_ffn: float32 [512], replicated, may hold values from 0.5 to 1.5
- feature_basis: bfloat16 [8, 64, 256], replicated, may hold values from -4 to 4
Outputs:
- out_tokens: bfloat16 [8, 4096, 512], P('dp', 'tp')
- grad_tokens: float32 [8, 4096, 512], P('dp', 'tp')
- grad_query: float32 [512, 512], replicated
- grad_key: float32 [512, 512], replicated
- grad_value: float32 [512, 512], replicated
- grad_out_proj: float32 [512, 512], replicated
- grad_up: float32 [512, 2048], P(None, 'tp')
- grad_down: float32 [2048, 512], P('tp')
- grad_gain_attn: float32 [512], replicated
- grad_gain_ffn: float32 [512], replicated
The draws below stay inside these ranges and needn't reach their ends.
Inputs may be any that keep to these rules, and one draw needn't show every extreme that they name: `segment_ids`: each row numbers its packed proteins 0 to 15 in order, never falling; each protein takes 1 to 2048 positions and one takes exactly 2048.
All inputs are finite; a program needn't handle non-finite values.
Results may differ from the reference program's by a relative error of at most 0.02.
Values may be sent and summed in bfloat16 or wider, within the bound.
A program may use at most 256 MiB of HBM per device.

```python
import math
import jax
import jax.numpy as jnp
import numpy as np
from jax import lax

D = 512
H = 8
DH = 64
M = 256
FF = 2048
BLK = 512
SEGS = 16
LEN = 4096
SEQS = 8


def shard_levels(stream_key, dims, cuts, low, high):
    def one(position, blocks):
        steps = jax.random.uniform(jax.random.fold_in(jax.random.fold_in(stream_key, 6), position), (blocks,), jnp.float32, low / len(cuts), high / len(cuts))
        return jnp.repeat(jnp.exp(steps), dims[position] // blocks).reshape((-1,) + (1,) * (len(dims) - position - 1))

    factor_of = one(*cuts[0])
    for cut in cuts[1:]:
        factor_of = factor_of * one(*cut)
    return factor_of


def length_profile(number_of, total, reach, slope):
    weights = [(1 << 20) // math.isqrt(grade ** slope) + 1 for grade in range(2, number_of + 1)]
    rest, counts = total - reach - (number_of - 1), [1] * (number_of - 1)
    while rest > 0:
        candidates = [i for i in range(number_of - 1) if counts[i] < reach]
        pool, budget = sum([weights[i] for i in candidates]), rest
        for i in candidates:
            addition = min(reach - counts[i], max(1, budget * weights[i] // pool), rest)
            counts[i] = counts[i] + addition
            rest = rest - addition
    return np.array([reach] + counts)


def ragged(stream_key, number_of, total, limit, slope):
    if number_of == 2:
        one = jax.random.randint(stream_key, (), max(1, total - limit), min(limit, total - 1) + 1)
        return jnp.stack([one, total - one])
    lengths = jnp.asarray(length_profile(number_of, total, limit, slope), jnp.int32)
    pairs = (number_of - 1) // 2
    giver, taker = lengths[1:1 + 2 * pairs:2], lengths[2:2 + 2 * pairs:2]
    room = jnp.minimum(giver - 1, limit - taker)
    moved = jax.random.randint(jax.random.fold_in(stream_key, 1), (pairs,), 0, 1 << 20) % (room + 1)
    lengths = lengths.at[1:1 + 2 * pairs:2].set(giver - moved).at[2:2 + 2 * pairs:2].set(taker + moved)
    return lengths[jax.random.permutation(jax.random.fold_in(stream_key, 2), number_of)]


def gaussian(stream_key, shape, scale, reach, pieces=(), kind=jnp.bfloat16):
    values = jax.random.normal(stream_key, shape, jnp.float32) * scale
    if len(pieces) > 0:
        values = shard_levels(stream_key, shape, pieces, -0.22, 0.18) * values
    return jnp.clip(values, min=-reach, max=reach).astype(kind)


def setup_inputs(seed: int = 0) -> dict:
    arg_keys = jax.random.split(jax.random.key(seed), 13)
    return {
        "tokens": gaussian(arg_keys[0], (SEQS, LEN, D), 1.0, 6.0, ((0, 8), (1, 4))),
        "segment_ids": jax.vmap(lambda own: jnp.searchsorted(jnp.cumsum(ragged(own, SEGS, LEN, LEN // 2, 1)), jnp.arange(LEN), side="right"))(jax.random.split(arg_keys[1], SEQS)).reshape((SEQS, LEN)).astype(jnp.int32),
        "grad_out": gaussian(arg_keys[2], (SEQS, LEN, D), 1.0, 6.0, ((0, 8), (1, 4))),
        "w_query": gaussian(arg_keys[3], (D, D), D ** -0.5, 0.25),
        "w_key": gaussian(arg_keys[4], (D, D), D ** -0.5, 0.25),
        "w_value": gaussian(arg_keys[5], (D, D), D ** -0.5, 0.25),
        "w_out": gaussian(arg_keys[6], (D, D), (D // 16) ** -0.5, 1.0),
        "w_up": gaussian(arg_keys[7], (D, FF), D ** -0.5, 0.25, ((1, 4),)),
        "w_down": gaussian(arg_keys[8], (FF, D), FF ** -0.5, 0.125, ((0, 4),)),
        "gain_attn": jnp.clip(1.0 + 0.1 * jax.random.normal(arg_keys[9], (D,), jnp.float32), 0.5, 1.5),
        "gain_ffn": jnp.clip(1.0 + 0.1 * jax.random.normal(arg_keys[10], (D,), jnp.float32), 0.5, 1.5),
        "feature_basis": gaussian(arg_keys[11], (H, DH, M), 1.0, 4.0),
    }


@jax.custom_vjp
def low(v):
    return lax.optimization_barrier(v.astype(jnp.bfloat16)).astype(jnp.float32)

@jax.custom_vjp
def low_back(v):
    return v

def low_keep(v):
    return (low(v), None)

def low_pass(kept, grad):
    return (grad,)

def back_keep(v):
    return (v, None)

def back_low(kept, grad):
    return (low(grad),)
low.defvjp(low_keep, low_pass)
low_back.defvjp(back_keep, back_low)
NORM_EPS = 1e-05
GELU_SCALE = 0.7978845608028654
GELU_CUBIC = 0.044715
PRECISE = lax.Precision.HIGHEST

def matmul(left, right):
    return jnp.dot(left, right, precision=PRECISE, preferred_element_type=jnp.float32)

def layer_norm(row_data, gain_vec):
    row_mean = lax.optimization_barrier(jnp.mean(row_data, axis=-1, keepdims=True))
    centred = row_data - row_mean
    inv_scale = lax.rsqrt(lax.optimization_barrier(jnp.mean(centred * centred, axis=-1, keepdims=True)) + NORM_EPS)
    return centred * inv_scale * gain_vec

def gelu_value(pre_act):
    inner_arg = GELU_SCALE * (pre_act + GELU_CUBIC * pre_act * pre_act * pre_act)
    return 0.5 * pre_act * (1.0 + jnp.tanh(inner_arg))

def feature_map(projected, feature_basis):
    exponent = jnp.einsum('lhd,hdm->lhm', projected, feature_basis, precision=PRECISE) * DH ** (-0.25)
    square = lax.optimization_barrier(jnp.sum(projected * projected, axis=-1, keepdims=True)) * (0.5 / math.sqrt(DH))
    return low(jnp.exp(low_back(exponent) - square))

def block_step(carry, block_in):
    carry_state, carry_keys = carry
    phi_q_blk, phi_k_blk, values_blk, seg_blk, before = block_in
    row_ids = jnp.arange(BLK)
    allowed = (row_ids[:, None] >= row_ids[None, :]) & (seg_blk[:, None] == seg_blk[None, :])
    mask_vals = allowed.astype(jnp.float32)
    scores = jnp.einsum('ihm,jhm->hij', phi_q_blk, phi_k_blk, precision=PRECISE)
    masked = low_back(scores * mask_vals[None])
    numerator = jnp.einsum('hij,jhd->ihd', low(masked), values_blk, precision=PRECISE)
    denominator = lax.optimization_barrier(jnp.sum(masked, axis=2)).T
    use_carry = (seg_blk == before).astype(jnp.float32)
    numerator = numerator + jnp.einsum('ihm,hdm->ihd', phi_q_blk, low(carry_state), precision=PRECISE) * use_carry[:, None, None]
    denominator = denominator + jnp.einsum('ihm,hm->ih', phi_q_blk, low(carry_keys), precision=PRECISE) * use_carry[:, None]
    numerator = low_back(numerator)
    denominator = low_back(denominator)
    result = numerator / denominator[:, :, None]
    last_seg = seg_blk[BLK - 1]
    keep_carry = (before == last_seg).astype(jnp.float32)
    tail_rows = (seg_blk == last_seg).astype(jnp.float32)
    tail_keys = phi_k_blk * tail_rows[:, None, None]
    carry_state = keep_carry * carry_state + low_back(jnp.einsum('jhm,jhd->hdm', tail_keys, values_blk, precision=PRECISE))
    carry_keys = keep_carry * carry_keys + lax.optimization_barrier(jnp.sum(tail_keys, axis=0))
    return ((carry_state, carry_keys), result)

def attend(phi_q, phi_k, value_proj, segment):
    block_count = LEN // BLK
    seg_blocks = segment.reshape(block_count, BLK)
    befores = jnp.concatenate([jnp.full((1,), -1, jnp.int32), seg_blocks[:-1, BLK - 1].astype(jnp.int32)])
    block_in = (phi_q.reshape(block_count, BLK, H, M), phi_k.reshape(block_count, BLK, H, M), value_proj.reshape(block_count, BLK, H, DH), seg_blocks, befores)
    start = (jnp.zeros((H, DH, M), jnp.float32), jnp.zeros((H, M), jnp.float32))
    _, result = lax.scan(jax.checkpoint(block_step), start, block_in)
    return result.reshape(LEN, D)

def sequence(x_seq, segment, w_query, w_key, w_value, w_out, w_up, w_down, gain_attn, gain_ffn, feature_basis):
    hidden_attn = low(layer_norm(x_seq, gain_attn))
    queries = low_back(low(matmul(hidden_attn, w_query))).reshape(LEN, H, DH)
    key_proj = low_back(low(matmul(hidden_attn, w_key))).reshape(LEN, H, DH)
    value_proj = low_back(low(matmul(hidden_attn, w_value))).reshape(LEN, H, DH)
    phi_q = feature_map(queries, feature_basis)
    phi_k = feature_map(key_proj, feature_basis)
    mixed_heads = attend(phi_q, phi_k, value_proj, segment)
    residual = x_seq + low_back(matmul(low(mixed_heads), w_out))
    hidden_ffn = low(layer_norm(residual, gain_ffn))
    up_proj = low_back(matmul(hidden_ffn, w_up))
    return residual + low_back(matmul(low(gelu_value(up_proj)), w_down))

def reference(tokens, segment_ids, grad_out, w_query, w_key, w_value, w_out, w_up, w_down, gain_attn, gain_ffn, feature_basis):
    basis_wide = feature_basis.astype(jnp.float32)

    def forward(tokens_f, wq_f, wk_f, wv_f, wo_f, wu_f, wd_f, ga_f, gf_f):

        def one_sequence(carry, seq_pair):
            x_seq, segment = seq_pair
            seq_out = jax.checkpoint(sequence)(x_seq, segment, wq_f, wk_f, wv_f, wo_f, wu_f, wd_f, ga_f, gf_f, basis_wide)
            return (carry, seq_out)
        _, seq_outs = lax.scan(one_sequence, jnp.zeros((), jnp.float32), (tokens_f, segment_ids))
        return seq_outs
    result, pullback = jax.vjp(forward, tokens.astype(jnp.float32), w_query.astype(jnp.float32), w_key.astype(jnp.float32), w_value.astype(jnp.float32), w_out.astype(jnp.float32), w_up.astype(jnp.float32), w_down.astype(jnp.float32), gain_attn.astype(jnp.float32), gain_ffn.astype(jnp.float32))
    grads = pullback(grad_out.astype(jnp.float32))
    return (result.astype(jnp.bfloat16), grads[0], grads[1], grads[2], grads[3], grads[4], grads[5], grads[6], grads[7], grads[8])
```

```python
import functools
import math
from types import SimpleNamespace

import jax
import jax.numpy as jnp
from jax import lax
from jax.experimental import pallas as pl
from jax.experimental.pallas import tpu as pltpu
from jax.sharding import PartitionSpec as P

MESH = pl.DeviceIdType.MESH
F32 = jnp.float32
BF16 = jnp.bfloat16
NORM_EPS = 1e-05
GELU_SCALE = 0.7978845608028654
GELU_CUBIC = 0.044715
LANES = 128
T = 256


def dot(a, b):
    return jnp.dot(a, b, preferred_element_type=F32)


def dot_t(a, b):
    return lax.dot_general(a, b, (((1,), (1,)), ((), ())), preferred_element_type=F32)


def dot_c(a, b):
    return lax.dot_general(a, b, (((0,), (0,)), ((), ())), preferred_element_type=F32)


def rows_at(start, size):
    return pl.ds(pl.multiple_of(start, 16), size)


def cat(parts, axis):
    return jnp.concatenate(parts, axis=axis)


def lane_groups():
    lane = lax.broadcasted_iota(jnp.int32, (1, 2 * LANES), 1)
    first = lax.rem(lane, LANES) < 64
    one = jnp.where(first, 1.0, 0.0)
    return one.astype(BF16), (1.0 - one).astype(BF16)


def layer_kernel(nz, names, *refs):
    r = SimpleNamespace(**dict(zip(names, refs)))
    L, D = r.tok.shape
    nt = L // T
    npair = r.basis.shape[0] // 2
    M = r.basis.shape[2]
    c4 = 64.0**-0.25
    exp_scale = c4 * math.log2(math.e)

    dp, tp = lax.axis_index("dp"), lax.axis_index("tp")
    ndp = 2 * nz
    core, ybit = lax.rem(tp, 2), lax.div(tp, 2)
    xbit, zi = lax.rem(dp, 2), lax.div(dp, 2)
    tp_core, tp_y, tp_far = tp + 1 - 2 * core, lax.rem(tp + 2, 4), 3 - tp
    dev_core, dev_y, dev_far = (dp, tp_core), (dp, tp_y), (dp, tp_far)
    dev_x = (dp + 1 - 2 * xbit, tp)

    def z_at(k):
        return lax.rem(zi + k, nz)

    def dev_z(k):
        return (z_at(k) * 2 + xbit, tp)

    used = [0]
    pending = []

    def sems(n):
        first = used[0]
        used[0] += n
        return first

    def remote(src, dst, idx, dev):
        return pltpu.make_async_remote_copy(
            src_ref=src, dst_ref=dst, send_sem=r.ss.at[idx], recv_sem=r.rs.at[idx],
            device_id=dev, device_id_type=MESH,
        )

    barrier = pltpu.get_barrier_semaphore()
    for k in (1, 2, 3):
        pl.semaphore_signal(barrier, inc=1, device_id=(dp, lax.rem(tp + k, 4)), device_id_type=MESH)
    for k in range(1, ndp):
        pl.semaphore_signal(barrier, inc=1, device_id=(lax.rem(dp + k, ndp), tp), device_id_type=MESH)

    own_up = pltpu.make_async_copy(r.wup, r.wu.at[tp], r.ls.at[0])
    own_down = pltpu.make_async_copy(r.wdn, r.wd.at[tp], r.ls.at[1])
    own_seg = pltpu.make_async_copy(r.seg, r.sg.at[tp], r.ls.at[2])
    own_up.start()
    own_down.start()
    own_seg.start()
    pl.semaphore_wait(barrier, 3 + ndp - 1)

    seg_base = sems(3)
    seg_copies = [
        remote(r.seg, r.sg.at[tp], seg_base + k - 1, (dp, lax.rem(tp + k, 4))) for k in (1, 2, 3)
    ]
    for copy in seg_copies:
        copy.start()

    w_base = sems(6)

    def weight_copies(i, mine, full):
        return (
            remote(mine, full.at[tp], w_base + 3 * i, dev_core),
            remote(mine, full.at[tp], w_base + 3 * i + 1, dev_y),
            remote(full.at[tp_y], full.at[tp_y], w_base + 3 * i + 2, dev_core),
        )

    up_core, up_y, up_on = weight_copies(0, r.wup, r.wu)
    down_core, down_y, down_on = weight_copies(1, r.wdn, r.wd)
    up_core.start()
    up_y.start()
    down_core.start()

    for p in range(npair):
        for h in range(2):
            fb = r.basis[2 * p + h]
            zero, one = jnp.zeros((64, M), BF16), jnp.ones((64, M), BF16)
            parts = [fb, zero, one, zero] if h == 0 else [zero, fb, zero, one]
            r.bb[p, :, h * M : (h + 1) * M] = cat(parts, 0)

    low, high = lane_groups()

    def project(t, _):
        rows = rows_at(t * T, T)
        x = r.tok[rows, :].astype(F32)
        mean = jnp.mean(x, axis=-1, keepdims=True)
        cen = x - mean
        inv = lax.rsqrt(jnp.mean(cen * cen, axis=-1, keepdims=True) + NORM_EPS)
        hid = ((cen * inv) * r.ga[...]).astype(BF16)
        r.ht[:, pl.ds(pl.multiple_of(t * T, LANES), T)] = hid.T
        k = dot(hid, r.wk[...]).astype(BF16)
        v = dot(hid, r.wv[...]).astype(BF16)
        q = dot(hid, r.wq[...]).astype(BF16)
        for p in range(npair):
            lanes = slice(p * LANES, (p + 1) * LANES)
            r.q[p, rows, :] = q[:, lanes]
            r.k[p, rows, :] = k[:, lanes]
            r.vp[p, rows, :LANES] = v[:, lanes]
            r.vp[p, rows, LANES:] = jnp.ones((T, LANES), BF16)
        return 0

    lax.fori_loop(0, nt, project, 0)

    own_seg.wait()
    for copy in seg_copies:
        copy.wait_recv()
    row_max, row_min = [], []
    for j in range(4):
        ids = r.sg[j].astype(F32)
        row_max.append(jnp.max(ids, axis=1, keepdims=True))
        row_min.append(jnp.min(ids, axis=1, keepdims=True))
    in_seg = jnp.full((1, 1), -1.0, F32)
    for j in range(4):
        in_seg = jnp.maximum(in_seg, jnp.where(j < tp, row_max[j], -1.0))
    mine = r.seg[...].astype(F32)
    ends = [jnp.max(mine[:, c * T : (c + 1) * T], axis=1, keepdims=True) for c in range(nt)]
    befores = [in_seg] + ends[:-1]
    keeps = [(befores[c] == ends[c]).astype(F32) for c in range(nt)]
    wide = lambda v: jnp.broadcast_to(v, (1, M))
    flag = jnp.ones((1, 1), F32)
    for c in range(nt):
        r.sc[c] = wide(keeps[c])
        r.sc[nt + c] = wide(flag)
        flag = flag * keeps[c]
    flag = jnp.ones((1, 1), F32)
    for c in reversed(range(nt)):
        r.sc[2 * nt + c] = wide(flag)
        flag = flag * keeps[c]
    for j in range(4):
        r.sc[3 * nt + j] = wide(jnp.where(j < tp, (row_max[j] == in_seg).astype(F32), 0.0))
        r.sc[3 * nt + 4 + j] = wide(jnp.where(j > tp, (row_min[j] == ends[-1]).astype(F32), 0.0))
    row_id = lax.broadcasted_iota(jnp.int32, (T, T), 0)
    col_id = lax.broadcasted_iota(jnp.int32, (T, T), 1)
    for c in range(nt):
        along = mine[:, c * T : (c + 1) * T]
        down = jnp.broadcast_to(along, (LANES, T)).T
        rows = slice(c * T, (c + 1) * T)
        use = (down == befores[c]).astype(F32).astype(BF16)
        tail = (down == ends[c]).astype(F32).astype(BF16)
        r.use[rows, :] = use
        r.tail[rows, :] = tail
        same = (cat([down, down], 1) == along).astype(F32)
        mask = (same * (row_id >= col_id).astype(F32)).astype(BF16)
        mask_t = (same * (row_id <= col_id).astype(F32)).astype(BF16)
        r.mask[c] = mask
        r.maskt[c] = mask_t

    def twice(v):
        return cat([v, v], 1)

    def features(u, p):
        wide_u = u.astype(F32)
        square = wide_u * wide_u * (-1.0 / (16.0 * c4))
        hi = square.astype(BF16)
        lo = (square - hi.astype(F32)).astype(BF16)
        expo = dot(cat([u, hi], 1), r.bb[p]) + dot(lo, r.bb[p, LANES:, :])
        return jnp.exp2(expo * exp_scale).astype(BF16)

    def merge(u):
        return cat([u[:64, :M], u[64:128, M:], u[128:192, :M], u[192:, M:]], 0)

    def split(s):
        zero = jnp.zeros((64, M), s.dtype)
        first = cat([s[:64], zero, s[128:192], zero], 0)
        second = cat([zero, s[64:128], zero, s[192:]], 0)
        return cat([first, second], 1)

    def state_exchange(i, own, got):
        base = sems(3 * npair)

        def copies(p):
            at = base + p * 3
            return (
                remote(own.at[p], got.at[tp, p], at, dev_core),
                remote(own.at[p], got.at[tp, p], at + 1, dev_y),
                remote(got.at[tp_y, p], got.at[tp_y, p], at + 2, dev_core),
            )

        def pack(p, state):
            own[p, :128, :] = state[:128].astype(BF16)
            own[p, 128:144, :] = state[128:144].astype(BF16)
            own[p, 144:160, :] = state[192:208].astype(BF16)
            to_core, to_y, _ = copies(p)
            to_y.start()
            to_core.start()

        def relay():
            def one(p, _):
                _, to_y, on = copies(p)
                to_y.wait_recv()
                on.start()
                return 0

            lax.fori_loop(0, npair, one, 0)

        def collect(first):
            def one(p, _):
                to_core, to_y, on = copies(p)
                to_core.wait_recv()
                on.wait_recv()
                total = jnp.zeros((160, M), F32)
                for k, slot in enumerate((tp_core, tp_y, tp_far)):
                    total = total + got[slot, p].astype(F32) * r.sc[first + slot]
                r.tin[p, :128, :] = total[:128]
                r.tin[p, 128:192, :] = jnp.broadcast_to(total[128:129], (64, M))
                r.tin[p, 192:, :] = jnp.broadcast_to(total[144:145], (64, M))
                to_core.wait_send()
                to_y.wait_send()
                on.wait_send()
                return 0

            lax.fori_loop(0, npair, one, 0)

        return pack, relay, collect

    pack, relay, collect = state_exchange(0, r.own, r.got)

    def key_side(i, _):
        p, c = lax.div(i, nt), lax.rem(i, nt)
        rows = rows_at(c * T, T)
        phi = features(r.k[p, rows, :], p)
        r.phik[p, rows, :] = phi
        gain = merge(dot_c(r.vp[p, rows, :] * twice(r.tail[rows, :]), phi))

        @pl.when(c == 0)
        def _():
            r.sl[p * (nt + 1)] = jnp.zeros((M, M), F32)

        state = r.sc[c] * r.sl[p * (nt + 1) + c] + gain
        r.sl[p * (nt + 1) + c + 1] = state

        @pl.when(c == nt - 1)
        def _():
            pack(p, state)

        return 0

    lax.fori_loop(0, npair * nt, key_side, 0)
    up_y.wait_recv()
    up_on.start()
    down_y.start()

    def query_side(i, _):
        p, c = lax.div(i, nt), lax.rem(i, nt)
        rows = rows_at(c * T, T)
        r.phiq[p, rows, :] = features(r.q[p, rows, :], p)
        return 0

    lax.fori_loop(0, npair * nt, query_side, 0)
    relay()
    collect(3 * nt)

    def attend(i, _):
        p, c = lax.div(i, nt), lax.rem(i, nt)
        rows = rows_at(c * T, T)
        state = (r.sl[p * (nt + 1) + c] + r.sc[nt + c] * r.tin[p]).astype(BF16)
        state = split(state)
        r.st[i] = state
        phi_q, phi_k = r.phiq[p, rows, :], r.phik[p, rows, :]
        scores = cat([dot_t(phi_q[:, :M], phi_k[:, :M]), dot_t(phi_q[:, M:], phi_k[:, M:])], 1)
        scores = scores.astype(BF16) * twice(r.mask[c])
        vals = r.vp[p, rows, :]
        both = dot(scores, cat([vals * low, vals * high], 0))
        both = both + twice(r.use[rows, :].astype(F32)) * dot_t(phi_q, state)
        inv = 1.0 / both[:, LANES:]
        lanes = pl.ds(pl.multiple_of(p * LANES, LANES), LANES)
        r.inv[rows, lanes] = inv
        r.mix[rows, lanes] = (both[:, :LANES] * inv).astype(BF16)
        return 0

    lax.fori_loop(0, npair * nt, attend, 0)

    def acc(t):
        return cat([r.sl[2 * t], r.sl[2 * t + 1]], 1)

    def add_acc(t, v):
        r.sl[2 * t] += v[:, :M]
        r.sl[2 * t + 1] += v[:, M:]

    def middle(t, _):
        rows = rows_at(t * T, T)
        res = r.tok[rows, :].astype(F32) + dot(r.mix[rows, :], r.wo[...])
        r.res[rows, :] = res
        mean = jnp.mean(res, axis=-1, keepdims=True)
        cen = res - mean
        inv = lax.rsqrt(jnp.mean(cen * cen, axis=-1, keepdims=True) + NORM_EPS)
        r.hf[rows, :] = ((cen * inv) * r.gf[...]).astype(BF16)
        r.sl[2 * t] = res[:, :M]
        r.sl[2 * t + 1] = res[:, M:]
        r.sl[2 * nt + 2 * t] = jnp.zeros((T, M), F32)
        r.sl[2 * nt + 2 * t + 1] = jnp.zeros((T, M), F32)
        return 0

    lax.fori_loop(0, nt, middle, 0)
    down_y.wait_recv()
    down_on.start()
    own_up.wait()
    own_down.wait()
    up_core.wait_recv()
    down_core.wait_recv()
    up_on.wait_recv()
    down_on.wait_recv()
    for t in range(nt):
        rows = slice(t * T, (t + 1) * T)
        r.hft[:, rows] = r.hf[rows, :].T
        r.got_t[:, rows] = r.go[rows, :].T

    f_base = sems(5 + 2 * (nz - 1))
    piece = D // nz

    f_c0 = remote(r.ct.at[0], r.fc.at[0], f_base, dev_core)
    f_y = remote(r.ct.at[1], r.fy, f_base + 1, dev_y)
    f_c1 = remote(r.ct.at[2], r.fc.at[1], f_base + 2, dev_core)
    f_x = remote(r.ct.at[3, pl.ds(1 - xbit, 1)], r.fx, f_base + 3, dev_x)
    f_z = [
        remote(
            r.ct.at[3, xbit, rows_at(z_at(k) * piece, piece)], r.fz.at[k - 1],
            f_base + 4 + k, dev_z(k),
        )
        for k in range(1, nz)
    ]
    f_own = rows_at(zi * piece, piece)
    f_zback = [
        remote(r.fo.at[xbit, f_own], r.fo.at[xbit, f_own], f_base + 4 + nz - 1 + k, dev_z(k))
        for k in range(1, nz)
    ]
    f_xback = remote(r.fo.at[xbit], r.fo.at[xbit], f_base + 4, dev_x)

    def add_rows(dst, start, src, n):
        step = min(n, 128)

        def one(b, _):
            at = rows_at(start + b * step, step)
            dst[:, at, :] = dst[:, at, :] + src[:, rows_at(b * step, step), :]
            return 0

        lax.fori_loop(0, n // step, one, 0)

    def ffn(s, out):
        def tile(t, _):
            rows = rows_at(t * T, T)
            up = dot(r.hf[rows, :], r.wu[s])
            grad_act = dot_t(r.go[rows, :], r.wd[s])
            sq = up * up
            cubic = (GELU_SCALE * GELU_CUBIC) * sq
            tang = jnp.tanh(up * (GELU_SCALE + cubic))
            hu = 0.5 * up
            act = (hu + hu * tang).astype(BF16)
            slope = (0.5 + 0.5 * tang) + hu * (1.0 - tang * tang) * (GELU_SCALE + 3.0 * cubic)
            gup = (grad_act * slope).astype(BF16)
            r.gp[rows, :D] = act
            r.gp[rows, D : 2 * D] = gup
            add_acc(t, dot(act, r.wd[s]))
            add_acc(nt + t, dot_t(gup, r.wu[s]))
            return 0

        lax.fori_loop(0, nt, tile, 0)

        def grads(t, _):
            rows = rows_at(t * T, T)
            out[0, rows, :] = dot(r.hft[rows, :], r.gp[:, D : 2 * D]).astype(BF16)
            out[1, rows, :] = dot(r.got_t[rows, :], r.gp[:, :D]).astype(BF16)
            return 0

        lax.fori_loop(0, D // T, grads, 0)

    ffn(tp_far, r.ct.at[0])
    f_c0.start()
    ffn(tp_y, r.ct.at[1])
    f_c0.wait_recv()
    add_rows(r.ct.at[1], 0, r.fc.at[0], D)
    f_y.start()
    ffn(tp_core, r.ct.at[2])
    f_c1.start()
    ffn(tp, r.ct.at[3])
    f_c1.wait_recv()
    add_rows(r.ct.at[3], 0, r.fc.at[1], D)

    def f5():
        f_y.wait_recv()
        add_rows(r.ct.at[3], 0, r.fy, D)
        f_x.start()

    def f6():
        f_x.wait_recv()
        add_rows(r.ct.at[3, pl.ds(xbit, 1)], 0, r.fx, D)
        for copy in f_z:
            copy.start()

    def f7():
        for copy in f_z:
            copy.wait_recv()
        total = r.ct[3, xbit, f_own, :].astype(F32)
        for k in range(1, nz):
            total = total + r.fz[k - 1].astype(F32)
        r.fo[xbit, f_own, :] = total.astype(BF16)
        for copy in f_zback:
            copy.start()

    def f8():
        for copy in f_zback:
            copy.wait_recv()
        f_xback.start()

    fo_out = pltpu.make_async_copy(r.fo, r.fo_out, r.ls.at[3])

    def f9():
        f_xback.wait_recv()
        fo_out.start()

    f_sends = [f_y, f_x] + f_z + f_zback + [f_xback]

    ones_row = lax.broadcasted_iota(jnp.int32, (2 * LANES, LANES), 0)
    ones_col = lax.broadcasted_iota(jnp.int32, (2 * LANES, LANES), 1)
    head_ones = (lax.div(lax.rem(ones_row, LANES), 64) == lax.div(ones_col, 64)).astype(F32).astype(BF16)
    r.gg[...] = jnp.zeros((2, 8, D), F32)

    def gn_at(c):
        return rows_at(lax.rem(c, 2) * T, T), pl.ds(pl.multiple_of(lax.div(c, 2) * T, T), T)

    def gn_of(p, c):
        at, wide_at = gn_at(c)
        return r.wd[p, at, wide_at]

    def fold(v):
        return jnp.sum(v.reshape(T // 8, 8, D), axis=0)

    for copy in (up_core, up_y, up_on, down_core, down_y, down_on):
        copy.wait_send()

    def back_middle(t, _):
        rows = rows_at(t * T, T)
        r.hf[rows, :] = acc(t).astype(BF16)
        res = r.res[rows, :]
        mean = jnp.mean(res, axis=-1, keepdims=True)
        cen = res - mean
        inv = lax.rsqrt(jnp.mean(cen * cen, axis=-1, keepdims=True) + NORM_EPS)
        n = cen * inv
        gh = acc(nt + t)
        r.gg[0] += fold(gh * n)
        sc = gh * r.gf[...]
        centre = jnp.mean(sc, axis=-1, keepdims=True)
        inner = jnp.mean(sc * n, axis=-1, keepdims=True)
        gres = r.go[rows, :].astype(F32) + inv * (sc - centre - n * inner)
        r.res[rows, :] = gres
        gattn = gres.astype(BF16)
        r.gp[rows, 2 * D :] = gattn
        gmi = dot_t(gattn, r.wo[...]) * r.inv[rows, :]
        w = gmi * r.mix[rows, :].astype(F32) * (-1.0)
        hi = w.astype(BF16)
        lo = (w - hi.astype(F32)).astype(BF16)
        gnum = gmi.astype(BF16)
        for p in range(npair):
            lanes = slice(p * LANES, (p + 1) * LANES)
            gden = dot(cat([hi[:, lanes], lo[:, lanes]], 1), head_ones).astype(BF16)
            at, wide_at = gn_at(t)
            r.wd[p, at, wide_at] = cat([gnum[:, lanes], gden * jnp.asarray(1.0 / 64.0, BF16)], 1)
        return 0

    lax.fori_loop(0, nt, back_middle, 0)
    out_copy = pltpu.make_async_copy(r.hf, r.out, r.ls.at[4])
    out_copy.start()

    bpack, brelay, bcollect = state_exchange(1, r.bown, r.bgot)

    def state_back(i, _):
        p, c = lax.div(i, nt), nt - 1 - lax.rem(i, nt)
        rows = rows_at(c * T, T)

        @pl.when(c == nt - 1)
        def _():
            r.sl[p * (nt + 1) + nt] = jnp.zeros((M, M), F32)

        gain = merge(dot_c(gn_of(p, c) * twice(r.use[rows, :]), r.phiq[p, rows, :]))
        state = r.sc[c] * r.sl[p * (nt + 1) + c + 1] + gain
        r.sl[p * (nt + 1) + c] = state

        @pl.when(c == 0)
        def _():
            bpack(p, state)

        return 0

    lax.fori_loop(0, npair * nt, state_back, 0)

    def all_sum(buf, res, rc, ry, rx, rz):
        n = buf.shape[1]
        n2, n4, n8 = n // 2, n // 4, n // 8
        cut = n8 // nz if (n8 // nz) % 16 == 0 else n8
        share = cut != n8
        base = sems(6 + 2 * (nz - 1))
        o2 = core * n2
        o4 = o2 + ybit * n4
        o8 = o4 + xbit * n8
        oz = o8 + (zi * cut if share else 0)
        to_c = remote(buf.at[:, rows_at((1 - core) * n2, n2)], rc, base, dev_core)
        to_y = remote(buf.at[:, rows_at(o2 + (1 - ybit) * n4, n4)], ry, base + 1, dev_y)
        to_x = remote(buf.at[:, rows_at(o4 + (1 - xbit) * n8, n8)], rx, base + 2, dev_x)
        to_z = [
            remote(
                buf.at[:, rows_at(o8 + (z_at(k) * cut if share else 0), cut)], rz.at[k - 1, :, :cut],
                base + 5 + k, dev_z(k),
            )
            for k in range(1, nz)
        ]
        mine = rows_at(oz, cut)
        back_z = [
            remote(res.at[:, mine], res.at[:, mine], base + 5 + nz - 1 + k, dev_z(k)) for k in range(1, nz)
        ] if share else []
        at8, at4, at2 = rows_at(o8, n8), rows_at(o4, n4), rows_at(o2, n2)
        back_x = remote(res.at[:, at8], res.at[:, at8], base + 3, dev_x)
        back_y = remote(res.at[:, at4], res.at[:, at4], base + 4, dev_y)
        back_c = remote(res.at[:, at2], res.at[:, at2], base + 5, dev_core)

        def s1():
            to_c.start()

        def s2():
            to_c.wait_recv()
            add_rows(buf, o2, rc, n2)
            to_y.start()

        def s3():
            to_y.wait_recv()
            add_rows(buf, o4, ry, n4)
            to_x.start()

        def s4():
            to_x.wait_recv()
            add_rows(buf, o8, rx, n8)
            for copy in to_z:
                copy.start()

        def s5():
            for copy in to_z:
                copy.wait_recv()
            total = buf[:, mine, :].astype(F32)
            for k in range(1, nz):
                total = total + rz[k - 1, :, :cut].astype(F32)
            res[:, mine, :] = total.astype(BF16)
            for copy in back_z:
                copy.start()

        def s6():
            for copy in back_z:
                copy.wait_recv()
            back_x.start()

        def s7():
            back_x.wait_recv()
            back_y.start()

        def s8():
            back_y.wait_recv()
            back_c.start()

        def s9():
            back_c.wait_recv()

        def drain():
            for copy in [to_c, to_y, to_x] + to_z + back_z + [back_x, back_y, back_c]:
                copy.wait_send()

        return [s1, s2, s3, s4, s5, s6, s7, s8, s9], drain

    oq, kva, kvb = r.ct.at[0], r.ct.at[2, 0:1], r.ct.at[2, 1:2]
    oqr, kvar, kvbr = r.wu.at[0:2], r.wu.at[2:3], r.wu.at[3:4]
    oq_steps, oq_drain = all_sum(oq, oqr, r.fc.at[0, :, : D // 2], r.oq_y, r.oq_x, r.oq_z)
    kva_steps, kva_drain = all_sum(kva, kvar, r.fc.at[0, 0:1, D // 2 :], r.kva_y, r.kva_x, r.kva_z)
    kvb_steps, kvb_drain = all_sum(kvb, kvbr, r.fc.at[0, 1:2, D // 2 :], r.kvb_y, r.kvb_x, r.kvb_z)
    oq_out = pltpu.make_async_copy(oqr, r.oq_out, r.ls.at[5])
    kva_out = pltpu.make_async_copy(kvar, r.kva_out, r.ls.at[6])
    kvb_out = pltpu.make_async_copy(kvbr, r.kvb_out, r.ls.at[7])

    def run_at(i, tasks):
        for at, task in tasks:
            pl.when(i == at)(task)

    f_c0.wait_send()
    f_c1.wait_send()
    for t in range(D // T):
        rows = slice(t * T, (t + 1) * T)
        oq[0, rows, :] = dot_c(r.mix[:, rows], r.gp[:, 2 * D :]).astype(BF16)
    brelay()

    def back_query(i, _):
        p, c = lax.div(i, nt), lax.rem(i, nt)
        rows = rows_at(c * T, T)
        vals, gn = r.vp[p, rows, :], gn_of(p, c)
        phi_q, phi_k = r.phiq[p, rows, :], r.phik[p, rows, :]
        g = dot_t(gn, cat([vals * low, vals * high], 0)).astype(BF16) * twice(r.mask[c])
        gphi = cat([dot(g[:, :M], phi_k[:, :M]), dot(g[:, M:], phi_k[:, M:])], 1)
        gphi = gphi + dot(gn * twice(r.use[rows, :]), r.st[i])
        t = (gphi * phi_q.astype(F32)).astype(BF16)
        o = dot_t(t, r.bb[p])
        gq = c4 * o[:, :LANES] - r.q[p, rows, :].astype(F32) * (o[:, LANES:] * 0.125)
        r.gp[rows, pl.ds(pl.multiple_of(p * LANES, LANES), LANES)] = gq.astype(BF16)
        run_at(i, [(8, f5), (14, f6)])
        return 0

    lax.fori_loop(0, npair * nt, back_query, 0)
    for t in range(D // T):
        rows = slice(t * T, (t + 1) * T)
        oq[1, rows, :] = dot(r.ht[rows, :], r.gp[:, :D]).astype(BF16)
    oq_steps[0]()
    bcollect(3 * nt + 4)

    def pair_grads(p, out, at):
        for t in range(D // T):
            rows = slice(t * T, (t + 1) * T)
            kv = cat(
                [r.gp[:, pl.ds(pl.multiple_of(o * D + p * LANES, LANES), LANES)] for o in (1, 2)], 1
            )
            part = dot(r.ht[rows, :], kv).astype(BF16)
            out[0, rows, at * LANES : (at + 1) * LANES] = part[:, :LANES]
            out[0, rows, 256 + at * LANES : 256 + (at + 1) * LANES] = part[:, LANES:]

    def back_key(i, _):
        p, c = lax.div(i, nt), lax.rem(i, nt)
        rows = rows_at(c * T, T)
        dstate = split((r.sl[p * (nt + 1) + c + 1] + r.sc[2 * nt + c] * r.tin[p]).astype(BF16))
        vals, gn = r.vp[p, rows, :], gn_of(p, c)
        phi_q, phi_k = r.phiq[p, rows, :], r.phik[p, rows, :]
        mask = twice(r.maskt[c])
        gt = cat([dot_t(vals * low, gn), dot_t(vals * high, gn)], 1).astype(BF16) * mask
        at = cat([dot_t(phi_k[:, :M], phi_q[:, :M]), dot_t(phi_k[:, M:], phi_q[:, M:])], 1)
        at = at.astype(BF16) * mask
        gphi = cat([dot(gt[:, :M], phi_q[:, :M]), dot(gt[:, M:], phi_q[:, M:])], 1)
        tail = r.tail[rows, :]
        gphi = gphi + dot(vals * twice(tail), dstate)
        gnum = gn[:, :LANES]
        gv = dot(at, cat([gnum * low[:, :LANES], gnum * high[:, :LANES]], 0))
        gv = gv + tail.astype(F32) * dot_t(phi_k, dstate[:LANES])
        t = (gphi * phi_k.astype(F32)).astype(BF16)
        o = dot_t(t, r.bb[p])
        gk = c4 * o[:, :LANES] - r.k[p, rows, :].astype(F32) * (o[:, LANES:] * 0.125)
        r.gp[rows, pl.ds(pl.multiple_of(D + p * LANES, LANES), LANES)] = gk.astype(BF16)
        r.gp[rows, pl.ds(pl.multiple_of(2 * D + p * LANES, LANES), LANES)] = gv.astype(BF16)

        @pl.when(c == nt - 1)
        def _():
            for q in range(npair):
                pl.when(p == q)(
                    functools.partial(pair_grads, q, kva if q < 2 else kvb, q % 2)
                )

        run_at(i, [
            (1, f7), (1, oq_steps[1]), (4, f8), (5, oq_steps[2]), (7, f9), (7, oq_steps[3]),
            (7, kva_steps[0]), (8, kva_steps[1]), (9, oq_steps[4]), (10, kva_steps[2]),
            (11, oq_steps[5]), (12, kva_steps[3]), (13, oq_steps[6]), (14, kva_steps[4]),
            (15, oq_steps[7]), (15, kva_steps[5]),
        ])
        return 0

    lax.fori_loop(0, npair * nt, back_key, 0)
    kvb_steps[0]()

    def back_first(t, _):
        rows = rows_at(t * T, T)
        gh = dot_t(r.gp[rows, :D], r.wq[...])
        gh = gh + dot_t(r.gp[rows, D : 2 * D], r.wk[...])
        gh = gh + dot_t(r.gp[rows, 2 * D :], r.wv[...])
        x = r.tok[rows, :].astype(F32)
        mean = jnp.mean(x, axis=-1, keepdims=True)
        cen = x - mean
        inv = lax.rsqrt(jnp.mean(cen * cen, axis=-1, keepdims=True) + NORM_EPS)
        n = cen * inv
        r.gg[1] += fold(gh * n)
        sc = gh * r.ga[...]
        centre = jnp.mean(sc, axis=-1, keepdims=True)
        inner = jnp.mean(sc * n, axis=-1, keepdims=True)
        r.res[rows, :] += inv * (sc - centre - n * inner)
        run_at(t, [(0, kvb_steps[1]), (1, kva_steps[6]), (2, kvb_steps[2])])
        return 0

    lax.fori_loop(0, nt, back_first, 0)
    gt_copy = pltpu.make_async_copy(r.res, r.gt, r.ls.at[8])
    gt_copy.start()

    g_base = sems(3 + ndp - 1)
    r.g1[...] = cat([jnp.sum(r.gg[0], axis=0, keepdims=True), jnp.sum(r.gg[1], axis=0, keepdims=True),
                     jnp.zeros((6, D), F32)], 0)
    g_tp = [remote(r.g1, r.gr.at[k - 1], g_base + k - 1, (dp, lax.rem(tp + k, 4))) for k in (1, 2, 3)]
    for copy in g_tp:
        copy.start()
    kvb_steps[3]()
    kva_steps[7]()
    oq_steps[8]()
    oq_out.start()
    for copy in g_tp:
        copy.wait_recv()
    r.g2[...] = r.g1[...] + r.gr[0] + r.gr[1] + r.gr[2]
    g_dp = [
        remote(r.g2, r.gr.at[2 + k], g_base + 2 + k, (lax.rem(dp + k, ndp), tp)) for k in range(1, ndp)
    ]
    for copy in g_dp:
        copy.start()
    kvb_steps[4]()
    kva_steps[8]()
    kva_out.start()
    kvb_steps[5]()
    total = r.g2[...]
    for k in range(1, ndp):
        g_dp[k - 1].wait_recv()
        total = total + r.gr[2 + k]
    r.gout[...] = total
    kvb_steps[6]()
    kvb_steps[7]()
    kvb_steps[8]()
    kvb_out.start()

    for copy in seg_copies + f_sends + g_tp + g_dp:
        copy.wait_send()
    oq_drain()
    kva_drain()
    kvb_drain()
    for copy in (fo_out, out_copy, oq_out, kva_out, kvb_out, gt_copy):
        copy.wait()
    assert used[0] <= r.ss.shape[0]


def layer(tokens, segment_ids, grad_out, w_query, w_key, w_value, w_out, w_up, w_down, gain_attn,
          gain_ffn, feature_basis):
    _, L, D = tokens.shape
    H, DH, M = feature_basis.shape
    F = w_up.shape[1]
    npair, nt = H // 2, L // T
    ndp = lax.axis_size("dp")
    nz = ndp // 2
    assert lax.axis_size("tp") == 4 and F == D and DH == 64 and M == T

    vmem, hbm = pl.BlockSpec(memory_space=pltpu.VMEM), pl.BlockSpec(memory_space=pl.ANY)
    ins = {
        "seg": (segment_ids, vmem),
        "tok": (tokens[0], vmem),
        "go": (grad_out[0], vmem),
        "wq": (w_query, vmem),
        "wk": (w_key, vmem),
        "wv": (w_value, vmem),
        "wo": (w_out, vmem),
        "wup": (w_up, hbm),
        "wdn": (w_down, hbm),
        "ga": (gain_attn[None], vmem),
        "gf": (gain_ffn[None], vmem),
        "basis": (feature_basis, vmem),
    }
    outs = {
        "out": ((L, D), BF16, hbm),
        "gt": ((L, D), F32, hbm),
        "fo_out": ((2, D, F), BF16, hbm),
        "oq_out": ((2, D, D), BF16, hbm),
        "kva_out": ((1, D, D), BF16, hbm),
        "kvb_out": ((1, D, D), BF16, hbm),
        "gout": ((8, D), F32, vmem),
    }

    def all_sum_buffers(name, g):
        return {
            name + "_y": ((g, D // 4, D), BF16),
            name + "_x": ((g, D // 8, D), BF16),
            name + "_z": ((nz - 1, g, D // 8, D), BF16),
        }

    scratch = {
        "sg": ((4, 1, L), jnp.int32),
        "wu": ((4, D, F), BF16),
        "wd": ((4, F, D), BF16),
        "bb": ((npair, 2 * LANES, 2 * M), BF16),
        "ht": ((D, L), BF16),
        "q": ((npair, L, LANES), BF16),
        "k": ((npair, L, LANES), BF16),
        "vp": ((npair, L, 2 * LANES), BF16),
        "sc": ((3 * nt + 8, 1, M), F32),
        "use": ((L, LANES), BF16),
        "tail": ((L, LANES), BF16),
        "mask": ((nt, T, M), BF16),
        "maskt": ((nt, T, M), BF16),
        "phik": ((npair, L, 2 * M), BF16),
        "phiq": ((npair, L, 2 * M), BF16),
        "sl": ((npair * (nt + 1), M, M), F32),
        "own": ((npair, 160, M), BF16),
        "got": ((4, npair, 160, M), BF16),
        "bown": ((npair, 160, M), BF16),
        "bgot": ((4, npair, 160, M), BF16),
        "tin": ((npair, M, M), F32),
        "st": ((npair * nt, M, 2 * M), BF16),
        "inv": ((L, D), F32),
        "mix": ((L, D), BF16),
        "res": ((L, D), F32),
        "hf": ((L, D), BF16),
        "hft": ((D, L), BF16),
        "got_t": ((D, L), BF16),
        "ct": ((4, 2, D, F), BF16),
        "fc": ((2, 2, D, F), BF16),
        "fy": ((2, D, F), BF16),
        "fx": ((1, D, F), BF16),
        "fz": ((nz - 1, D // nz, F), BF16),
        "fo": ((2, D, F), BF16),
        "gg": ((2, 8, D), F32),
        "gp": ((L, 3 * D), BF16),
        "g1": ((8, D), F32),
        "g2": ((8, D), F32),
        "gr": ((3 + ndp - 1, 8, D), F32),
    }
    scratch.update(all_sum_buffers("oq", 2))
    scratch.update(all_sum_buffers("kva", 1))
    scratch.update(all_sum_buffers("kvb", 1))
    n_sems = 3 + 6 + 6 * npair + 5 + 2 * (nz - 1) + 3 * (6 + 2 * (nz - 1)) + 3 + ndp - 1
    names = list(ins) + list(outs) + list(scratch) + ["ls", "ss", "rs"]
    res = pl.pallas_call(
        functools.partial(layer_kernel, nz, names),
        out_shape=[jax.ShapeDtypeStruct(s, d) for s, d, _ in outs.values()],
        in_specs=[spec for _, spec in ins.values()],
        out_specs=[spec for _, _, spec in outs.values()],
        scratch_shapes=[pltpu.VMEM(s, d) for s, d in scratch.values()]
        + [
            pltpu.SemaphoreType.DMA((9,)),
            pltpu.SemaphoreType.DMA((n_sems,)),
            pltpu.SemaphoreType.DMA((n_sems,)),
        ],
        name="layer",
        compiler_params=pltpu.CompilerParams(
            collective_id=0, has_side_effects=True, vmem_limit_bytes=67043328
        ),
    )(*[a for a, _ in ins.values()])
    out, gt, fo, oq, kva, kvb, gains = res
    up, down = fo[0].astype(F32), fo[1].T.astype(F32)
    key = cat([kva[0, :, :256], kvb[0, :, :256]], 1).astype(F32)
    value = cat([kva[0, :, 256:], kvb[0, :, 256:]], 1).astype(F32)
    return (
        out[None], gt[None], oq[1].astype(F32), key, value, oq[0].astype(F32), up, down,
        gains[1], gains[0],
    )


def solution(mesh):
    whole = P()
    in_specs = (
        P("dp", "tp", None), P("dp", "tp"), P("dp", "tp", None), whole, whole, whole, whole,
        P(None, "tp"), P("tp", None), whole, whole, whole,
    )
    out_specs = (
        P("dp", "tp", None), P("dp", "tp", None), whole, whole, whole, whole,
        P(None, "tp"), P("tp", None), whole, whole,
    )
    return jax.shard_map(layer, mesh=mesh, in_specs=in_specs, out_specs=out_specs, check_vma=False)
```

```python
import functools
import math
from types import SimpleNamespace

import jax
import jax.numpy as jnp
from jax import lax
from jax.experimental import pallas as pl
from jax.experimental.pallas import tpu as pltpu
from jax.sharding import PartitionSpec as P

MESH = pl.DeviceIdType.MESH
F32 = jnp.float32
BF16 = jnp.bfloat16
NORM_EPS = 1e-05
GELU_SCALE = 0.7978845608028654
GELU_CUBIC = 0.044715
LANES = 128
PLAN = (
    ("project", 3, "D"),
    ("key_side", 15, "D"),
    ("query_side", 2, "U"),
    ("query_side", 15, "S"),
    ("attend", 0, "D"),
    ("back_middle", 2, "F0"),
    ("out_grads", 0, "O"),
    ("back_query", 1, "F0"),
    ("back_query", 2, "O"),
    ("back_query", 4, "F1"),
    ("back_query", 10, "O"),
    ("back_query", 15, "B"),
    ("back_query", 15, "F0"),
    ("query_grads", 0, "Q"),
    ("query_grads", 0, "O"),
    ("back_key", 0, "F1"),
    ("back_key", 0, "Q"),
    ("back_key", 3, "K0"),
    ("back_key", 6, "K0"),
    ("back_key", 6, "Q"),
    ("back_key", 7, "K1"),
    ("back_key", 7, "F0"),
    ("back_key", 7, "O"),
    ("back_key", 9, "K1"),
    ("back_key", 9, "K0"),
    ("back_key", 9, "Q"),
    ("back_key", 11, "K2"),
    ("back_key", 12, "K0"),
    ("back_key", 12, "F1"),
    ("back_key", 13, "K2"),
    ("back_key", 13, "Q"),
    ("back_key", 13, "O"),
    ("back_key", 15, "K3"),
    ("back_key", 15, "F0"),
    ("back_key", 15, "K1"),
    ("back_key", 15, "K0"),
    ("back_first", 1, "K3"),
    ("back_first", 1, "K2"),
    ("back_first", 1, "O"),
    ("back_first", 2, "K1"),
    ("tail", 0, "K2"),
    ("tail", 0, "F1"),
    ("tail", 0, "K3"),
    ("tail", 0, "Q"),
    ("tail", 0, "K0"),
    ("tail", 0, "G"),
    ("tail", 0, "K1"),
    ("tail", 0, "K3"),
    ("tail", 0, "O"),
    ("tail", 0, "K2"),
    ("tail", 0, "Q"),
    ("tail", 0, "O"),
    ("tail", 0, "K0"),
    ("tail", 0, "G"),
    ("tail", 0, "K1"),
    ("tail", 0, "K3"),
    ("tail", 0, "K2"),
    ("tail", 0, "F1"),
    ("tail", 0, "K1"),
    ("tail", 0, "K2"),
    ("tail", 0, "K3"),
    ("tail", 0, "Q"),
    ("tail", 0, "K0"),
    ("tail", 0, "Q"),
    ("tail", 0, "K3"),
    ("tail", 0, "K1"),
    ("tail", 0, "K0"),
    ("tail", 0, "K2"),
    ("tail", 0, "K1"),
    ("tail", 0, "K3"),
    ("tail", 0, "K2"),
    ("tail", 0, "K3"),
)
ORDER = {"O": "cxy", "Q": "cxy", "K": "cxy"}
T = 256


def dot(a, b):
    return jnp.dot(a, b, preferred_element_type=F32)


def dot_t(a, b):
    return lax.dot_general(a, b, (((1,), (1,)), ((), ())), preferred_element_type=F32)


def dot_c(a, b):
    return lax.dot_general(a, b, (((0,), (0,)), ((), ())), preferred_element_type=F32)


def rows_at(start, size):
    return pl.ds(pl.multiple_of(start, 16), size)


def cat(parts, axis):
    return jnp.concatenate(parts, axis=axis)


def lane_groups():
    lane = lax.broadcasted_iota(jnp.int32, (1, 2 * LANES), 1)
    first = lax.rem(lane, LANES) < 64
    one = jnp.where(first, 1.0, 0.0)
    return one.astype(BF16), (1.0 - one).astype(BF16)


def layer_kernel(nz, names, *refs):
    r = SimpleNamespace(**dict(zip(names, refs)))
    L, D = r.tok.shape
    nt = L // T
    npair = r.basis.shape[0] // 2
    M = r.basis.shape[2]
    c4 = 64.0**-0.25
    exp_scale = c4 * math.log2(math.e)

    dp, tp = lax.axis_index("dp"), lax.axis_index("tp")
    ndp = 2 * nz
    core, ybit = lax.rem(tp, 2), lax.div(tp, 2)
    xbit, zi = lax.rem(dp, 2), lax.div(dp, 2)
    tp_core, tp_y, tp_far = tp + 1 - 2 * core, lax.rem(tp + 2, 4), 3 - tp
    dev_core, dev_y, dev_far = (dp, tp_core), (dp, tp_y), (dp, tp_far)
    dev_x = (dp + 1 - 2 * xbit, tp)

    def z_at(k):
        return lax.rem(zi + k, nz)

    def dev_z(k):
        return (z_at(k) * 2 + xbit, tp)

    plan, steps = {}, {}
    for place, i, chunk in PLAN:
        plan.setdefault((place, i), []).append(chunk)

    def advance(place, i):
        for chunk in plan.pop((place, i), ()):
            steps[chunk].pop(0)()

    def loop(name, n, body, tasks=()):
        def step(i, _):
            body(i)
            for when, task in tasks:
                pl.when(when(i))(functools.partial(task, i))
            for k in range(n):
                if (name, k) in plan:
                    pl.when(i == k)(functools.partial(advance, name, k))
            return 0

        lax.fori_loop(0, n, step, 0)

    def once(name, body):
        body()
        advance(name, 0)

    used = [0]

    def sems(n):
        first = used[0]
        used[0] += n
        return first

    def remote(src, dst, idx, dev):
        return pltpu.make_async_remote_copy(
            src_ref=src, dst_ref=dst, send_sem=r.ss.at[idx], recv_sem=r.rs.at[idx],
            device_id=dev, device_id_type=MESH,
        )

    barrier = pltpu.get_barrier_semaphore()
    for k in (1, 2, 3):
        pl.semaphore_signal(barrier, inc=1, device_id=(dp, lax.rem(tp + k, 4)), device_id_type=MESH)
    for k in range(1, ndp):
        pl.semaphore_signal(barrier, inc=1, device_id=(lax.rem(dp + k, ndp), tp), device_id_type=MESH)

    own_up = pltpu.make_async_copy(r.wup, r.wu.at[tp], r.ls.at[0])
    own_down = pltpu.make_async_copy(r.wdn, r.wd.at[tp], r.ls.at[1])
    own_seg = pltpu.make_async_copy(r.seg, r.sg.at[tp], r.ls.at[2])
    own_up.start()
    own_down.start()
    own_seg.start()
    pl.semaphore_wait(barrier, 3 + ndp - 1)

    seg_base = sems(3)
    seg_copies = [
        remote(r.seg, r.sg.at[tp], seg_base + k - 1, (dp, lax.rem(tp + k, 4))) for k in (1, 2, 3)
    ]
    for copy in seg_copies:
        copy.start()

    up_base, down_base = sems(3), sems(4 + nz - 1)
    pr = r.wdn.shape[0] // ndp
    up_core = remote(r.wup, r.wu.at[tp], up_base, dev_core)
    up_y = remote(r.wup, r.wu.at[tp], up_base + 1, dev_y)
    up_on = remote(r.wu.at[tp_y], r.wu.at[tp_y], up_base + 2, dev_core)
    down_core = remote(r.wdn, r.wd.at[tp], down_base, dev_core)
    down_piece = rows_at((xbit * nz + zi) * pr, pr)
    down_plane = rows_at(xbit * nz * pr, nz * pr)
    down_y = remote(r.wdn.at[down_piece], r.wd.at[tp, down_piece], down_base + 1, dev_y)
    down_z = [
        remote(r.wd.at[tp_y, down_piece], r.wd.at[tp_y, down_piece], down_base + 3 + k, dev_z(k))
        for k in range(1, nz)
    ]
    down_x = remote(r.wd.at[tp_y, down_plane], r.wd.at[tp_y, down_plane], down_base + 2, dev_x)
    down_on = remote(r.wd.at[tp_y], r.wd.at[tp_y], down_base + 3, dev_core)
    w_sends = [up_core, up_y, up_on, down_core, down_y, down_x, down_on] + down_z

    def start_all(*copies):
        for copy in copies:
            copy.start()

    def chain(name, *tasks):
        steps[name] = list(tasks)

    def then(waits, *starts):
        def task():
            for copy in waits:
                copy.wait_recv()
            start_all(*starts)

        return task

    chain("U", then([up_y], up_on))
    chain("D", then([down_y], *down_z), then(down_z, down_x), then([down_x], down_on))
    down_y.start()
    up_y.start()
    up_core.start()
    down_core.start()

    for p in range(npair):
        for h in range(2):
            fb = r.basis[2 * p + h]
            zero, one = jnp.zeros((64, M), BF16), jnp.ones((64, M), BF16)
            parts = [fb, zero, one, zero] if h == 0 else [zero, fb, zero, one]
            r.bb[p, :, h * M : (h + 1) * M] = cat(parts, 0)

    low, high = lane_groups()

    def project(t):
        rows = rows_at(t * T, T)
        x = r.tok[rows, :].astype(F32)
        mean = jnp.mean(x, axis=-1, keepdims=True)
        cen = x - mean
        inv = lax.rsqrt(jnp.mean(cen * cen, axis=-1, keepdims=True) + NORM_EPS)
        hid = ((cen * inv) * r.ga[...]).astype(BF16)
        r.ht[:, pl.ds(pl.multiple_of(t * T, LANES), T)] = hid.T
        k = dot(hid, r.wk[...]).astype(BF16)
        v = dot(hid, r.wv[...]).astype(BF16)
        q = dot(hid, r.wq[...]).astype(BF16)
        for p in range(npair):
            lanes = slice(p * LANES, (p + 1) * LANES)
            r.q[p, rows, :] = q[:, lanes]
            r.k[p, rows, :] = k[:, lanes]
            r.vp[p, rows, :LANES] = v[:, lanes]
            r.vp[p, rows, LANES:] = jnp.ones((T, LANES), BF16)

    loop("project", nt, project)

    own_seg.wait()
    for copy in seg_copies:
        copy.wait_recv()
    row_max, row_min = [], []
    for j in range(4):
        ids = r.sg[j].astype(F32)
        row_max.append(jnp.max(ids, axis=1, keepdims=True))
        row_min.append(jnp.min(ids, axis=1, keepdims=True))
    in_seg = jnp.full((1, 1), -1.0, F32)
    for j in range(4):
        in_seg = jnp.maximum(in_seg, jnp.where(j < tp, row_max[j], -1.0))
    mine = r.seg[...].astype(F32)
    ends = [jnp.max(mine[:, c * T : (c + 1) * T], axis=1, keepdims=True) for c in range(nt)]
    befores = [in_seg] + ends[:-1]
    keeps = [(befores[c] == ends[c]).astype(F32) for c in range(nt)]
    wide = lambda v: jnp.broadcast_to(v, (1, M))
    flag = jnp.ones((1, 1), F32)
    for c in range(nt):
        r.sc[c] = wide(keeps[c])
        r.sc[nt + c] = wide(flag)
        flag = flag * keeps[c]
    flag = jnp.ones((1, 1), F32)
    for c in reversed(range(nt)):
        r.sc[2 * nt + c] = wide(flag)
        flag = flag * keeps[c]
    for j in range(4):
        r.sc[3 * nt + j] = wide(jnp.where(j < tp, (row_max[j] == in_seg).astype(F32), 0.0))
        r.sc[3 * nt + 4 + j] = wide(jnp.where(j > tp, (row_min[j] == ends[-1]).astype(F32), 0.0))
    row_id = lax.broadcasted_iota(jnp.int32, (T, T), 0)
    col_id = lax.broadcasted_iota(jnp.int32, (T, T), 1)
    for c in range(nt):
        along = mine[:, c * T : (c + 1) * T]
        down = jnp.broadcast_to(along, (LANES, T)).T
        rows = slice(c * T, (c + 1) * T)
        use = (down == befores[c]).astype(F32).astype(BF16)
        tail = (down == ends[c]).astype(F32).astype(BF16)
        r.use[rows, :] = use
        r.tail[rows, :] = tail
        same = (cat([down, down], 1) == along).astype(F32)
        mask = (same * (row_id >= col_id).astype(F32)).astype(BF16)
        mask_t = (same * (row_id <= col_id).astype(F32)).astype(BF16)
        r.mask[c] = mask
        r.maskt[c] = mask_t

    def twice(v):
        return cat([v, v], 1)

    def features(u, p):
        wide_u = u.astype(F32)
        square = wide_u * wide_u * (-1.0 / (16.0 * c4))
        hi = square.astype(BF16)
        lo = (square - hi.astype(F32)).astype(BF16)
        expo = dot(cat([u, hi], 1), r.bb[p]) + dot(lo, r.bb[p, LANES:, :])
        return jnp.exp2(expo * exp_scale).astype(BF16)

    def merge(u):
        return cat([u[:64, :M], u[64:128, M:], u[128:192, :M], u[192:, M:]], 0)

    def split(s):
        zero = jnp.zeros((64, M), s.dtype)
        first = cat([s[:64], zero, s[128:192], zero], 0)
        second = cat([zero, s[64:128], zero, s[192:]], 0)
        return cat([first, second], 1)

    def state_exchange(i, own, got):
        base = sems(3 * npair)

        def copies(p):
            at = base + p * 3
            return (
                remote(own.at[p], got.at[tp, p], at, dev_core),
                remote(own.at[p], got.at[tp, p], at + 1, dev_y),
                remote(got.at[tp_y, p], got.at[tp_y, p], at + 2, dev_core),
            )

        def pack(p, slot):
            state = r.sl[p * (nt + 1) + slot]
            own[p, :128, :] = state[:128].astype(BF16)
            own[p, 128:144, :] = state[128:144].astype(BF16)
            own[p, 144:160, :] = state[192:208].astype(BF16)
            to_core, to_y, _ = copies(p)
            to_y.start()
            to_core.start()

        def relay():
            def one(p, _):
                _, to_y, on = copies(p)
                to_y.wait_recv()
                on.start()
                return 0

            lax.fori_loop(0, npair, one, 0)

        def collect(first):
            def one(p, _):
                to_core, to_y, on = copies(p)
                to_core.wait_recv()
                on.wait_recv()
                total = jnp.zeros((160, M), F32)
                for k, slot in enumerate((tp_core, tp_y, tp_far)):
                    total = total + got[slot, p].astype(F32) * r.sc[first + slot]
                r.tin[p, :128, :] = total[:128]
                r.tin[p, 128:192, :] = jnp.broadcast_to(total[128:129], (64, M))
                r.tin[p, 192:, :] = jnp.broadcast_to(total[144:145], (64, M))
                to_core.wait_send()
                to_y.wait_send()
                on.wait_send()
                return 0

            lax.fori_loop(0, npair, one, 0)

        return pack, [relay], collect

    pack, steps["S"], collect = state_exchange(0, r.own, r.got)

    def key_side(i):
        p, c = lax.div(i, nt), lax.rem(i, nt)
        rows = rows_at(c * T, T)
        phi = features(r.k[p, rows, :], p)
        r.phik[p, rows, :] = phi
        gain = merge(dot_c(r.vp[p, rows, :] * twice(r.tail[rows, :]), phi))

        @pl.when(c == 0)
        def _():
            r.sl[p * (nt + 1)] = jnp.zeros((M, M), F32)

        state = r.sc[c] * r.sl[p * (nt + 1) + c] + gain
        r.sl[p * (nt + 1) + c + 1] = state

    leaves = (lambda i: lax.rem(i, nt) == nt - 1), (lambda i: pack(lax.div(i, nt), nt))

    loop("key_side", npair * nt, key_side, [leaves])

    def query_side(i):
        p, c = lax.div(i, nt), lax.rem(i, nt)
        rows = rows_at(c * T, T)
        r.phiq[p, rows, :] = features(r.q[p, rows, :], p)

    loop("query_side", npair * nt, query_side)
    collect(3 * nt)

    def attend(i):
        p, c = lax.div(i, nt), lax.rem(i, nt)
        rows = rows_at(c * T, T)
        state = (r.sl[p * (nt + 1) + c] + r.sc[nt + c] * r.tin[p]).astype(BF16)
        state = split(state)
        r.st[i] = state
        phi_q, phi_k = r.phiq[p, rows, :], r.phik[p, rows, :]
        scores = cat([dot_t(phi_q[:, :M], phi_k[:, :M]), dot_t(phi_q[:, M:], phi_k[:, M:])], 1)
        scores = scores.astype(BF16) * twice(r.mask[c])
        vals = r.vp[p, rows, :]
        both = dot(scores, cat([vals * low, vals * high], 0))
        both = both + twice(r.use[rows, :].astype(F32)) * dot_t(phi_q, state)
        inv = 1.0 / both[:, LANES:]
        lanes = pl.ds(pl.multiple_of(p * LANES, LANES), LANES)
        r.inv[rows, lanes] = inv
        r.mix[rows, lanes] = (both[:, :LANES] * inv).astype(BF16)

    loop("attend", npair * nt, attend)

    def acc(t):
        return cat([r.sl[2 * t], r.sl[2 * t + 1]], 1)

    def add_acc(t, v):
        r.sl[2 * t] += v[:, :M]
        r.sl[2 * t + 1] += v[:, M:]

    def middle(t):
        rows = rows_at(t * T, T)
        res = r.tok[rows, :].astype(F32) + dot(r.mix[rows, :], r.wo[...])
        r.res[rows, :] = res
        mean = jnp.mean(res, axis=-1, keepdims=True)
        cen = res - mean
        inv = lax.rsqrt(jnp.mean(cen * cen, axis=-1, keepdims=True) + NORM_EPS)
        r.hf[rows, :] = ((cen * inv) * r.gf[...]).astype(BF16)
        r.sl[2 * t] = res[:, :M]
        r.sl[2 * t + 1] = res[:, M:]
        r.sl[2 * nt + 2 * t] = jnp.zeros((T, M), F32)
        r.sl[2 * nt + 2 * t + 1] = jnp.zeros((T, M), F32)

    loop("middle", nt, middle)
    own_up.wait()
    own_down.wait()
    up_core.wait_recv()
    down_core.wait_recv()
    up_on.wait_recv()
    down_on.wait_recv()
    def transposes():
        for t in range(nt):
            rows = slice(t * T, (t + 1) * T)
            r.hft[:, rows] = r.hf[rows, :].T
            r.got_t[:, rows] = r.go[rows, :].T

    once("transposes", transposes)

    def add_rows(dst, start, src, n):
        step = min(n, 128)

        def one(b, _):
            at = rows_at(start + b * step, step)
            dst[at, :] = dst[at, :] + src[rows_at(b * step, step), :]
            return 0

        lax.fori_loop(0, n // step, one, 0)

    def sum_chain(name, buf, res, axes, recvs, recv_z, out, before=None):
        start, n, to, back, spans = 0, buf.shape[0], [], [], []
        base = sems(2 * len(axes) + 2 * (nz - 1))
        for j, (axis, recv) in enumerate(zip(axes, recvs)):
            bit, dev = halves[axis]
            n = n // 2
            to.append(remote(buf.at[rows_at(start + (1 - bit) * n, n)], recv, base + 2 * j, dev))
            start = start + bit * n
            kept = rows_at(start, n)
            back.append(remote(res.at[kept], res.at[kept], base + 2 * j + 1, dev))
            spans.append((start, n))
        base = base + 2 * len(axes) - 1
        cut = n // nz if (n // nz) % 16 == 0 else n
        share = cut != n
        piece = lambda z: rows_at(start + (z * cut if share else 0), cut)
        to_z = [
            remote(buf.at[piece(z_at(k))], recv_z.at[k - 1, :cut], base + k, dev_z(k))
            for k in range(1, nz)
        ]
        own = piece(zi)
        back_z = [
            remote(res.at[own], res.at[own], base + nz - 1 + k, dev_z(k)) for k in range(1, nz)
        ] if share else []

        def first():
            if before is not None:
                before()
            to[0].start()

        def half_sum(j):
            to[j].wait_recv()
            add_rows(buf, spans[j][0], recvs[j], spans[j][1])
            start_all(*(to_z if j + 1 == len(to) else to[j + 1 : j + 2]))

        def sum_z():
            for copy in to_z:
                copy.wait_recv()
            total = buf[own, :].astype(F32)
            for k in range(1, nz):
                total = total + recv_z[k - 1, :cut].astype(F32)
            res[own, :] = total.astype(BF16)
            start_all(*back_z)

        handed = [back_z] + [[copy] for copy in back[::-1]]
        follow = [[copy] for copy in back[::-1]] + [[out]]
        chain(
            name, first, *[functools.partial(half_sum, j) for j in range(len(to))], sum_z,
            *[then(a, *b) for a, b in zip(handed, follow)],
        )
        last_sends.extend(to + to_z + back_z + back)
        outs.append(out)

    halves = {"c": (core, dev_core), "x": (xbit, dev_x), "y": (ybit, dev_y)}
    f_base = sems(4)
    f_c0 = remote(r.ct.at[0], r.fc.at[0], f_base, dev_core)
    f_c1 = remote(r.ct.at[2], r.fc.at[1], f_base + 1, dev_core)
    f_y = [remote(r.ct.at[1, g], r.fy.at[g], f_base + 2 + g, dev_y) for g in range(2)]
    f_outs = [pltpu.make_async_copy(r.fo.at[g], r.fo_out.at[g], r.ls.at[3 + g]) for g in range(2)]
    last_sends, outs = list(f_y), []

    def ffn_across(g):
        f_y[g].wait_recv()
        add_rows(r.ct.at[3, g], 0, r.fy.at[g], D)

    for g in range(2):
        sum_chain(
            "F%d" % g, r.ct.at[3, g], r.fo.at[g], "x", [r.fx.at[g]], r.fz.at[g], f_outs[g],
            functools.partial(ffn_across, g),
        )

    def ffn(k, s, out):
        def tile(t):
            rows = rows_at(t * T, T)
            up = dot(r.hf[rows, :], r.wu[s])
            grad_act = dot_t(r.go[rows, :], r.wd[s])
            sq = up * up
            cubic = (GELU_SCALE * GELU_CUBIC) * sq
            tang = jnp.tanh(up * (GELU_SCALE + cubic))
            hu = 0.5 * up
            act = (hu + hu * tang).astype(BF16)
            slope = (0.5 + 0.5 * tang) + hu * (1.0 - tang * tang) * (GELU_SCALE + 3.0 * cubic)
            gup = (grad_act * slope).astype(BF16)
            r.gp[rows, :D] = act
            r.gp[rows, D : 2 * D] = gup
            add_acc(t, dot(act, r.wd[s]))
            add_acc(nt + t, dot_t(gup, r.wu[s]))

        loop("ffn_tile%d" % k, nt, tile)

        def grads(t):
            rows = rows_at(t * T, T)
            out[0, rows, :] = dot(r.hft[rows, :], r.gp[:, D : 2 * D]).astype(BF16)
            out[1, rows, :] = dot(r.got_t[rows, :], r.gp[:, :D]).astype(BF16)

        loop("ffn_grads%d" % k, D // T, grads)

    ffn(0, tp_far, r.ct.at[0])
    f_c0.start()
    ffn(1, tp_y, r.ct.at[1])
    f_c0.wait_recv()
    for g in range(2):
        add_rows(r.ct.at[1, g], 0, r.fc.at[0, g], D)
        f_y[g].start()
    ffn(2, tp_core, r.ct.at[2])
    f_c1.start()
    ffn(3, tp, r.ct.at[3])
    f_c1.wait_recv()
    for g in range(2):
        add_rows(r.ct.at[3, g], 0, r.fc.at[1, g], D)

    ones_row = lax.broadcasted_iota(jnp.int32, (2 * LANES, LANES), 0)
    ones_col = lax.broadcasted_iota(jnp.int32, (2 * LANES, LANES), 1)
    head_ones = (lax.div(lax.rem(ones_row, LANES), 64) == lax.div(ones_col, 64)).astype(F32).astype(BF16)
    r.gg[...] = jnp.zeros((2, 8, D), F32)

    def gn_at(c):
        return rows_at(lax.rem(c, 2) * T, T), pl.ds(pl.multiple_of(lax.div(c, 2) * T, T), T)

    def gn_of(p, c):
        at, wide_at = gn_at(c)
        return r.wd[p, at, wide_at]

    def fold(v):
        return jnp.sum(v.reshape(T // 8, 8, D), axis=0)

    for copy in w_sends:
        copy.wait_send()

    def back_middle(t):
        rows = rows_at(t * T, T)
        r.hf[rows, :] = acc(t).astype(BF16)
        res = r.res[rows, :]
        mean = jnp.mean(res, axis=-1, keepdims=True)
        cen = res - mean
        inv = lax.rsqrt(jnp.mean(cen * cen, axis=-1, keepdims=True) + NORM_EPS)
        n = cen * inv
        gh = acc(nt + t)
        r.gg[0] += fold(gh * n)
        sc = gh * r.gf[...]
        centre = jnp.mean(sc, axis=-1, keepdims=True)
        inner = jnp.mean(sc * n, axis=-1, keepdims=True)
        gres = r.go[rows, :].astype(F32) + inv * (sc - centre - n * inner)
        r.res[rows, :] = gres
        gattn = gres.astype(BF16)
        r.gp[rows, 2 * D :] = gattn
        gmi = dot_t(gattn, r.wo[...]) * r.inv[rows, :]
        w = gmi * r.mix[rows, :].astype(F32) * (-1.0)
        hi = w.astype(BF16)
        lo = (w - hi.astype(F32)).astype(BF16)
        gnum = gmi.astype(BF16)
        for p in range(npair):
            lanes = slice(p * LANES, (p + 1) * LANES)
            gden = dot(cat([hi[:, lanes], lo[:, lanes]], 1), head_ones).astype(BF16)
            at, wide_at = gn_at(t)
            r.wd[p, at, wide_at] = cat([gnum[:, lanes], gden * jnp.asarray(1.0 / 64.0, BF16)], 1)

    loop("back_middle", nt, back_middle)
    out_copy = pltpu.make_async_copy(r.hf, r.out, r.ls.at[12])
    out_copy.start()

    bpack, steps["B"], bcollect = state_exchange(1, r.bown, r.bgot)

    def state_back(i):
        p, c = lax.div(i, nt), nt - 1 - lax.rem(i, nt)
        rows = rows_at(c * T, T)

        @pl.when(c == nt - 1)
        def _():
            r.sl[p * (nt + 1) + nt] = jnp.zeros((M, M), F32)

        gain = merge(dot_c(gn_of(p, c) * twice(r.use[rows, :]), r.phiq[p, rows, :]))
        state = r.sc[c] * r.sl[p * (nt + 1) + c + 1] + gain
        r.sl[p * (nt + 1) + c] = state

    bleaves = (lambda i: lax.rem(i, nt) == nt - 1), (lambda i: bpack(lax.div(i, nt), 0))

    loop("state_back", npair * nt, state_back, [bleaves])

    half = D // 2
    for i, name in enumerate("OQ"):
        sum_chain(
            name, r.ct.at[0, i], r.wu.at[i], ORDER[name],
            [r.fc.at[0, i, :half], r.oq_a.at[i], r.oq_b.at[i]], r.oq_z.at[i],
            pltpu.make_async_copy(r.wu.at[i], r.oq_out.at[i], r.ls.at[5 + i]),
        )
    for p in range(npair):
        g, lanes = p // 2, slice((p % 2) * half, (p % 2 + 1) * half)
        sum_chain(
            "K%d" % p, r.ct.at[2, g, :, lanes], r.wu.at[2 + g, :, lanes], ORDER["K"],
            [r.fc.at[0, g, half:, lanes], r.kv_a.at[p], r.kv_b.at[p]], r.kv_z.at[p],
            pltpu.make_async_copy(r.wu.at[2 + g, :, lanes], r.kv_out.at[p], r.ls.at[7 + p]),
        )

    f_c0.wait_send()
    f_c1.wait_send()
    def out_grads():
        for t in range(D // T):
            rows = slice(t * T, (t + 1) * T)
            r.ct[0, 0, rows, :] = dot_c(r.mix[:, rows], r.gp[:, 2 * D :]).astype(BF16)

    once("out_grads", out_grads)

    def back_query(i):
        p, c = lax.div(i, nt), lax.rem(i, nt)
        rows = rows_at(c * T, T)
        vals, gn = r.vp[p, rows, :], gn_of(p, c)
        phi_q, phi_k = r.phiq[p, rows, :], r.phik[p, rows, :]
        g = dot_t(gn, cat([vals * low, vals * high], 0)).astype(BF16) * twice(r.mask[c])
        gphi = cat([dot(g[:, :M], phi_k[:, :M]), dot(g[:, M:], phi_k[:, M:])], 1)
        gphi = gphi + dot(gn * twice(r.use[rows, :]), r.st[i])
        t = (gphi * phi_q.astype(F32)).astype(BF16)
        o = dot_t(t, r.bb[p])
        gq = c4 * o[:, :LANES] - r.q[p, rows, :].astype(F32) * (o[:, LANES:] * 0.125)
        r.gp[rows, pl.ds(pl.multiple_of(p * LANES, LANES), LANES)] = gq.astype(BF16)

    loop("back_query", npair * nt, back_query)
    def query_grads():
        for t in range(D // T):
            rows = slice(t * T, (t + 1) * T)
            r.ct[0, 1, rows, :] = dot(r.ht[rows, :], r.gp[:, :D]).astype(BF16)

    once("query_grads", query_grads)
    bcollect(3 * nt + 4)

    def pair_grads(i):
        p = lax.div(i, nt)
        kv = cat(
            [r.gp[:, pl.ds(pl.multiple_of(o * D + p * LANES, LANES), LANES)] for o in (1, 2)], 1
        )
        wide_at = pl.ds(pl.multiple_of(lax.rem(p, 2) * half, half), half)
        for t in range(D // T):
            rows = slice(t * T, (t + 1) * T)
            r.ct[2, lax.div(p, 2), rows, wide_at] = dot(r.ht[rows, :], kv).astype(BF16)

    def back_key(i):
        p, c = lax.div(i, nt), lax.rem(i, nt)
        rows = rows_at(c * T, T)
        dstate = split((r.sl[p * (nt + 1) + c + 1] + r.sc[2 * nt + c] * r.tin[p]).astype(BF16))
        vals, gn = r.vp[p, rows, :], gn_of(p, c)
        phi_q, phi_k = r.phiq[p, rows, :], r.phik[p, rows, :]
        mask = twice(r.maskt[c])
        gt = cat([dot_t(vals * low, gn), dot_t(vals * high, gn)], 1).astype(BF16) * mask
        st = cat([dot_t(phi_k[:, :M], phi_q[:, :M]), dot_t(phi_k[:, M:], phi_q[:, M:])], 1)
        st = st.astype(BF16) * mask
        gphi = cat([dot(gt[:, :M], phi_q[:, :M]), dot(gt[:, M:], phi_q[:, M:])], 1)
        tail = r.tail[rows, :]
        gphi = gphi + dot(vals * twice(tail), dstate)
        gnum = gn[:, :LANES]
        gv = dot(st, cat([gnum * low[:, :LANES], gnum * high[:, :LANES]], 0))
        gv = gv + tail.astype(F32) * dot_t(phi_k, dstate[:LANES])
        t = (gphi * phi_k.astype(F32)).astype(BF16)
        o = dot_t(t, r.bb[p])
        gk = c4 * o[:, :LANES] - r.k[p, rows, :].astype(F32) * (o[:, LANES:] * 0.125)
        r.gp[rows, pl.ds(pl.multiple_of(D + p * LANES, LANES), LANES)] = gk.astype(BF16)
        r.gp[rows, pl.ds(pl.multiple_of(2 * D + p * LANES, LANES), LANES)] = gv.astype(BF16)

    loop("back_key", npair * nt, back_key, [((lambda i: lax.rem(i, nt) == nt - 1), pair_grads)])

    def back_first(t):
        rows = rows_at(t * T, T)
        gh = dot_t(r.gp[rows, :D], r.wq[...])
        gh = gh + dot_t(r.gp[rows, D : 2 * D], r.wk[...])
        gh = gh + dot_t(r.gp[rows, 2 * D :], r.wv[...])
        x = r.tok[rows, :].astype(F32)
        mean = jnp.mean(x, axis=-1, keepdims=True)
        cen = x - mean
        inv = lax.rsqrt(jnp.mean(cen * cen, axis=-1, keepdims=True) + NORM_EPS)
        n = cen * inv
        r.gg[1] += fold(gh * n)
        sc = gh * r.ga[...]
        centre = jnp.mean(sc, axis=-1, keepdims=True)
        inner = jnp.mean(sc * n, axis=-1, keepdims=True)
        r.res[rows, :] += inv * (sc - centre - n * inner)

    loop("back_first", nt, back_first)
    gt_copy = pltpu.make_async_copy(r.res, r.gt, r.ls.at[11])
    gt_copy.start()

    g_base = sems(3 + ndp - 1)
    r.g1[...] = cat([jnp.sum(r.gg[0], axis=0, keepdims=True), jnp.sum(r.gg[1], axis=0, keepdims=True),
                     jnp.zeros((6, D), F32)], 0)
    g_tp = [remote(r.g1, r.gr.at[k - 1], g_base + k - 1, (dp, lax.rem(tp + k, 4))) for k in (1, 2, 3)]
    g_dp = [
        remote(r.g2, r.gr.at[2 + k], g_base + 2 + k, (lax.rem(dp + k, ndp), tp)) for k in range(1, ndp)
    ]
    start_all(*g_tp)

    def gains_tp():
        for copy in g_tp:
            copy.wait_recv()
        r.g2[...] = r.g1[...] + r.gr[0] + r.gr[1] + r.gr[2]
        start_all(*g_dp)

    def gains_dp():
        total = r.g2[...]
        for k in range(1, ndp):
            g_dp[k - 1].wait_recv()
            total = total + r.gr[2 + k]
        r.gout[...] = total

    chain("G", gains_tp, gains_dp)
    advance("tail", 0)
    assert not plan and not any(steps.values()), (plan, {k: len(v) for k, v in steps.items() if v})

    for copy in seg_copies + last_sends + g_tp + g_dp:
        copy.wait_send()
    for copy in outs + [out_copy, gt_copy]:
        copy.wait()
    assert used[0] <= r.ss.shape[0]


def layer(tokens, segment_ids, grad_out, w_query, w_key, w_value, w_out, w_up, w_down, gain_attn,
          gain_ffn, feature_basis):
    _, L, D = tokens.shape
    H, DH, M = feature_basis.shape
    F = w_up.shape[1]
    npair, nt = H // 2, L // T
    ndp = lax.axis_size("dp")
    nz = ndp // 2
    assert lax.axis_size("tp") == 4 and F == D and DH == 64 and M == T

    vmem, hbm = pl.BlockSpec(memory_space=pltpu.VMEM), pl.BlockSpec(memory_space=pl.ANY)
    ins = {
        "seg": (segment_ids, vmem),
        "tok": (tokens[0], vmem),
        "go": (grad_out[0], vmem),
        "wq": (w_query, vmem),
        "wk": (w_key, vmem),
        "wv": (w_value, vmem),
        "wo": (w_out, vmem),
        "wup": (w_up, hbm),
        "wdn": (w_down, hbm),
        "ga": (gain_attn[None], vmem),
        "gf": (gain_ffn[None], vmem),
        "basis": (feature_basis, vmem),
    }
    outs = {
        "out": ((L, D), BF16, hbm),
        "gt": ((L, D), F32, hbm),
        "fo_out": ((2, D, F), BF16, hbm),
        "oq_out": ((2, D, D), BF16, hbm),
        "kv_out": ((npair, D, 2 * LANES), BF16, hbm),
        "gout": ((8, D), F32, vmem),
    }

    def all_sum_buffers(name, g, n):
        return {
            name + "_a": ((g, D // 4, n), BF16),
            name + "_b": ((g, D // 8, n), BF16),
            name + "_z": ((g, nz - 1, D // 8, n), BF16),
        }

    scratch = {
        "sg": ((4, 1, L), jnp.int32),
        "wu": ((4, D, F), BF16),
        "wd": ((4, F, D), BF16),
        "bb": ((npair, 2 * LANES, 2 * M), BF16),
        "ht": ((D, L), BF16),
        "q": ((npair, L, LANES), BF16),
        "k": ((npair, L, LANES), BF16),
        "vp": ((npair, L, 2 * LANES), BF16),
        "sc": ((3 * nt + 8, 1, M), F32),
        "use": ((L, LANES), BF16),
        "tail": ((L, LANES), BF16),
        "mask": ((nt, T, M), BF16),
        "maskt": ((nt, T, M), BF16),
        "phik": ((npair, L, 2 * M), BF16),
        "phiq": ((npair, L, 2 * M), BF16),
        "sl": ((npair * (nt + 1), M, M), F32),
        "own": ((npair, 160, M), BF16),
        "got": ((4, npair, 160, M), BF16),
        "bown": ((npair, 160, M), BF16),
        "bgot": ((4, npair, 160, M), BF16),
        "tin": ((npair, M, M), F32),
        "st": ((npair * nt, M, 2 * M), BF16),
        "inv": ((L, D), F32),
        "mix": ((L, D), BF16),
        "res": ((L, D), F32),
        "hf": ((L, D), BF16),
        "hft": ((D, L), BF16),
        "got_t": ((D, L), BF16),
        "ct": ((4, 2, D, F), BF16),
        "fc": ((2, 2, D, F), BF16),
        "fy": ((2, D, F), BF16),
        "fx": ((2, D // 2, F), BF16),
        "fz": ((2, nz - 1, D // 2 // nz, F), BF16),
        "fo": ((2, D, F), BF16),
        "gg": ((2, 8, D), F32),
        "gp": ((L, 3 * D), BF16),
        "g1": ((8, D), F32),
        "g2": ((8, D), F32),
        "gr": ((3 + ndp - 1, 8, D), F32),
    }
    scratch.update(all_sum_buffers("oq", 2, D))
    scratch.update(all_sum_buffers("kv", npair, 2 * LANES))
    n_sems = 3 + 7 + nz - 1 + 6 * npair + 4 + 2 * (2 + 2 * (nz - 1)) + 3 + ndp - 1
    n_sems += (2 + npair) * (6 + 2 * (nz - 1))
    names = list(ins) + list(outs) + list(scratch) + ["ls", "ss", "rs"]
    res = pl.pallas_call(
        functools.partial(layer_kernel, nz, names),
        out_shape=[jax.ShapeDtypeStruct(s, d) for s, d, _ in outs.values()],
        in_specs=[spec for _, spec in ins.values()],
        out_specs=[spec for _, _, spec in outs.values()],
        scratch_shapes=[pltpu.VMEM(s, d) for s, d in scratch.values()]
        + [
            pltpu.SemaphoreType.DMA((13,)),
            pltpu.SemaphoreType.DMA((n_sems,)),
            pltpu.SemaphoreType.DMA((n_sems,)),
        ],
        name="layer",
        compiler_params=pltpu.CompilerParams(
            collective_id=0, has_side_effects=True, vmem_limit_bytes=67043328
        ),
    )(*[a for a, _ in ins.values()])
    return hand_out(*res)


def hand_out_kernel(out, gt, up, down, oq, kv, gains, *refs):
    o_out, o_gt, o_query, o_key, o_value, o_proj, o_up, o_down, o_attn, o_ffn = refs
    o_out[0] = out[...]
    o_gt[0] = gt[...]
    o_up[...] = up[0].astype(F32)
    o_down[...] = down[0].astype(F32).T
    o_proj[...] = oq[0].astype(F32)
    o_query[...] = oq[1].astype(F32)
    for p in range(kv.shape[0]):
        lanes = slice(p * LANES, (p + 1) * LANES)
        o_key[:, lanes] = kv[p, :, :LANES].astype(F32)
        o_value[:, lanes] = kv[p, :, LANES:].astype(F32)
    o_ffn[...] = gains[0:1, :]
    o_attn[...] = gains[1:2, :]


def hand_out(out, gt, fo, oq, kv, gains):
    (L, D), npair, steps = out.shape, kv.shape[0], 4
    lr, dr = L // steps, D // steps
    tall = pl.BlockSpec((1, lr, D), lambda i: (0, i, 0))
    flat = pl.BlockSpec((dr, D), lambda i: (i, 0))
    row = pl.BlockSpec((1, D), lambda i: (0, 0))
    f32 = lambda *shape: jax.ShapeDtypeStruct(shape, F32)
    res = pl.pallas_call(
        hand_out_kernel,
        grid=(steps,),
        in_specs=[
            pl.BlockSpec((lr, D), lambda i: (i, 0)),
            pl.BlockSpec((lr, D), lambda i: (i, 0)),
            pl.BlockSpec((1, dr, D), lambda i: (0, i, 0)),
            pl.BlockSpec((1, D, dr), lambda i: (1, 0, i)),
            pl.BlockSpec((2, dr, D), lambda i: (0, i, 0)),
            pl.BlockSpec((npair, dr, 2 * LANES), lambda i: (0, i, 0)),
            pl.BlockSpec((8, D), lambda i: (0, 0)),
        ],
        out_specs=[tall, tall, flat, flat, flat, flat, flat, flat, row, row],
        out_shape=[jax.ShapeDtypeStruct((1, L, D), BF16), f32(1, L, D)]
        + [f32(D, D)] * 6 + [f32(1, D)] * 2,
        name="hand_out",
    )(out, gt, fo, fo, oq, kv, gains)
    return (*res[:8], res[8][0], res[9][0])


def solution(mesh):
    whole = P()
    in_specs = (
        P("dp", "tp", None), P("dp", "tp"), P("dp", "tp", None), whole, whole, whole, whole,
        P(None, "tp"), P("tp", None), whole, whole, whole,
    )
    out_specs = (
        P("dp", "tp", None), P("dp", "tp", None), whole, whole, whole, whole,
        P(None, "tp"), P("tp", None), whole, whole,
    )
    return jax.shard_map(layer, mesh=mesh, in_specs=in_specs, out_specs=out_specs, check_vma=False)
```

```python
import functools
import math
from types import SimpleNamespace

import jax
import jax.numpy as jnp
from jax import lax
from jax.experimental import pallas as pl
from jax.experimental.pallas import tpu as pltpu
from jax.sharding import PartitionSpec as P

MESH = pl.DeviceIdType.MESH
F32 = jnp.float32
BF16 = jnp.bfloat16
NORM_EPS = 1e-05
GELU_SCALE = 0.7978845608028654
GELU_CUBIC = 0.044715
LANES = 128
PLAN = (
    ("project", 1, "E"),
    ("key_side", 2, "D"),
    ("project_query", 0, "S"),
    ("project_query", 0, "U"),
    ("project_query", 3, "S"),
    ("query_side", 1, "D"),
    ("query_side", 4, "S"),
    ("query_side", 9, "S"),
    ("attend", 3, "D"),
    ("attend", 3, "U"),
    ("ffn_tile3", 2, "X"),
    ("back_middle", 2, "F0"),
    ("state_back", 13, "F1"),
    ("out_grads", 0, "B"),
    ("out_grads", 0, "O"),
    ("back_query", 2, "B"),
    ("back_query", 3, "O"),
    ("back_query", 4, "B"),
    ("back_query", 5, "F0"),
    ("back_query", 6, "B"),
    ("back_query", 11, "F1"),
    ("query_grads", 0, "Q"),
    ("query_grads", 0, "O"),
    ("back_key", 1, "Q"),
    ("back_key", 3, "K0"),
    ("back_key", 3, "F0"),
    ("back_key", 6, "K0"),
    ("back_key", 7, "K1"),
    ("back_key", 7, "Q"),
    ("back_key", 10, "K1"),
    ("back_key", 10, "F1"),
    ("back_key", 11, "K2"),
    ("back_key", 11, "K0"),
    ("back_key", 11, "O"),
    ("back_key", 14, "K2"),
    ("back_key", 15, "K3"),
    ("back_key", 15, "K1"),
    ("last_query", 2, "K3"),
    ("last_query", 2, "F0"),
    ("last_query", 3, "Q"),
    ("last_grads", 0, "Q3"),
    ("last_grads", 0, "K0"),
    ("back_first", 1, "F1"),
    ("back_first", 1, "Q3"),
    ("back_first", 1, "O"),
    ("back_first", 2, "K1"),
    ("back_first", 3, "K2"),
    ("tail", 0, "Q"),
    ("tail", 0, "K3"),
    ("tail", 0, "K0"),
    ("tail", 0, "G"),
    ("tail", 0, "K1"),
    ("tail", 0, "K2"),
    ("tail", 0, "K3"),
    ("tail", 0, "F0"),
    ("tail", 0, "Q3"),
    ("tail", 0, "G"),
    ("tail", 0, "K2"),
    ("tail", 0, "K3"),
    ("tail", 0, "O"),
    ("tail", 0, "Q3"),
    ("tail", 0, "O"),
    ("tail", 0, "Q"),
    ("tail", 0, "K0"),
    ("tail", 0, "Q"),
    ("tail", 0, "Q3"),
    ("tail", 0, "K0"),
    ("tail", 0, "K1"),
    ("tail", 0, "K2"),
    ("tail", 0, "K1"),
    ("tail", 0, "K2"),
    ("tail", 0, "K3"),
    ("tail", 0, "Q3"),
    ("tail", 0, "K3"),
    ("tail", 0, "Q3"),
)
UNROLL = {**{k: 2 for k in "project middle back_middle back_first back_key ffn_tile".split()}, **{k: 4 for k in "key_side query_side attend state_back back_query last_query".split()}}
STAGES = {"O": ("c", "xy"), "Q": ("c", "xy"), "K": ("c", "xy")}
T = 256


def dot(a, b):
    return jnp.dot(a, b, preferred_element_type=F32)


def dot_t(a, b):
    return lax.dot_general(a, b, (((1,), (1,)), ((), ())), preferred_element_type=F32)


def dot_c(a, b):
    return lax.dot_general(a, b, (((0,), (0,)), ((), ())), preferred_element_type=F32)


def rows_at(start, size):
    return pl.ds(pl.multiple_of(start, 16), size)


def cat(parts, axis):
    return jnp.concatenate(parts, axis=axis)


def lane_groups():
    lane = lax.broadcasted_iota(jnp.int32, (1, 2 * LANES), 1)
    first = lax.rem(lane, LANES) < 64
    one = jnp.where(first, 1.0, 0.0)
    return one.astype(BF16), (1.0 - one).astype(BF16)


def layer_kernel(nz, names, *refs):
    r = SimpleNamespace(**dict(zip(names, refs)))
    L, D = r.tok.shape
    nt = L // T
    npair = r.basis_in.shape[0] // 2
    M = r.basis_in.shape[2]
    c4 = 64.0**-0.25
    exp_scale = c4 * math.log2(math.e)

    dp, tp = lax.axis_index("dp"), lax.axis_index("tp")
    ndp = 2 * nz
    core, ybit = lax.rem(tp, 2), lax.div(tp, 2)
    xbit, zi = lax.rem(dp, 2), lax.div(dp, 2)
    tp_core, tp_y, tp_far = tp + 1 - 2 * core, lax.rem(tp + 2, 4), 3 - tp
    dev_core, dev_y, dev_far = (dp, tp_core), (dp, tp_y), (dp, tp_far)
    dev_x = (dp + 1 - 2 * xbit, tp)

    def z_at(k):
        return lax.rem(zi + k, nz)

    def dev_z(k):
        return (z_at(k) * 2 + xbit, tp)

    plan, steps = {}, {}
    for place, i, chunk in PLAN:
        plan.setdefault((place, i), []).append(chunk)

    def advance(place, i):
        for chunk in plan.pop((place, i), ()):
            steps[chunk].pop(0)()

    def loop(name, n, body, tasks=()):
        u = UNROLL.get(name.rstrip("0123"), 1)

        def step(i, _):
            for k in range(u):
                body(i * u + k)
            for when, task in tasks:
                pl.when(when(i * u + u - 1))(functools.partial(task, i * u + u - 1))
            for k in range(n):
                if (name, k) in plan:
                    pl.when(i == k // u)(functools.partial(advance, name, k))
            return 0

        lax.fori_loop(0, n // u, step, 0)

    def once(name, body):
        body()
        advance(name, 0)

    used = [0]

    def sems(n):
        first = used[0]
        used[0] += n
        return first

    def remote(src, dst, idx, dev):
        return pltpu.make_async_remote_copy(
            src_ref=src, dst_ref=dst, send_sem=r.ss.at[idx], recv_sem=r.rs.at[idx],
            device_id=dev, device_id_type=MESH,
        )

    loads = {
        name: pltpu.make_async_copy(getattr(r, name + "_in"), getattr(r, name), r.ls.at[14 + k])
        for k, name in enumerate(("tok", "wk", "wv", "wq", "wo", "go"))
    }
    own_up = pltpu.make_async_copy(r.wup, r.wu.at[tp], r.ls.at[0])
    own_down = pltpu.make_async_copy(r.wdn, r.wd.at[tp], r.ls.at[1])
    own_seg = pltpu.make_async_copy(r.seg, r.sg.at[tp], r.ls.at[2])
    basis_copies = [
        pltpu.make_async_copy(
            r.basis_in.at[h], r.bb.at[h // 2, pl.ds((h % 2) * 64, 64), pl.ds((h % 2) * M, M)], r.ls.at[20 + h]
        )
        for h in range(2 * npair)
    ]
    own_seg.start()
    for copy in list(loads.values()) + basis_copies:
        copy.start()
    own_up.start()
    own_down.start()

    barrier = pltpu.get_barrier_semaphore()
    for k in (1, 2, 3):
        pl.semaphore_signal(barrier, inc=1, device_id=(dp, lax.rem(tp + k, 4)), device_id_type=MESH)
    for k in range(1, ndp):
        pl.semaphore_signal(barrier, inc=1, device_id=(lax.rem(dp + k, ndp), tp), device_id_type=MESH)


    seg_base = sems(3)
    seg_copies = [
        remote(r.seg, r.sg.at[tp], seg_base + k - 1, (dp, lax.rem(tp + k, 4))) for k in (1, 2, 3)
    ]

    up_base, down_base = sems(5), sems(4 + nz - 1)
    pr = r.wdn.shape[0] // ndp
    up_core = remote(r.wup, r.wu.at[tp], up_base, dev_core)
    hd = r.wup.shape[0] // 2
    up_y = [
        remote(r.wup.at[pl.ds(g * hd, hd)], r.wu.at[tp, pl.ds(g * hd, hd)], up_base + 1 + g, dev_y)
        for g in range(2)
    ]
    up_on = [
        remote(r.wu.at[tp_y, pl.ds(g * hd, hd)], r.wu.at[tp_y, pl.ds(g * hd, hd)], up_base + 3 + g, dev_core)
        for g in range(2)
    ]
    down_core = remote(r.wdn, r.wd.at[tp], down_base, dev_core)
    down_piece = rows_at((xbit * nz + zi) * pr, pr)
    down_plane = rows_at(xbit * nz * pr, nz * pr)
    down_y = remote(r.wdn.at[down_piece], r.wd.at[tp, down_piece], down_base + 1, dev_y)
    down_z = [
        remote(r.wd.at[tp_y, down_piece], r.wd.at[tp_y, down_piece], down_base + 3 + k, dev_z(k))
        for k in range(1, nz)
    ]
    down_x = remote(r.wd.at[tp_y, down_plane], r.wd.at[tp_y, down_plane], down_base + 2, dev_x)
    down_on = remote(r.wd.at[tp_y], r.wd.at[tp_y], down_base + 3, dev_core)
    w_sends = [up_core, down_core, down_y, down_x, down_on] + up_y + up_on + down_z

    def start_all(*copies):
        for copy in copies:
            copy.start()

    def chain(name, *tasks):
        steps[name] = list(tasks)

    def then(waits, *starts):
        def task():
            for copy in waits:
                copy.wait_recv()
            start_all(*starts)

        return task

    chain("U", then(up_y[:1], up_on[0]), then(up_y[1:], up_on[1]))
    chain("D", then([down_y], *down_z), then(down_z, down_x), then([down_x], down_on))

    def enter():
        pl.semaphore_wait(barrier, 3 + ndp - 1)
        start_all(*seg_copies, down_y, up_y[0], up_core, down_core)

    steps["E"] = [enter]

    def basis_blocks():
        zero, one = jnp.zeros((64, M), BF16), jnp.ones((64, M), BF16)
        for p in range(npair):
            for h in range(2):
                lanes = slice(h * M, (h + 1) * M)
                r.bb[p, (1 - h) * 64 : (2 - h) * 64, lanes] = zero
                r.bb[p, LANES:, lanes] = cat([one, zero, one, zero] if h == 0 else [zero, one, zero, one], 0)
        for copy in basis_copies:
            copy.wait()

    once("basis_blocks", basis_blocks)
    low, high = lane_groups()

    def project(t):
        rows = rows_at(t * T, T)
        x = r.tok[rows, :].astype(F32)
        mean = jnp.mean(x, axis=-1, keepdims=True)
        cen = x - mean
        inv = lax.rsqrt(jnp.mean(cen * cen, axis=-1, keepdims=True) + NORM_EPS)
        hid = ((cen * inv) * r.ga[...]).astype(BF16)
        r.hf[rows, :] = hid
        k = dot(hid, r.wk[...]).astype(BF16)
        v = dot(hid, r.wv[...]).astype(BF16)
        for p in range(npair):
            lanes = slice(p * LANES, (p + 1) * LANES)
            r.k[p, rows, :] = k[:, lanes]
            r.vp[p, rows, :LANES] = v[:, lanes]
            r.vp[p, rows, LANES:] = jnp.ones((T, LANES), BF16)

    loads["tok"].wait()
    loads["wk"].wait()
    loads["wv"].wait()
    loop("project", nt, project)

    own_seg.wait()
    for copy in seg_copies:
        copy.wait_recv()
    row_max, row_min = [], []
    for j in range(4):
        ids = r.sg[j].astype(F32)
        row_max.append(jnp.max(ids, axis=1, keepdims=True))
        row_min.append(jnp.min(ids, axis=1, keepdims=True))
    in_seg = jnp.full((1, 1), -1.0, F32)
    for j in range(4):
        in_seg = jnp.maximum(in_seg, jnp.where(j < tp, row_max[j], -1.0))
    mine = r.seg[...].astype(F32)
    ends = [jnp.max(mine[:, c * T : (c + 1) * T], axis=1, keepdims=True) for c in range(nt)]
    befores = [in_seg] + ends[:-1]
    keeps = [(befores[c] == ends[c]).astype(F32) for c in range(nt)]
    wide = lambda v: jnp.broadcast_to(v, (1, M))
    flag = jnp.ones((1, 1), F32)
    for c in range(nt):
        r.sc[c] = wide(keeps[c])
        r.sc[nt + c] = wide(flag)
        flag = flag * keeps[c]
    flag = jnp.ones((1, 1), F32)
    for c in reversed(range(nt)):
        r.sc[2 * nt + c] = wide(flag)
        flag = flag * keeps[c]
    for j in range(4):
        r.sc[3 * nt + j] = wide(jnp.where(j < tp, (row_max[j] == in_seg).astype(F32), 0.0))
        r.sc[3 * nt + 4 + j] = wide(jnp.where(j > tp, (row_min[j] == ends[-1]).astype(F32), 0.0))
    row_id = lax.broadcasted_iota(jnp.int32, (T, T), 0)
    col_id = lax.broadcasted_iota(jnp.int32, (T, T), 1)
    for c in range(nt):
        along = mine[:, c * T : (c + 1) * T]
        down = jnp.broadcast_to(along, (LANES, T)).T
        rows = slice(c * T, (c + 1) * T)
        use = (down == befores[c]).astype(F32).astype(BF16)
        tail = (down == ends[c]).astype(F32).astype(BF16)
        r.use[rows, :] = use
        r.tail[rows, :] = tail

    def masks(c):
        along = mine[:, c * T : (c + 1) * T]
        down = jnp.broadcast_to(along, (LANES, T)).T
        same = (cat([down, down], 1) == along).astype(F32)
        mask = (same * (row_id >= col_id).astype(F32)).astype(BF16)
        mask_t = (same * (row_id <= col_id).astype(F32)).astype(BF16)
        r.mask[c] = mask
        r.maskt[c] = mask_t

    def twice(v):
        return cat([v, v], 1)

    def features(u, p):
        wide_u = u.astype(F32)
        square = wide_u * wide_u * (-1.0 / (16.0 * c4))
        hi = square.astype(BF16)
        lo = (square - hi.astype(F32)).astype(BF16)
        expo = dot(cat([u, hi], 1), r.bb[p, : 2 * LANES]) + dot(lo, r.bb[p, 2 * LANES :])
        return jnp.exp2(expo * exp_scale).astype(BF16)

    def merge(u):
        return cat([u[:64, :M], u[64:128, M:], u[128:192, :M], u[192:, M:]], 0)

    def split(s):
        zero = jnp.zeros((64, M), s.dtype)
        first = cat([s[:64], zero, s[128:192], zero], 0)
        second = cat([zero, s[64:128], zero, s[192:]], 0)
        return cat([first, second], 1)

    def state_exchange(i, own, got):
        base = sems(3 * npair)

        def copies(p):
            at = base + p * 3
            return (
                remote(own.at[p], got.at[tp, p], at, dev_core),
                remote(own.at[p], got.at[tp, p], at + 1, dev_y),
                remote(got.at[tp_y, p], got.at[tp_y, p], at + 2, dev_core),
            )

        def pack(p, slot):
            state = r.sl[p * (nt + 1) + slot]
            own[p, :128, :] = state[:128].astype(BF16)
            own[p, 128:, :] = cat([state[128:136], state[192:200]], 0).astype(BF16)
            to_core, to_y, _ = copies(p)
            to_y.start()
            to_core.start()

        def relay(p):
            _, to_y, on = copies(p)
            to_y.wait_recv()
            on.start()

        def collect(first):
            def one(p, _):
                to_core, to_y, on = copies(p)
                to_core.wait_recv()
                on.wait_recv()
                total = jnp.zeros((144, M), F32)
                for k, slot in enumerate((tp_core, tp_y, tp_far)):
                    total = total + got[slot, p].astype(F32) * r.sc[first + slot]
                r.tin[p, :128, :] = total[:128]
                r.tin[p, 128:192, :] = jnp.broadcast_to(total[128:129], (64, M))
                r.tin[p, 192:, :] = jnp.broadcast_to(total[136:137], (64, M))
                to_core.wait_send()
                to_y.wait_send()
                on.wait_send()
                return 0

            lax.fori_loop(0, npair, one, 0)

        return pack, [functools.partial(relay, p) for p in range(npair)], collect

    pack, steps["S"], collect = state_exchange(0, r.own, r.got)

    def key_side(i):
        p, c = lax.div(i, nt), lax.rem(i, nt)
        rows = rows_at(c * T, T)
        phi = features(r.k[p, rows, :], p)
        r.phik[p, rows, :] = phi
        gain = merge(dot_c(r.vp[p, rows, :] * twice(r.tail[rows, :]), phi))

        @pl.when(c == 0)
        def _():
            r.sl[p * (nt + 1)] = jnp.zeros((M, M), F32)

        state = r.sc[c] * r.sl[p * (nt + 1) + c] + gain
        r.sl[p * (nt + 1) + c + 1] = state

    leaves = (lambda i: lax.rem(i, nt) == nt - 1), (lambda i: pack(lax.div(i, nt), nt))

    loop("key_side", npair * nt, key_side, [leaves])

    up_y[1].start()

    def project_query(t):
        rows = rows_at(t * T, T)
        hid = r.hf[rows, :]
        r.ht[:, pl.ds(pl.multiple_of(t * T, LANES), T)] = hid.T
        q = dot(hid, r.wq[...]).astype(BF16)
        for p in range(npair):
            r.q[p, rows, :] = q[:, p * LANES : (p + 1) * LANES]

    loads["wq"].wait()
    loop("project_query", nt, project_query)

    def query_side(i):
        p, c = lax.div(i, nt), lax.rem(i, nt)
        rows = rows_at(c * T, T)
        r.phiq[p, rows, :] = features(r.q[p, rows, :], p)

    loop("query_side", npair * nt, query_side)

    def all_masks():
        for c in range(nt):
            masks(c)

    once("all_masks", all_masks)
    collect(3 * nt)

    def attend(i):
        p, c = lax.div(i, nt), lax.rem(i, nt)
        rows = rows_at(c * T, T)
        state = (r.sl[p * (nt + 1) + c] + r.sc[nt + c] * r.tin[p]).astype(BF16)
        state = split(state)
        r.st[i] = state
        phi_q, phi_k = r.phiq[p, rows, :], r.phik[p, rows, :]
        scores = cat([dot_t(phi_q[:, :M], phi_k[:, :M]), dot_t(phi_q[:, M:], phi_k[:, M:])], 1)
        scores = scores.astype(BF16) * twice(r.mask[c])
        vals = r.vp[p, rows, :]
        both = dot(scores, cat([vals * low, vals * high], 0))
        both = both + twice(r.use[rows, :].astype(F32)) * dot_t(phi_q, state)
        inv = 1.0 / both[:, LANES:]
        lanes = pl.ds(pl.multiple_of(p * LANES, LANES), LANES)
        r.inv[rows, lanes] = inv
        r.mix[rows, lanes] = (both[:, :LANES] * inv).astype(BF16)

    loop("attend", npair * nt, attend)

    def acc(t):
        return cat([r.sl[2 * t], r.sl[2 * t + 1]], 1)

    def add_acc(t, v):
        r.sl[2 * t] += v[:, :M]
        r.sl[2 * t + 1] += v[:, M:]

    def middle(t):
        rows = rows_at(t * T, T)
        res = r.tok[rows, :].astype(F32) + dot(r.mix[rows, :], r.wo[...])
        r.res[rows, :] = res
        mean = jnp.mean(res, axis=-1, keepdims=True)
        cen = res - mean
        inv = lax.rsqrt(jnp.mean(cen * cen, axis=-1, keepdims=True) + NORM_EPS)
        r.hf[rows, :] = ((cen * inv) * r.gf[...]).astype(BF16)
        r.sl[2 * t] = res[:, :M]
        r.sl[2 * t + 1] = res[:, M:]
        r.sl[2 * nt + 2 * t] = jnp.zeros((T, M), F32)
        r.sl[2 * nt + 2 * t + 1] = jnp.zeros((T, M), F32)

    loads["wo"].wait()
    loop("middle", nt, middle)
    loads["go"].wait()
    own_up.wait()
    own_down.wait()
    up_core.wait_recv()
    down_core.wait_recv()
    for copy in up_on:
        copy.wait_recv()
    down_on.wait_recv()
    def transposes():
        for t in range(nt):
            rows = slice(t * T, (t + 1) * T)
            r.hft[:, rows] = r.hf[rows, :].T
            r.got_t[:, rows] = r.go[rows, :].T

    once("transposes", transposes)

    def add_rows(dst, start, src, n):
        step = min(n, 128)

        def one(b, _):
            at = rows_at(start + b * step, step)
            dst[at, :] = dst[at, :] + src[rows_at(b * step, step), :]
            return 0

        lax.fori_loop(0, n // step, one, 0)

    bits = {"c": core, "x": xbit, "y": ybit}

    def flips(axes):
        out = [""]
        for axis in axes:
            out = out + [f + axis for f in out]
        return out[1:]

    def device(flip):
        to = {"": tp, "c": tp_core, "y": tp_y, "cy": tp_far}["".join(a for a in "cy" if a in flip)]
        return (dp + 1 - 2 * xbit if "x" in flip else dp, to)

    def place(axes, flip):
        index = 0
        for axis in axes:
            index = index * 2 + (1 - bits[axis] if axis in flip else bits[axis])
        return index

    def sum_chain(name, buf, res, stages, recvs, recv_z, out, starts=True, extra=None):
        start, n, to, back, spans = 0, buf.shape[0], [], [], []
        count = sum(len(flips(axes)) for axes in stages)
        base = sems(2 * count + 2 * (nz - 1))
        for axes, recv in zip(stages, recvs):
            n = n // 2 ** len(axes)
            others = flips(axes)
            to.append([])
            back.append([])
            here = start + place(axes, "") * n
            kept = rows_at(here, n)
            for flip, landing in zip(others, recv):
                there = rows_at(start + place(axes, flip) * n, n)
                to[-1].append(remote(buf.at[there], landing, base, device(flip)))
                back[-1].append(remote(res.at[kept], res.at[kept], base + 1, device(flip)))
                base = base + 2
            start = here
            spans.append((start, n))
        base = base - 1
        cut = n // nz if (n // nz) % 16 == 0 else n
        share = cut != n
        piece = lambda z: rows_at(start + (z * cut if share else 0), cut)
        to_z = [
            remote(buf.at[piece(z_at(k))], recv_z.at[k - 1, :cut], base + k, dev_z(k))
            for k in range(1, nz)
        ]
        own = piece(zi)
        back_z = [
            remote(res.at[own], res.at[own], base + nz - 1 + k, dev_z(k)) for k in range(1, nz)
        ] if share else []

        def part_sum(j):
            for copy in to[j]:
                copy.wait_recv()
            for landing in recvs[j]:
                add_rows(buf, spans[j][0], landing, spans[j][1])
            if extra is not None:
                extra(spans[j])
            start_all(*(to_z if j + 1 == len(to) else to[j + 1]))

        def sum_z():
            for copy in to_z:
                copy.wait_recv()
            total = buf[own, :].astype(F32)
            for k in range(1, nz):
                total = total + recv_z[k - 1, :cut].astype(F32)
            res[own, :] = total.astype(BF16)
            start_all(*back_z)

        handed = [back_z] + back[::-1]
        follow = back[::-1] + [[out]]
        first = [functools.partial(start_all, *to[0])] if starts else []
        chain(
            name, *first, *[functools.partial(part_sum, j) for j in range(len(to))], sum_z,
            *[then(a, *b) for a, b in zip(handed, follow)],
        )
        for group in to + [to_z, back_z] + back:
            last_sends.extend(group)
        outs.append(out)
        return to[0]

    f_base = sems(5)
    f_c0 = remote(r.ct.at[0], r.fc.at[0], f_base, dev_core)
    f_c1 = remote(r.ct.at[2], r.fc.at[1], f_base + 1, dev_core)
    f_part = rows_at(xbit * (D // 2), D // 2)
    f_other = rows_at((1 - xbit) * (D // 2), D // 2)
    f_y = remote(r.ct.at[1, 0], r.fy.at[0], f_base + 2, dev_y)
    f_x = remote(r.ct.at[1, 1, f_other], r.fy.at[1, D // 2 :], f_base + 3, dev_x)
    f_xy = remote(r.ct.at[1, 1, f_part], r.fy.at[1, : D // 2], f_base + 4, dev_y)
    f_outs = [pltpu.make_async_copy(r.fo.at[g], r.fo_out.at[g], r.ls.at[3 + g]) for g in range(2)]
    last_sends, outs = [f_y, f_x, f_xy], []

    def across_up():
        f_y.wait_recv()
        add_rows(r.ct.at[3, 0], 0, r.fy.at[0], D)
        start_all(*f0)

    def plane_down():
        f_x.wait_recv()
        add_rows(r.ct.at[1, 1], xbit * (D // 2), r.fy.at[1, D // 2 :], D // 2)
        f_xy.start()

    def across_down(span):
        f_xy.wait_recv()
        add_rows(r.ct.at[3, 1], span[0], r.fy.at[1, : D // 2], span[1])

    f0 = sum_chain(
        "F0", r.ct.at[3, 0], r.fo.at[0], ["x"], [[r.fx.at[0]]], r.fz.at[0], f_outs[0], False
    )
    f1 = sum_chain(
        "F1", r.ct.at[3, 1], r.fo.at[1], ["x"], [[r.fx.at[1]]], r.fz.at[1], f_outs[1], False, across_down
    )
    steps["F0"].insert(0, across_up)
    chain("X", plane_down)

    def ffn(k, s, out):
        def tile(t):
            rows = rows_at(t * T, T)
            up = dot(r.hf[rows, :], r.wu[s])
            grad_act = dot_t(r.go[rows, :], r.wd[s])
            sq = up * up
            cubic = (GELU_SCALE * GELU_CUBIC) * sq
            tang = jnp.tanh(up * (GELU_SCALE + cubic))
            hu = 0.5 * up
            act = (hu + hu * tang).astype(BF16)
            slope = (0.5 + 0.5 * tang) + hu * (1.0 - tang * tang) * (GELU_SCALE + 3.0 * cubic)
            gup = (grad_act * slope).astype(BF16)
            r.gp[rows, :D] = act
            r.gp[rows, D : 2 * D] = gup
            add_acc(t, dot(act, r.wd[s]))
            add_acc(nt + t, dot_t(gup, r.wu[s]))

        loop("ffn_tile%d" % k, nt, tile)

        def grads(t):
            rows = rows_at(t * T, T)
            out[0, rows, :] = dot(r.hft[rows, :], r.gp[:, D : 2 * D]).astype(BF16)
            out[1, rows, :] = dot(r.got_t[rows, :], r.gp[:, :D]).astype(BF16)

        loop("ffn_grads%d" % k, D // T, grads)

    ffn(0, tp_far, r.ct.at[0])
    f_c0.start()
    ffn(1, tp_y, r.ct.at[1])
    f_c0.wait_recv()
    add_rows(r.ct.at[1, 1], 0, r.fc.at[0, 1], D)
    f_x.start()
    add_rows(r.ct.at[1, 0], 0, r.fc.at[0, 0], D)
    f_y.start()
    ffn(2, tp_core, r.ct.at[2])
    f_c1.start()
    ffn(3, tp, r.ct.at[3])
    f_c1.wait_recv()
    add_rows(r.ct.at[3, 1], 0, r.fc.at[1, 1], D)
    start_all(*f1)
    add_rows(r.ct.at[3, 0], 0, r.fc.at[1, 0], D)

    ones_row = lax.broadcasted_iota(jnp.int32, (2 * LANES, LANES), 0)
    ones_col = lax.broadcasted_iota(jnp.int32, (2 * LANES, LANES), 1)
    head_ones = (lax.div(lax.rem(ones_row, LANES), 64) == lax.div(ones_col, 64)).astype(F32).astype(BF16)
    r.gg[...] = jnp.zeros((2, 8, D), F32)

    def gn_at(c):
        return rows_at(lax.rem(c, 2) * T, T), pl.ds(pl.multiple_of(lax.div(c, 2) * T, T), T)

    def gn_of(p, c):
        at, wide_at = gn_at(c)
        return r.wd[p, at, wide_at]

    def fold(v):
        return jnp.sum(v.reshape(T // 8, 8, D), axis=0)

    for copy in w_sends:
        copy.wait_send()

    def back_middle(t):
        rows = rows_at(t * T, T)
        r.hf[rows, :] = acc(t).astype(BF16)
        res = r.res[rows, :]
        mean = jnp.mean(res, axis=-1, keepdims=True)
        cen = res - mean
        inv = lax.rsqrt(jnp.mean(cen * cen, axis=-1, keepdims=True) + NORM_EPS)
        n = cen * inv
        gh = acc(nt + t)
        r.gg[0] += fold(gh * n)
        sc = gh * r.gf[...]
        centre = jnp.mean(sc, axis=-1, keepdims=True)
        inner = jnp.mean(sc * n, axis=-1, keepdims=True)
        gres = r.go[rows, :].astype(F32) + inv * (sc - centre - n * inner)
        r.res[rows, :] = gres
        gattn = gres.astype(BF16)
        r.gp[rows, 2 * D :] = gattn
        gmi = dot_t(gattn, r.wo[...]) * r.inv[rows, :]
        w = gmi * r.mix[rows, :].astype(F32) * (-1.0)
        hi = w.astype(BF16)
        lo = (w - hi.astype(F32)).astype(BF16)
        gnum = gmi.astype(BF16)
        for p in range(npair):
            lanes = slice(p * LANES, (p + 1) * LANES)
            gden = dot(cat([hi[:, lanes], lo[:, lanes]], 1), head_ones).astype(BF16)
            at, wide_at = gn_at(t)
            r.wd[p, at, wide_at] = cat([gnum[:, lanes], gden * jnp.asarray(1.0 / 64.0, BF16)], 1)

    loop("back_middle", nt, back_middle)
    out_copy = pltpu.make_async_copy(r.hf, r.out, r.ls.at[13])
    out_copy.start()

    bpack, steps["B"], bcollect = state_exchange(1, r.own, r.bgot)

    def state_back(i):
        p, c = lax.div(i, nt), nt - 1 - lax.rem(i, nt)
        rows = rows_at(c * T, T)

        @pl.when(c == nt - 1)
        def _():
            r.sl[p * (nt + 1) + nt] = jnp.zeros((M, M), F32)

        gain = merge(dot_c(gn_of(p, c) * twice(r.use[rows, :]), r.phiq[p, rows, :]))
        state = r.sc[c] * r.sl[p * (nt + 1) + c + 1] + gain
        r.sl[p * (nt + 1) + c] = state

    bleaves = (lambda i: lax.rem(i, nt) == nt - 1), (lambda i: bpack(lax.div(i, nt), 0))

    loop("state_back", npair * nt, state_back, [bleaves])

    half = D // 2
    parts = [("O", 0, 0, D), ("Q", 1, 0, D - LANES), ("Q3", 1, D - LANES, LANES)]
    parts = parts + [("K%d" % p, 2 + p // 2, (p % 2) * half, half) for p in range(npair)]
    for i, (name, g, lane, n) in enumerate(parts):
        lanes = slice(lane, lane + n)
        core_land = r.fc.at[0, g, :half, lanes] if g < 2 else r.fc.at[0, g - 2, half:, lanes]
        stages = STAGES["K" if name == "Q3" else name[0]]
        recvs, at = [[core_land]], 0
        rows = D // 2
        for axes in stages[1:]:
            rows = rows // 2 ** len(axes)
            recvs.append([r.land.at[g, pl.ds(at + k * rows, rows), lanes] for k in range(2 ** len(axes) - 1)])
            at = at + rows * (2 ** len(axes) - 1)
        rz = r.land_z.at[g, :, :, lanes]
        source = r.ct.at[0 if g < 2 else 2, g % 2, :, lanes]
        sum_chain(
            name, source, r.wu.at[g, :, lanes], stages, recvs, rz,
            pltpu.make_async_copy(r.wu.at[g, :, lanes], r.grads.at[g, :, lanes], r.ls.at[5 + i]),
        )

    f_c0.wait_send()
    f_c1.wait_send()
    def out_grads():
        for t in range(D // T):
            rows = slice(t * T, (t + 1) * T)
            r.ct[0, 0, rows, :] = dot_c(r.mix[:, rows], r.gp[:, 2 * D :]).astype(BF16)

    once("out_grads", out_grads)

    def back_query(i):
        p, c = lax.div(i, nt), lax.rem(i, nt)
        rows = rows_at(c * T, T)
        vals, gn = r.vp[p, rows, :], gn_of(p, c)
        phi_q, phi_k = r.phiq[p, rows, :], r.phik[p, rows, :]
        g = dot_t(gn, cat([vals * low, vals * high], 0)).astype(BF16) * twice(r.mask[c])
        used = gn * twice(r.use[rows, :])
        gphi = cat([dot(g[:, :M], phi_k[:, :M]), dot(g[:, M:], phi_k[:, M:])], 1)
        gphi = gphi + dot(used, r.st[i])
        t = (gphi * phi_q.astype(F32)).astype(BF16)
        o = dot_t(t, r.bb[p, : 2 * LANES])
        gq = c4 * o[:, :LANES] - r.q[p, rows, :].astype(F32) * (o[:, LANES:] * 0.125)
        r.gp[rows, pl.ds(pl.multiple_of(p * LANES, LANES), LANES)] = gq.astype(BF16)

    loop("back_query", (npair - 1) * nt, back_query)
    def query_grads(lanes):
        for t in range(D // T):
            rows = slice(t * T, (t + 1) * T)
            r.ct[0, 1, rows, lanes] = dot(r.ht[rows, :], r.gp[:, lanes]).astype(BF16)

    once("query_grads", lambda: query_grads(slice(0, D - LANES)))
    bcollect(3 * nt + 4)

    def pair_grads(i):
        p = lax.div(i, nt)
        kv = cat(
            [r.gp[:, pl.ds(pl.multiple_of(o * D + p * LANES, LANES), LANES)] for o in (1, 2)], 1
        )
        wide_at = pl.ds(pl.multiple_of(lax.rem(p, 2) * half, half), half)
        for t in range(D // T):
            rows = slice(t * T, (t + 1) * T)
            r.ct[2, lax.div(p, 2), rows, wide_at] = dot(r.ht[rows, :], kv).astype(BF16)

    def back_key(i):
        p, c = lax.div(i, nt), lax.rem(i, nt)
        rows = rows_at(c * T, T)
        dstate = split((r.sl[p * (nt + 1) + c + 1] + r.sc[2 * nt + c] * r.tin[p]).astype(BF16))
        vals, gn = r.vp[p, rows, :], gn_of(p, c)
        phi_q, phi_k = r.phiq[p, rows, :], r.phik[p, rows, :]
        mask = twice(r.maskt[c])
        gt = cat([dot_t(vals * low, gn), dot_t(vals * high, gn)], 1).astype(BF16) * mask
        st = cat([dot_t(phi_k[:, :M], phi_q[:, :M]), dot_t(phi_k[:, M:], phi_q[:, M:])], 1)
        st = st.astype(BF16) * mask
        tail = r.tail[rows, :]
        left = vals * twice(tail)
        gphi = cat(
            [
                dot(cat([gt[:, m], left], 1), cat([phi_q[:, m], dstate[:, m]], 0))
                for m in (slice(0, M), slice(M, 2 * M))
            ],
            1,
        )
        gnum = gn[:, :LANES]
        gv = dot(st, cat([gnum * low[:, :LANES], gnum * high[:, :LANES]], 0))
        gv = gv + tail.astype(F32) * dot_t(phi_k, dstate[:LANES])
        t = (gphi * phi_k.astype(F32)).astype(BF16)
        o = dot_t(t, r.bb[p, : 2 * LANES])
        gk = c4 * o[:, :LANES] - r.k[p, rows, :].astype(F32) * (o[:, LANES:] * 0.125)
        r.gp[rows, pl.ds(pl.multiple_of(D + p * LANES, LANES), LANES)] = gk.astype(BF16)
        r.gp[rows, pl.ds(pl.multiple_of(2 * D + p * LANES, LANES), LANES)] = gv.astype(BF16)

    loop("back_key", npair * nt, back_key, [((lambda i: lax.rem(i, nt) == nt - 1), pair_grads)])

    loop("last_query", nt, lambda c: back_query((npair - 1) * nt + c))
    once("last_grads", lambda: query_grads(slice(D - LANES, D)))

    def back_first(t):
        rows = rows_at(t * T, T)
        gh = dot_t(r.gp[rows, :D], r.wq[...])
        gh = gh + dot_t(r.gp[rows, D : 2 * D], r.wk[...])
        gh = gh + dot_t(r.gp[rows, 2 * D :], r.wv[...])
        x = r.tok[rows, :].astype(F32)
        mean = jnp.mean(x, axis=-1, keepdims=True)
        cen = x - mean
        inv = lax.rsqrt(jnp.mean(cen * cen, axis=-1, keepdims=True) + NORM_EPS)
        n = cen * inv
        r.gg[1] += fold(gh * n)
        sc = gh * r.ga[...]
        centre = jnp.mean(sc, axis=-1, keepdims=True)
        inner = jnp.mean(sc * n, axis=-1, keepdims=True)
        r.res[rows, :] += inv * (sc - centre - n * inner)

    loop("back_first", nt, back_first)
    gt_copy = pltpu.make_async_copy(r.res, r.gt, r.ls.at[3 + 9])
    gt_copy.start()

    g_base = sems(3 + ndp - 1)
    sums = [jnp.sum(r.gg[k], axis=0, keepdims=True) for k in range(2)]
    r.g1[...] = cat([v[:, j : j + LANES] for v in sums for j in range(0, D, LANES)], 0)
    g_tp = [remote(r.g1, r.gr.at[k - 1], g_base + k - 1, (dp, lax.rem(tp + k, 4))) for k in (1, 2, 3)]
    g_dp = [
        remote(r.g2, r.gr.at[2 + k], g_base + 2 + k, (lax.rem(dp + k, ndp), tp)) for k in range(1, ndp)
    ]
    start_all(*g_tp)

    def gains_tp():
        for copy in g_tp:
            copy.wait_recv()
        r.g2[...] = r.g1[...] + r.gr[0] + r.gr[1] + r.gr[2]
        start_all(*g_dp)

    def gains_dp():
        total = r.g2[...]
        for k in range(1, ndp):
            g_dp[k - 1].wait_recv()
            total = total + r.gr[2 + k]
        r.gout[...] = total

    chain("G", gains_tp, gains_dp)
    advance("tail", 0)
    assert not plan and not any(steps.values()), (plan, {k: len(v) for k, v in steps.items() if v})

    for copy in seg_copies + last_sends + g_tp + g_dp:
        copy.wait_send()
    for copy in outs + [out_copy, gt_copy]:
        copy.wait()
    assert used[0] <= r.ss.shape[0]


def layer(tokens, segment_ids, grad_out, w_query, w_key, w_value, w_out, w_up, w_down, gain_attn,
          gain_ffn, feature_basis):
    _, L, D = tokens.shape
    H, DH, M = feature_basis.shape
    F = w_up.shape[1]
    npair, nt = H // 2, L // T
    ndp = lax.axis_size("dp")
    nz = ndp // 2
    assert lax.axis_size("tp") == 4 and F == D and DH == 64 and M == T

    vmem, hbm = pl.BlockSpec(memory_space=pltpu.VMEM), pl.BlockSpec(memory_space=pl.ANY)
    ins = {
        "seg": (segment_ids, vmem),
        "tok_in": (tokens[0], hbm),
        "go_in": (grad_out[0], hbm),
        "wq_in": (w_query, hbm),
        "wk_in": (w_key, hbm),
        "wv_in": (w_value, hbm),
        "wo_in": (w_out, hbm),
        "wup": (w_up, hbm),
        "wdn": (w_down, hbm),
        "ga": (gain_attn[None], vmem),
        "gf": (gain_ffn[None], vmem),
        "basis_in": (feature_basis, hbm),
    }
    outs = {
        "out": ((L, D), BF16, hbm),
        "gt": ((L, D), F32, hbm),
        "fo_out": ((2, D, F), BF16, hbm),
        "grads": ((4, D, D), BF16, hbm),
        "gout": ((8, LANES), F32, vmem),
    }

    scratch = {
        "tok": ((L, D), BF16),
        "wk": ((D, D), BF16),
        "wv": ((D, D), BF16),
        "wq": ((D, D), BF16),
        "wo": ((D, D), BF16),
        "go": ((L, D), BF16),
        "sg": ((4, 1, L), jnp.int32),
        "wu": ((4, D, F), BF16),
        "wd": ((4, F, D), BF16),
        "bb": ((npair, 3 * LANES, 2 * M), BF16),
        "ht": ((D, L), BF16),
        "q": ((npair, L, LANES), BF16),
        "k": ((npair, L, LANES), BF16),
        "vp": ((npair, L, 2 * LANES), BF16),
        "sc": ((3 * nt + 8, 1, M), F32),
        "use": ((L, LANES), BF16),
        "tail": ((L, LANES), BF16),
        "mask": ((nt, T, M), BF16),
        "maskt": ((nt, T, M), BF16),
        "phik": ((npair, L, 2 * M), BF16),
        "phiq": ((npair, L, 2 * M), BF16),
        "sl": ((npair * (nt + 1), M, M), F32),
        "own": ((npair, 144, M), BF16),
        "got": ((4, npair, 144, M), BF16),
        "bgot": ((4, npair, 144, M), BF16),
        "tin": ((npair, M, M), F32),
        "st": ((npair * nt, M, 2 * M), BF16),
        "inv": ((L, D), F32),
        "mix": ((L, D), BF16),
        "res": ((L, D), F32),
        "hf": ((L, D), BF16),
        "hft": ((D, L), BF16),
        "got_t": ((D, L), BF16),
        "ct": ((4, 2, D, F), BF16),
        "fc": ((2, 2, D, F), BF16),
        "land": ((4, 192, D), BF16),
        "land_z": ((4, nz - 1, D // 8, D), BF16),
        "fy": ((2, D, F), BF16),
        "fx": ((2, D // 2, F), BF16),
        "fz": ((2, nz - 1, D // 2 // nz, F), BF16),
        "fo": ((2, D, F), BF16),
        "gg": ((2, 8, D), F32),
        "gp": ((L, 3 * D), BF16),
        "g1": ((8, LANES), F32),
        "g2": ((8, LANES), F32),
        "gr": ((3 + ndp - 1, 8, LANES), F32),
    }
    n_sems = 40 + 6 * npair + ndp + (4 + npair) * (10 + 2 * (nz - 1)) + 5 * (nz - 1)
    names = list(ins) + list(outs) + list(scratch) + ["ls", "ss", "rs"]
    res = pl.pallas_call(
        functools.partial(layer_kernel, nz, names),
        out_shape=[jax.ShapeDtypeStruct(s, d) for s, d, _ in outs.values()],
        in_specs=[spec for _, spec in ins.values()],
        out_specs=[spec for _, _, spec in outs.values()],
        scratch_shapes=[pltpu.VMEM(s, d) for s, d in scratch.values()]
        + [
            pltpu.SemaphoreType.DMA((28,)),
            pltpu.SemaphoreType.DMA((n_sems,)),
            pltpu.SemaphoreType.DMA((n_sems,)),
        ],
        name="layer",
        compiler_params=pltpu.CompilerParams(
            collective_id=0, has_side_effects=True, vmem_limit_bytes=67043328
        ),
    )(*[a for a, _ in ins.values()])
    return hand_out(*res)


def hand_out_kernel(out, gt, up, down, grads, gains, *refs):
    o_out, o_gt, o_query, o_key, o_value, o_proj, o_up, o_down, o_attn, o_ffn = refs
    o_out[0] = out[...]
    o_gt[0] = gt[...]
    o_up[...] = up[0].astype(F32)
    o_down[...] = down[0].astype(F32).T
    o_proj[...] = grads[0].astype(F32)
    o_query[...] = grads[1].astype(F32)
    for p in range(grads.shape[2] // LANES):
        lanes = slice(p * LANES, (p + 1) * LANES)
        at = (p % 2) * 2 * LANES
        o_key[:, lanes] = grads[2 + p // 2, :, at : at + LANES].astype(F32)
        o_value[:, lanes] = grads[2 + p // 2, :, at + LANES : at + 2 * LANES].astype(F32)
    for j in range(4):
        lanes = slice(j * LANES, (j + 1) * LANES)
        o_ffn[:, lanes] = gains[j : j + 1, :]
        o_attn[:, lanes] = gains[4 + j : 5 + j, :]


def hand_out(out, gt, fo, grads, gains):
    (L, D), steps = out.shape, 4
    lr, dr = L // steps, D // steps
    tall = pl.BlockSpec((1, lr, D), lambda i: (0, i, 0))
    flat = pl.BlockSpec((dr, D), lambda i: (i, 0))
    row = pl.BlockSpec((1, D), lambda i: (0, 0))
    f32 = lambda *shape: jax.ShapeDtypeStruct(shape, F32)
    res = pl.pallas_call(
        hand_out_kernel,
        grid=(steps,),
        in_specs=[
            pl.BlockSpec((lr, D), lambda i: (i, 0)),
            pl.BlockSpec((lr, D), lambda i: (i, 0)),
            pl.BlockSpec((1, dr, D), lambda i: (0, i, 0)),
            pl.BlockSpec((1, D, dr), lambda i: (1, 0, i)),
            pl.BlockSpec((4, dr, D), lambda i: (0, i, 0)),
            pl.BlockSpec((8, LANES), lambda i: (0, 0)),
        ],
        out_specs=[tall, tall, flat, flat, flat, flat, flat, flat, row, row],
        out_shape=[jax.ShapeDtypeStruct((1, L, D), BF16), f32(1, L, D)]
        + [f32(D, D)] * 6 + [f32(1, D)] * 2,
        name="hand_out",
    )(out, gt, fo, fo, grads, gains)
    return (*res[:8], res[8][0], res[9][0])


def solution(mesh):
    whole = P()
    in_specs = (
        P("dp", "tp", None), P("dp", "tp"), P("dp", "tp", None), whole, whole, whole, whole,
        P(None, "tp"), P("tp", None), whole, whole, whole,
    )
    out_specs = (
        P("dp", "tp", None), P("dp", "tp", None), whole, whole, whole, whole,
        P(None, "tp"), P("tp", None), whole, whole,
    )
    return jax.shard_map(layer, mesh=mesh, in_specs=in_specs, out_specs=out_specs, check_vma=False)
```

```python
import functools
import math
from types import SimpleNamespace

import jax
import jax.numpy as jnp
from jax import lax
from jax.experimental import pallas as pl
from jax.experimental.pallas import tpu as pltpu
from jax.sharding import PartitionSpec as P

MESH = pl.DeviceIdType.MESH
F32 = jnp.float32
BF16 = jnp.bfloat16
NORM_EPS = 1e-05
GELU_SCALE = 0.7978845608028654
GELU_CUBIC = 0.044715
LANES = 128
PLAN = (
    ("project", 1, "E"),
    ("key_side", 3, "D"),
    ("project_query", 0, "U"),
    ("query_side", 3, "S"),
    ("query_side", 11, "S"),
    ("query_side", 15, "D"),
    ("attend", 3, "S"),
    ("attend", 7, "S"),
    ("middle", 3, "U"),
    ("middle", 3, "D"),
    ("ffn_tile3", 3, "X"),
    ("back_middle", 3, "F0"),
    ("out_grads", 0, "O"),
    ("out_grads", 0, "F1"),
    ("back_query", 3, "B"),
    ("back_query", 3, "O"),
    ("back_query", 7, "B"),
    ("back_query", 11, "B"),
    ("back_query", 11, "F0"),
    ("back_query", 11, "B"),
    ("query_grads", 0, "Q"),
    ("back_key", 3, "O"),
    ("back_key", 3, "F1"),
    ("back_key", 3, "K0"),
    ("back_key", 3, "Q"),
    ("back_key", 5, "K0"),
    ("back_key", 7, "O"),
    ("back_key", 7, "K1"),
    ("back_key", 9, "F0"),
    ("back_key", 9, "K1"),
    ("back_key", 11, "K2"),
    ("back_key", 11, "Q"),
    ("back_key", 13, "K2"),
    ("back_key", 13, "K0"),
    ("back_key", 15, "F1"),
    ("back_key", 15, "K1"),
    ("back_key", 15, "K3"),
    ("back_key", 15, "Q"),
    ("last_query", 3, "O"),
    ("last_query", 3, "K3"),
    ("last_query", 3, "K2"),
    ("last_grads", 0, "Q3"),
    ("back_first", 1, "Q3"),
    ("tail", 0, "F0"),
    ("tail", 0, "K0"),
    ("tail", 0, "F1"),
    ("tail", 0, "K1"),
    ("tail", 0, "G"),
    ("tail", 0, "Q"),
    ("tail", 0, "K3"),
    ("tail", 0, "O"),
    ("tail", 0, "Q3"),
    ("tail", 0, "K2"),
    ("tail", 0, "K0"),
    ("tail", 0, "K1"),
    ("tail", 0, "G"),
    ("tail", 0, "F0"),
    ("tail", 0, "Q"),
    ("tail", 0, "K3"),
    ("tail", 0, "O"),
    ("tail", 0, "Q3"),
    ("tail", 0, "K2"),
    ("tail", 0, "Q"),
    ("tail", 0, "K0"),
    ("tail", 0, "K0"),
    ("tail", 0, "K1"),
    ("tail", 0, "K3"),
    ("tail", 0, "Q3"),
    ("tail", 0, "O"),
    ("tail", 0, "K1"),
    ("tail", 0, "Q"),
    ("tail", 0, "O"),
    ("tail", 0, "K2"),
    ("tail", 0, "Q"),
    ("tail", 0, "K2"),
    ("tail", 0, "K3"),
    ("tail", 0, "Q3"),
    ("tail", 0, "K3"),
    ("tail", 0, "Q3"),
)
UNROLL = {
    "project": 2,
    "middle": 2,
    "back_middle": 2,
    "back_first": 2,
    "back_key": 2,
    "ffn_tile": 2,
    "key_side": 4,
    "query_side": 4,
    "attend": 4,
    "state_back": 4,
    "back_query": 4,
    "last_query": 4,
}
STAGES = {"O": ("c", "y", "x"), "Q": ("c", "x", "y"), "K": ("c", "xy")}
T = 256


def dot(a, b):
    return jnp.dot(a, b, preferred_element_type=F32)


def dot_t(a, b):
    return lax.dot_general(a, b, (((1,), (1,)), ((), ())), preferred_element_type=F32)


def dot_c(a, b):
    return lax.dot_general(a, b, (((0,), (0,)), ((), ())), preferred_element_type=F32)


def rows_at(start, size):
    return pl.ds(pl.multiple_of(start, 16), size)


def cat(parts, axis):
    return jnp.concatenate(parts, axis=axis)


def lane_groups():
    lane = lax.broadcasted_iota(jnp.int32, (1, 2 * LANES), 1)
    first = lax.rem(lane, LANES) < 64
    one = jnp.where(first, 1.0, 0.0)
    return one.astype(BF16), (1.0 - one).astype(BF16)


def layer_kernel(nz, names, *refs):
    r = SimpleNamespace(**dict(zip(names, refs)))
    L, D = r.tok.shape
    nt = L // T
    npair = r.basis_in.shape[0] // 2
    M = r.basis_in.shape[2]
    c4 = 64.0**-0.25
    exp_scale = c4 * math.log2(math.e)

    dp, tp = lax.axis_index("dp"), lax.axis_index("tp")
    ndp = 2 * nz
    core, ybit = lax.rem(tp, 2), lax.div(tp, 2)
    xbit, zi = lax.rem(dp, 2), lax.div(dp, 2)
    tp_core, tp_y, tp_far = tp + 1 - 2 * core, lax.rem(tp + 2, 4), 3 - tp
    dev_core, dev_y, dev_far = (dp, tp_core), (dp, tp_y), (dp, tp_far)
    dev_x = (dp + 1 - 2 * xbit, tp)

    def z_at(k):
        return lax.rem(zi + k, nz)

    def dev_z(k):
        return (z_at(k) * 2 + xbit, tp)

    plan, steps = {}, {}
    for place, i, chunk in PLAN:
        plan.setdefault((place, i), []).append(chunk)

    def advance(place, i):
        for chunk in plan.pop((place, i), ()):
            steps[chunk].pop(0)()

    def loop(name, n, body, tasks=(), before=None):
        u = UNROLL.get(name.rstrip("0123"), 1)

        def step(i, _):
            if before is not None:
                pl.when(lax.rem(i * u, nt) == 0)(lambda: before(lax.div(i * u, nt)))
            for k in range(u):
                body(i * u + k)
            for when, task in tasks:
                pl.when(when(i * u + u - 1))(functools.partial(task, i * u + u - 1))
            for k in range(n):
                if (name, k) in plan:
                    pl.when(i == k // u)(functools.partial(advance, name, k))
            return 0

        lax.fori_loop(0, n // u, step, 0)

    def once(name, body):
        body()
        advance(name, 0)

    used = [0]

    def sems(n):
        first = used[0]
        used[0] += n
        return first

    def remote(src, dst, idx, dev):
        return pltpu.make_async_remote_copy(
            src_ref=src, dst_ref=dst, send_sem=r.ss.at[idx], recv_sem=r.rs.at[idx],
            device_id=dev, device_id_type=MESH,
        )

    loads = {
        name: pltpu.make_async_copy(getattr(r, name + "_in"), getattr(r, name), r.ls.at[14 + k])
        for k, name in enumerate(("tok", "wk", "wv", "wq", "wo", "go"))
    }
    own_up = pltpu.make_async_copy(r.wup, r.wu.at[tp], r.ls.at[0])
    own_down = pltpu.make_async_copy(r.wdn, r.wd.at[tp], r.ls.at[1])
    own_seg = pltpu.make_async_copy(r.seg, r.sg.at[tp], r.ls.at[2])
    basis_copies = [
        pltpu.make_async_copy(
            r.basis_in.at[h], r.bb.at[h // 2, pl.ds((h % 2) * 64, 64), pl.ds((h % 2) * M, M)], r.ls.at[20 + h]
        )
        for h in range(2 * npair)
    ]
    own_seg.start()
    for copy in list(loads.values()) + basis_copies:
        copy.start()
    own_up.start()
    own_down.start()

    barrier = pltpu.get_barrier_semaphore()
    for k in (1, 2, 3):
        pl.semaphore_signal(barrier, inc=1, device_id=(dp, lax.rem(tp + k, 4)), device_id_type=MESH)
    for k in range(1, ndp):
        pl.semaphore_signal(barrier, inc=1, device_id=(lax.rem(dp + k, ndp), tp), device_id_type=MESH)


    seg_base = sems(3)
    seg_copies = [
        remote(r.seg, r.sg.at[tp], seg_base + k - 1, (dp, lax.rem(tp + k, 4))) for k in (1, 2, 3)
    ]

    up_base, down_base = sems(5), sems(4 + nz - 1)
    pr = r.wdn.shape[0] // ndp
    up_core = remote(r.wup, r.wu.at[tp], up_base, dev_core)
    hd = r.wup.shape[0] // 2
    up_y = [
        remote(r.wup.at[pl.ds(g * hd, hd)], r.wu.at[tp, pl.ds(g * hd, hd)], up_base + 1 + g, dev_y)
        for g in range(2)
    ]
    up_on = [
        remote(r.wu.at[tp_y, pl.ds(g * hd, hd)], r.wu.at[tp_y, pl.ds(g * hd, hd)], up_base + 3 + g, dev_core)
        for g in range(2)
    ]
    down_core = remote(r.wdn, r.wd.at[tp], down_base, dev_core)
    down_piece = rows_at((xbit * nz + zi) * pr, pr)
    down_plane = rows_at(xbit * nz * pr, nz * pr)
    down_y = remote(r.wdn.at[down_piece], r.wd.at[tp, down_piece], down_base + 1, dev_y)
    down_z = [
        remote(r.wd.at[tp_y, down_piece], r.wd.at[tp_y, down_piece], down_base + 3 + k, dev_z(k))
        for k in range(1, nz)
    ]
    down_x = remote(r.wd.at[tp_y, down_plane], r.wd.at[tp_y, down_plane], down_base + 2, dev_x)
    down_on = remote(r.wd.at[tp_y], r.wd.at[tp_y], down_base + 3, dev_core)
    w_sends = [up_core, down_core, down_y, down_x, down_on] + up_y + up_on + down_z

    def start_all(*copies):
        for copy in copies:
            copy.start()

    def chain(name, *tasks):
        steps[name] = list(tasks)

    def then(waits, *starts):
        def task():
            for copy in waits:
                copy.wait_recv()
            start_all(*starts)

        return task

    chain("U", then(up_y[:1], up_on[0]), then(up_y[1:], up_on[1]))
    chain("D", then([down_y], *down_z), then(down_z, down_x), then([down_x], down_on))

    def enter():
        pl.semaphore_wait(barrier, 3 + ndp - 1)
        start_all(*seg_copies, down_y, up_y[0], up_core, down_core)

    steps["E"] = [enter]

    def basis_blocks():
        zero, one = jnp.zeros((64, M), BF16), jnp.ones((64, M), BF16)
        for p in range(npair):
            for h in range(2):
                lanes = slice(h * M, (h + 1) * M)
                r.bb[p, (1 - h) * 64 : (2 - h) * 64, lanes] = zero
                r.bb[p, LANES:, lanes] = cat([one, zero, one, zero] if h == 0 else [zero, one, zero, one], 0)
        for copy in basis_copies:
            copy.wait()

    once("basis_blocks", basis_blocks)
    low, high = lane_groups()

    def project(t):
        rows = rows_at(t * T, T)
        x = r.tok[rows, :].astype(F32)
        mean = jnp.mean(x, axis=-1, keepdims=True)
        cen = x - mean
        inv = lax.rsqrt(jnp.mean(cen * cen, axis=-1, keepdims=True) + NORM_EPS)
        hid = ((cen * inv) * r.ga[...]).astype(BF16)
        r.hf[rows, :] = hid
        k = dot(hid, r.wk[...]).astype(BF16)
        v = dot(hid, r.wv[...]).astype(BF16)
        for p in range(npair):
            lanes = slice(p * LANES, (p + 1) * LANES)
            r.k[p, rows, :] = k[:, lanes]
            r.vp[p, rows, :LANES] = v[:, lanes]
            r.vp[p, rows, LANES:] = jnp.ones((T, LANES), BF16)

    loads["tok"].wait()
    loads["wk"].wait()
    loads["wv"].wait()
    loop("project", nt, project)

    own_seg.wait()
    for copy in seg_copies:
        copy.wait_recv()
    row_max, row_min = [], []
    for j in range(4):
        ids = r.sg[j].astype(F32)
        row_max.append(jnp.max(ids, axis=1, keepdims=True))
        row_min.append(jnp.min(ids, axis=1, keepdims=True))
    in_seg = jnp.full((1, 1), -1.0, F32)
    for j in range(4):
        in_seg = jnp.maximum(in_seg, jnp.where(j < tp, row_max[j], -1.0))
    mine = r.seg[...].astype(F32)
    ends = [jnp.max(mine[:, c * T : (c + 1) * T], axis=1, keepdims=True) for c in range(nt)]
    befores = [in_seg] + ends[:-1]
    keeps = [(befores[c] == ends[c]).astype(F32) for c in range(nt)]
    wide = lambda v: jnp.broadcast_to(v, (1, M))
    flag = jnp.ones((1, 1), F32)
    for c in range(nt):
        r.sc[c] = wide(keeps[c])
        r.sc[nt + c] = wide(flag)
        flag = flag * keeps[c]
    flag = jnp.ones((1, 1), F32)
    for c in reversed(range(nt)):
        r.sc[2 * nt + c] = wide(flag)
        flag = flag * keeps[c]
    for j in range(4):
        r.sc[3 * nt + j] = wide(jnp.where(j < tp, (row_max[j] == in_seg).astype(F32), 0.0))
        r.sc[3 * nt + 4 + j] = wide(jnp.where(j > tp, (row_min[j] == ends[-1]).astype(F32), 0.0))
    row_id = lax.broadcasted_iota(jnp.int32, (T, T), 0)
    col_id = lax.broadcasted_iota(jnp.int32, (T, T), 1)
    for c in range(nt):
        along = mine[:, c * T : (c + 1) * T]
        down = jnp.broadcast_to(along, (LANES, T)).T
        rows = slice(c * T, (c + 1) * T)
        use = (down == befores[c]).astype(F32).astype(BF16)
        tail = (down == ends[c]).astype(F32).astype(BF16)
        r.use[rows, :] = use
        r.tail[rows, :] = tail

    def masks(c):
        along = mine[:, c * T : (c + 1) * T]
        down = jnp.broadcast_to(along, (LANES, T)).T
        same = (cat([down, down], 1) == along).astype(F32)
        mask = (same * (row_id >= col_id).astype(F32)).astype(BF16)
        mask_t = (same * (row_id <= col_id).astype(F32)).astype(BF16)
        r.mask[c] = mask
        r.maskt[c] = mask_t

    def twice(v):
        return cat([v, v], 1)

    def features(u, p):
        wide_u = u.astype(F32)
        square = wide_u * wide_u * (-1.0 / (16.0 * c4))
        hi = square.astype(BF16)
        lo = (square - hi.astype(F32)).astype(BF16)
        expo = dot(cat([u, hi], 1), r.bb[p, : 2 * LANES]) + dot(lo, r.bb[p, 2 * LANES :])
        return jnp.exp2(expo * exp_scale).astype(BF16)

    def merge(u):
        return cat([u[:64, :M], u[64:128, M:], u[128:192, :M], u[192:, M:]], 0)

    def split(s):
        zero = jnp.zeros((64, M), s.dtype)
        first = cat([s[:64], zero, s[128:192], zero], 0)
        second = cat([zero, s[64:128], zero, s[192:]], 0)
        return cat([first, second], 1)

    def state_exchange(i, own, got):
        base = sems(3 * npair)

        def copies(p):
            at = base + p * 3
            return (
                remote(own.at[p], got.at[tp, p], at, dev_core),
                remote(own.at[p], got.at[tp, p], at + 1, dev_y),
                remote(got.at[tp_y, p], got.at[tp_y, p], at + 2, dev_core),
            )

        def pack(p, slot):
            state = r.sl[p * (nt + 1) + slot]
            own[p, :128, :] = state[:128].astype(BF16)
            own[p, 128:, :] = cat([state[128:136], state[192:200]], 0).astype(BF16)
            to_core, to_y, _ = copies(p)
            to_y.start()
            to_core.start()

        def relay(p):
            _, to_y, on = copies(p)
            to_y.wait_recv()
            on.start()

        def collect(p):
            to_core, to_y, on = copies(p)
            to_core.wait_recv()
            on.wait_recv()
            total = jnp.zeros((144, M), F32)
            for slot in (tp_core, tp_y, tp_far):
                total = total + got[slot, p].astype(F32) * r.sc[3 * nt + 4 * i + slot]
            r.tin[p, :128, :] = total[:128]
            r.tin[p, 128:192, :] = jnp.broadcast_to(total[128:129], (64, M))
            r.tin[p, 192:, :] = jnp.broadcast_to(total[136:137], (64, M))
            to_core.wait_send()
            to_y.wait_send()
            on.wait_send()

        return pack, [functools.partial(relay, p) for p in range(npair)], collect

    pack, steps["S"], collect = state_exchange(0, r.own, r.got)

    def key_side(i):
        p, c = lax.div(i, nt), lax.rem(i, nt)
        rows = rows_at(c * T, T)
        phi = features(r.k[p, rows, :], p)
        r.phik[p, rows, :] = phi
        gain = merge(dot_c(r.vp[p, rows, :] * twice(r.tail[rows, :]), phi))

        @pl.when(c == 0)
        def _():
            r.sl[p * (nt + 1)] = jnp.zeros((M, M), F32)

        state = r.sc[c] * r.sl[p * (nt + 1) + c] + gain
        r.sl[p * (nt + 1) + c + 1] = state

    leaves = (lambda i: lax.rem(i, nt) == nt - 1), (lambda i: pack(lax.div(i, nt), nt))

    loop("key_side", npair * nt, key_side, [leaves])

    up_y[1].start()

    def project_query(t):
        rows = rows_at(t * T, T)
        hid = r.hf[rows, :]
        r.ht[:, pl.ds(pl.multiple_of(t * T, LANES), T)] = hid.T
        q = dot(hid, r.wq[...]).astype(BF16)
        for p in range(npair):
            r.q[p, rows, :] = q[:, p * LANES : (p + 1) * LANES]

    loads["wq"].wait()
    loop("project_query", nt, project_query)

    def query_side(i):
        p, c = lax.div(i, nt), lax.rem(i, nt)
        rows = rows_at(c * T, T)
        r.phiq[p, rows, :] = features(r.q[p, rows, :], p)

    loop("query_side", npair * nt, query_side)

    def all_masks():
        for c in range(nt):
            masks(c)

    once("all_masks", all_masks)

    def attend(i):
        p, c = lax.div(i, nt), lax.rem(i, nt)
        rows = rows_at(c * T, T)
        state = (r.sl[p * (nt + 1) + c] + r.sc[nt + c] * r.tin[p]).astype(BF16)
        state = split(state)
        r.st[i] = state
        phi_q, phi_k = r.phiq[p, rows, :], r.phik[p, rows, :]
        scores = cat([dot_t(phi_q[:, :M], phi_k[:, :M]), dot_t(phi_q[:, M:], phi_k[:, M:])], 1)
        scores = scores.astype(BF16) * twice(r.mask[c])
        vals = r.vp[p, rows, :]
        both = dot(scores, cat([vals * low, vals * high], 0))
        both = both + twice(r.use[rows, :].astype(F32)) * dot_t(phi_q, state)
        inv = 1.0 / both[:, LANES:]
        lanes = pl.ds(pl.multiple_of(p * LANES, LANES), LANES)
        r.inv[rows, lanes] = inv
        r.mix[rows, lanes] = (both[:, :LANES] * inv).astype(BF16)

    loop("attend", npair * nt, attend, before=collect)

    def acc(t):
        return cat([r.sl[2 * t], r.sl[2 * t + 1]], 1)

    def add_acc(t, v):
        r.sl[2 * t] += v[:, :M]
        r.sl[2 * t + 1] += v[:, M:]

    def middle(t):
        rows = rows_at(t * T, T)
        res = r.tok[rows, :].astype(F32) + dot(r.mix[rows, :], r.wo[...])
        r.res[rows, :] = res
        mean = jnp.mean(res, axis=-1, keepdims=True)
        cen = res - mean
        inv = lax.rsqrt(jnp.mean(cen * cen, axis=-1, keepdims=True) + NORM_EPS)
        r.hf[rows, :] = ((cen * inv) * r.gf[...]).astype(BF16)
        r.sl[2 * t] = res[:, :M]
        r.sl[2 * t + 1] = res[:, M:]
        r.sl[2 * nt + 2 * t] = jnp.zeros((T, M), F32)
        r.sl[2 * nt + 2 * t + 1] = jnp.zeros((T, M), F32)

    loads["wo"].wait()
    loop("middle", nt, middle)
    loads["go"].wait()
    own_up.wait()
    own_down.wait()
    up_core.wait_recv()
    down_core.wait_recv()
    for copy in up_on:
        copy.wait_recv()
    down_on.wait_recv()
    def transposes():
        for t in range(nt):
            rows = slice(t * T, (t + 1) * T)
            r.hft[:, rows] = r.hf[rows, :].T
            r.got_t[:, rows] = r.go[rows, :].T

    once("transposes", transposes)

    def add_rows(dst, start, src, n):
        step = min(n, 128)

        def one(b, _):
            at = rows_at(start + b * step, step)
            dst[at, :] = dst[at, :] + src[rows_at(b * step, step), :]
            return 0

        lax.fori_loop(0, n // step, one, 0)

    bits = {"c": core, "x": xbit, "y": ybit}

    def flips(axes):
        out = [""]
        for axis in axes:
            out = out + [f + axis for f in out]
        return out[1:]

    def device(flip):
        to = {"": tp, "c": tp_core, "y": tp_y, "cy": tp_far}["".join(a for a in "cy" if a in flip)]
        return (dp + 1 - 2 * xbit if "x" in flip else dp, to)

    def place(axes, flip):
        index = 0
        for axis in axes:
            index = index * 2 + (1 - bits[axis] if axis in flip else bits[axis])
        return index

    def sum_chain(name, buf, res, stages, recvs, recv_z, out, starts=True, extra=None):
        start, n, to, back, spans = 0, buf.shape[0], [], [], []
        count = sum(len(flips(axes)) for axes in stages)
        base = sems(2 * count + 2 * (nz - 1))
        for axes, recv in zip(stages, recvs):
            n = n // 2 ** len(axes)
            others = flips(axes)
            to.append([])
            back.append([])
            here = start + place(axes, "") * n
            kept = rows_at(here, n)
            for flip, landing in zip(others, recv):
                there = rows_at(start + place(axes, flip) * n, n)
                to[-1].append(remote(buf.at[there], landing, base, device(flip)))
                back[-1].append(remote(res.at[kept], res.at[kept], base + 1, device(flip)))
                base = base + 2
            start = here
            spans.append((start, n))
        base = base - 1
        cut = n // nz if (n // nz) % 16 == 0 else n
        share = cut != n
        piece = lambda z: rows_at(start + (z * cut if share else 0), cut)
        to_z = [
            remote(buf.at[piece(z_at(k))], recv_z.at[k - 1, :cut], base + k, dev_z(k))
            for k in range(1, nz)
        ]
        own = piece(zi)
        back_z = [
            remote(res.at[own], res.at[own], base + nz - 1 + k, dev_z(k)) for k in range(1, nz)
        ] if share else []

        def part_sum(j):
            for copy in to[j]:
                copy.wait_recv()
            for landing in recvs[j]:
                add_rows(buf, spans[j][0], landing, spans[j][1])
            if extra is not None:
                extra(spans[j])
            start_all(*(to_z if j + 1 == len(to) else to[j + 1]))

        def sum_z():
            for copy in to_z:
                copy.wait_recv()
            total = buf[own, :].astype(F32)
            for k in range(1, nz):
                total = total + recv_z[k - 1, :cut].astype(F32)
            res[own, :] = total.astype(BF16)
            start_all(*back_z)

        handed = [back_z] + back[::-1]
        follow = back[::-1] + [[out]]
        first = [functools.partial(start_all, *to[0])] if starts else []
        chain(
            name, *first, *[functools.partial(part_sum, j) for j in range(len(to))], sum_z,
            *[then(a, *b) for a, b in zip(handed, follow)],
        )
        for group in to + [to_z, back_z] + back:
            last_sends.extend(group)
        outs.append(out)
        return to[0]

    f_base = sems(5)
    f_c0 = remote(r.ct.at[0], r.fc.at[0], f_base, dev_core)
    f_c1 = remote(r.ct.at[2], r.fc.at[1], f_base + 1, dev_core)
    f_part = rows_at(xbit * (D // 2), D // 2)
    f_other = rows_at((1 - xbit) * (D // 2), D // 2)
    f_y = remote(r.ct.at[1, 0], r.fy.at[0], f_base + 2, dev_y)
    f_x = remote(r.ct.at[1, 1, f_other], r.fy.at[1, D // 2 :], f_base + 3, dev_x)
    f_xy = remote(r.ct.at[1, 1, f_part], r.fy.at[1, : D // 2], f_base + 4, dev_y)
    f_outs = [pltpu.make_async_copy(r.fo.at[g], r.fo_out.at[g], r.ls.at[3 + g]) for g in range(2)]
    last_sends, outs = [f_y, f_x, f_xy], []

    def across_up():
        f_y.wait_recv()
        add_rows(r.ct.at[3, 0], 0, r.fy.at[0], D)
        start_all(*f0)

    def plane_down():
        f_x.wait_recv()
        add_rows(r.ct.at[1, 1], xbit * (D // 2), r.fy.at[1, D // 2 :], D // 2)
        f_xy.start()

    def across_down(span):
        f_xy.wait_recv()
        add_rows(r.ct.at[3, 1], span[0], r.fy.at[1, : D // 2], span[1])

    f0 = sum_chain(
        "F0", r.ct.at[3, 0], r.fo.at[0], ["x"], [[r.fx.at[0]]], r.fz.at[0], f_outs[0], False
    )
    f1 = sum_chain(
        "F1", r.ct.at[3, 1], r.fo.at[1], ["x"], [[r.fx.at[1]]], r.fz.at[1], f_outs[1], False, across_down
    )
    steps["F0"].insert(0, across_up)
    chain("X", plane_down)

    def ffn(k, s, out):
        def tile(t):
            rows = rows_at(t * T, T)
            for h in range(2):
                lanes = slice(h * (D // 2), (h + 1) * (D // 2))
                up = dot(r.hf[rows, :], r.wu[s, :, lanes])
                grad_act = dot_t(r.go[rows, :], r.wd[s, lanes, :])
                cubic = (GELU_SCALE * GELU_CUBIC) * (up * up)
                tang = jnp.tanh(up * (GELU_SCALE + cubic))
                half_up, half_t = 0.5 * up, 0.5 + 0.5 * tang
                slope = half_t + half_up * (1.0 - tang * tang) * (GELU_SCALE + 3.0 * cubic)
                r.gp[rows, lanes] = (up * half_t).astype(BF16)
                r.gp[rows, slice(D + lanes.start, D + lanes.stop)] = (grad_act * slope).astype(BF16)
            add_acc(t, dot(r.gp[rows, :D], r.wd[s]))
            add_acc(nt + t, dot_t(r.gp[rows, D : 2 * D], r.wu[s]))

        loop("ffn_tile%d" % k, nt, tile)

        def grads(t):
            rows = rows_at(t * T, T)
            out[0, rows, :] = dot(r.hft[rows, :], r.gp[:, D : 2 * D]).astype(BF16)
            out[1, rows, :] = dot(r.got_t[rows, :], r.gp[:, :D]).astype(BF16)

        loop("ffn_grads%d" % k, D // T, grads)

    ffn(0, tp_far, r.ct.at[0])
    f_c0.start()
    ffn(1, tp_y, r.ct.at[1])
    f_c0.wait_recv()
    add_rows(r.ct.at[1, 1], 0, r.fc.at[0, 1], D)
    f_x.start()
    add_rows(r.ct.at[1, 0], 0, r.fc.at[0, 0], D)
    f_y.start()
    ffn(2, tp_core, r.ct.at[2])
    f_c1.start()
    ffn(3, tp, r.ct.at[3])
    f_c1.wait_recv()
    add_rows(r.ct.at[3, 1], 0, r.fc.at[1, 1], D)
    start_all(*f1)
    add_rows(r.ct.at[3, 0], 0, r.fc.at[1, 0], D)

    ones_row = lax.broadcasted_iota(jnp.int32, (2 * LANES, LANES), 0)
    ones_col = lax.broadcasted_iota(jnp.int32, (2 * LANES, LANES), 1)
    head_ones = (lax.div(lax.rem(ones_row, LANES), 64) == lax.div(ones_col, 64)).astype(F32).astype(BF16)
    r.gg[...] = jnp.zeros((2, 8, D), F32)

    def gn_at(c):
        return rows_at(lax.rem(c, 2) * T, T), pl.ds(pl.multiple_of(lax.div(c, 2) * T, T), T)

    def gn_of(p, c):
        at, wide_at = gn_at(c)
        return r.wd[p, at, wide_at]

    def fold(v):
        return jnp.sum(v.reshape(T // 8, 8, D), axis=0)

    for copy in w_sends:
        copy.wait_send()

    def back_middle(t):
        rows = rows_at(t * T, T)
        r.hf[rows, :] = acc(t).astype(BF16)
        res = r.res[rows, :]
        mean = jnp.mean(res, axis=-1, keepdims=True)
        cen = res - mean
        inv = lax.rsqrt(jnp.mean(cen * cen, axis=-1, keepdims=True) + NORM_EPS)
        n = cen * inv
        gh = acc(nt + t)
        r.gg[0] += fold(gh * n)
        sc = gh * r.gf[...]
        centre = jnp.mean(sc, axis=-1, keepdims=True)
        inner = jnp.mean(sc * n, axis=-1, keepdims=True)
        gres = r.go[rows, :].astype(F32) + inv * (sc - centre - n * inner)
        r.res[rows, :] = gres
        gattn = gres.astype(BF16)
        r.gp[rows, 2 * D :] = gattn
        gmi = dot_t(gattn, r.wo[...]) * r.inv[rows, :]
        w = gmi * r.mix[rows, :].astype(F32) * (-1.0)
        hi = w.astype(BF16)
        lo = (w - hi.astype(F32)).astype(BF16)
        gnum = gmi.astype(BF16)
        for p in range(npair):
            lanes = slice(p * LANES, (p + 1) * LANES)
            gden = dot(cat([hi[:, lanes], lo[:, lanes]], 1), head_ones).astype(BF16)
            at, wide_at = gn_at(t)
            r.wd[p, at, wide_at] = cat([gnum[:, lanes], gden * jnp.asarray(1.0 / 64.0, BF16)], 1)

    loop("back_middle", nt, back_middle)
    out_copy = pltpu.make_async_copy(r.hf, r.out, r.ls.at[13])
    out_copy.start()

    bpack, steps["B"], bcollect = state_exchange(1, r.own, r.bgot)

    def state_back(i):
        p, c = lax.div(i, nt), nt - 1 - lax.rem(i, nt)
        rows = rows_at(c * T, T)

        @pl.when(c == nt - 1)
        def _():
            r.sl[p * (nt + 1) + nt] = jnp.zeros((M, M), F32)

        gain = merge(dot_c(gn_of(p, c) * twice(r.use[rows, :]), r.phiq[p, rows, :]))
        state = r.sc[c] * r.sl[p * (nt + 1) + c + 1] + gain
        r.sl[p * (nt + 1) + c] = state

    bleaves = (lambda i: lax.rem(i, nt) == nt - 1), (lambda i: bpack(lax.div(i, nt), 0))

    loop("state_back", npair * nt, state_back, [bleaves])

    half = D // 2
    parts = [("O", 0, 0, D), ("Q", 1, 0, D - LANES), ("Q3", 1, D - LANES, LANES)]
    parts = parts + [("K%d" % p, 2 + p // 2, (p % 2) * half, half) for p in range(npair)]
    for i, (name, g, lane, n) in enumerate(parts):
        lanes = slice(lane, lane + n)
        core_land = r.fc.at[0, g, :half, lanes] if g < 2 else r.fc.at[0, g - 2, half:, lanes]
        stages = STAGES["K" if name == "Q3" else name[0]]
        recvs, at = [[core_land]], 0
        rows = D // 2
        for axes in stages[1:]:
            rows = rows // 2 ** len(axes)
            recvs.append([r.land.at[g, pl.ds(at + k * rows, rows), lanes] for k in range(2 ** len(axes) - 1)])
            at = at + rows * (2 ** len(axes) - 1)
        rz = r.land_z.at[g, :, :, lanes]
        source = r.ct.at[0 if g < 2 else 2, g % 2, :, lanes]
        sum_chain(
            name, source, r.wu.at[g, :, lanes], stages, recvs, rz,
            pltpu.make_async_copy(r.wu.at[g, :, lanes], r.grads.at[g, :, lanes], r.ls.at[5 + i]),
        )

    f_c0.wait_send()
    f_c1.wait_send()
    def out_grads():
        for t in range(D // T):
            rows = slice(t * T, (t + 1) * T)
            r.ct[0, 0, rows, :] = dot_c(r.mix[:, rows], r.gp[:, 2 * D :]).astype(BF16)

    once("out_grads", out_grads)

    def back_query(i):
        p, c = lax.div(i, nt), lax.rem(i, nt)
        rows = rows_at(c * T, T)
        vals, gn = r.vp[p, rows, :], gn_of(p, c)
        phi_q, phi_k = r.phiq[p, rows, :], r.phik[p, rows, :]
        g = dot_t(gn, cat([vals * low, vals * high], 0)).astype(BF16) * twice(r.mask[c])
        used = gn * twice(r.use[rows, :])
        gphi = cat([dot(g[:, :M], phi_k[:, :M]), dot(g[:, M:], phi_k[:, M:])], 1)
        gphi = gphi + dot(used, r.st[i])
        t = (gphi * phi_q.astype(F32)).astype(BF16)
        o = dot_t(t, r.bb[p, : 2 * LANES])
        gq = c4 * o[:, :LANES] - r.q[p, rows, :].astype(F32) * (o[:, LANES:] * 0.125)
        r.gp[rows, pl.ds(pl.multiple_of(p * LANES, LANES), LANES)] = gq.astype(BF16)

    loop("back_query", (npair - 1) * nt, back_query)
    def query_grads(lanes):
        for t in range(D // T):
            rows = slice(t * T, (t + 1) * T)
            r.ct[0, 1, rows, lanes] = dot(r.ht[rows, :], r.gp[:, lanes]).astype(BF16)

    once("query_grads", lambda: query_grads(slice(0, D - LANES)))

    def pair_grads(i):
        p = lax.div(i, nt)
        kv = cat(
            [r.gp[:, pl.ds(pl.multiple_of(o * D + p * LANES, LANES), LANES)] for o in (1, 2)], 1
        )
        wide_at = pl.ds(pl.multiple_of(lax.rem(p, 2) * half, half), half)
        for t in range(D // T):
            rows = slice(t * T, (t + 1) * T)
            r.ct[2, lax.div(p, 2), rows, wide_at] = dot(r.ht[rows, :], kv).astype(BF16)

    def back_key(i):
        p, c = lax.div(i, nt), lax.rem(i, nt)
        rows = rows_at(c * T, T)
        dstate = split((r.sl[p * (nt + 1) + c + 1] + r.sc[2 * nt + c] * r.tin[p]).astype(BF16))
        vals, gn = r.vp[p, rows, :], gn_of(p, c)
        phi_q, phi_k = r.phiq[p, rows, :], r.phik[p, rows, :]
        mask = twice(r.maskt[c])
        gt = cat([dot_t(vals * low, gn), dot_t(vals * high, gn)], 1).astype(BF16) * mask
        st = cat([dot_t(phi_k[:, :M], phi_q[:, :M]), dot_t(phi_k[:, M:], phi_q[:, M:])], 1)
        st = st.astype(BF16) * mask
        tail = r.tail[rows, :]
        left = vals * twice(tail)
        gphi = cat(
            [
                dot(cat([gt[:, m], left], 1), cat([phi_q[:, m], dstate[:, m]], 0))
                for m in (slice(0, M), slice(M, 2 * M))
            ],
            1,
        )
        gnum = gn[:, :LANES]
        gv = dot(st, cat([gnum * low[:, :LANES], gnum * high[:, :LANES]], 0))
        gv = gv + tail.astype(F32) * dot_t(phi_k, dstate[:LANES])
        t = (gphi * phi_k.astype(F32)).astype(BF16)
        o = dot_t(t, r.bb[p, : 2 * LANES])
        gk = c4 * o[:, :LANES] - r.k[p, rows, :].astype(F32) * (o[:, LANES:] * 0.125)
        r.gp[rows, pl.ds(pl.multiple_of(D + p * LANES, LANES), LANES)] = gk.astype(BF16)
        r.gp[rows, pl.ds(pl.multiple_of(2 * D + p * LANES, LANES), LANES)] = gv.astype(BF16)

    loop("back_key", npair * nt, back_key, [((lambda i: lax.rem(i, nt) == nt - 1), pair_grads)], bcollect)

    loop("last_query", nt, lambda c: back_query((npair - 1) * nt + c))
    once("last_grads", lambda: query_grads(slice(D - LANES, D)))

    def back_first(t):
        rows = rows_at(t * T, T)
        gh = dot_t(r.gp[rows, :D], r.wq[...])
        gh = gh + dot_t(r.gp[rows, D : 2 * D], r.wk[...])
        gh = gh + dot_t(r.gp[rows, 2 * D :], r.wv[...])
        x = r.tok[rows, :].astype(F32)
        mean = jnp.mean(x, axis=-1, keepdims=True)
        cen = x - mean
        inv = lax.rsqrt(jnp.mean(cen * cen, axis=-1, keepdims=True) + NORM_EPS)
        n = cen * inv
        r.gg[1] += fold(gh * n)
        sc = gh * r.ga[...]
        centre = jnp.mean(sc, axis=-1, keepdims=True)
        inner = jnp.mean(sc * n, axis=-1, keepdims=True)
        r.res[rows, :] += inv * (sc - centre - n * inner)

    loop("back_first", nt, back_first)
    gt_copy = pltpu.make_async_copy(r.res, r.gt, r.ls.at[3 + 9])
    gt_copy.start()

    g_base = sems(3 + ndp - 1)
    sums = [jnp.sum(r.gg[k], axis=0, keepdims=True) for k in range(2)]
    r.g1[...] = cat([v[:, j : j + LANES] for v in sums for j in range(0, D, LANES)], 0)
    g_tp = [remote(r.g1, r.gr.at[k - 1], g_base + k - 1, (dp, lax.rem(tp + k, 4))) for k in (1, 2, 3)]
    g_dp = [
        remote(r.g2, r.gr.at[2 + k], g_base + 2 + k, (lax.rem(dp + k, ndp), tp)) for k in range(1, ndp)
    ]
    start_all(*g_tp)

    def gains_tp():
        for copy in g_tp:
            copy.wait_recv()
        r.g2[...] = r.g1[...] + r.gr[0] + r.gr[1] + r.gr[2]
        start_all(*g_dp)

    def gains_dp():
        total = r.g2[...]
        for k in range(1, ndp):
            g_dp[k - 1].wait_recv()
            total = total + r.gr[2 + k]
        r.gout[...] = total

    chain("G", gains_tp, gains_dp)
    advance("tail", 0)
    assert not plan and not any(steps.values()), (plan, {k: len(v) for k, v in steps.items() if v})

    for copy in seg_copies + last_sends + g_tp + g_dp:
        copy.wait_send()
    for copy in outs + [out_copy, gt_copy]:
        copy.wait()
    assert used[0] <= r.ss.shape[0]


def layer(tokens, segment_ids, grad_out, w_query, w_key, w_value, w_out, w_up, w_down, gain_attn,
          gain_ffn, feature_basis):
    _, L, D = tokens.shape
    H, DH, M = feature_basis.shape
    F = w_up.shape[1]
    npair, nt = H // 2, L // T
    ndp = lax.axis_size("dp")
    nz = ndp // 2
    assert lax.axis_size("tp") == 4 and F == D and DH == 64 and M == T

    vmem, hbm = pl.BlockSpec(memory_space=pltpu.VMEM), pl.BlockSpec(memory_space=pl.ANY)
    ins = {
        "seg": (segment_ids, vmem),
        "tok_in": (tokens[0], hbm),
        "go_in": (grad_out[0], hbm),
        "wq_in": (w_query, hbm),
        "wk_in": (w_key, hbm),
        "wv_in": (w_value, hbm),
        "wo_in": (w_out, hbm),
        "wup": (w_up, hbm),
        "wdn": (w_down, hbm),
        "ga": (gain_attn[None], vmem),
        "gf": (gain_ffn[None], vmem),
        "basis_in": (feature_basis, hbm),
    }
    outs = {
        "out": ((L, D), BF16, hbm),
        "gt": ((L, D), F32, hbm),
        "fo_out": ((2, D, F), BF16, hbm),
        "grads": ((4, D, D), BF16, hbm),
        "gout": ((8, LANES), F32, vmem),
    }

    scratch = {
        "tok": ((L, D), BF16),
        "wk": ((D, D), BF16),
        "wv": ((D, D), BF16),
        "wq": ((D, D), BF16),
        "wo": ((D, D), BF16),
        "go": ((L, D), BF16),
        "sg": ((4, 1, L), jnp.int32),
        "wu": ((4, D, F), BF16),
        "wd": ((4, F, D), BF16),
        "bb": ((npair, 3 * LANES, 2 * M), BF16),
        "ht": ((D, L), BF16),
        "q": ((npair, L, LANES), BF16),
        "k": ((npair, L, LANES), BF16),
        "vp": ((npair, L, 2 * LANES), BF16),
        "sc": ((3 * nt + 8, 1, M), F32),
        "use": ((L, LANES), BF16),
        "tail": ((L, LANES), BF16),
        "mask": ((nt, T, M), BF16),
        "maskt": ((nt, T, M), BF16),
        "phik": ((npair, L, 2 * M), BF16),
        "phiq": ((npair, L, 2 * M), BF16),
        "sl": ((npair * (nt + 1), M, M), F32),
        "own": ((npair, 144, M), BF16),
        "got": ((4, npair, 144, M), BF16),
        "bgot": ((4, npair, 144, M), BF16),
        "tin": ((npair, M, M), F32),
        "st": ((npair * nt, M, 2 * M), BF16),
        "inv": ((L, D), F32),
        "mix": ((L, D), BF16),
        "res": ((L, D), F32),
        "hf": ((L, D), BF16),
        "hft": ((D, L), BF16),
        "got_t": ((D, L), BF16),
        "ct": ((4, 2, D, F), BF16),
        "fc": ((2, 2, D, F), BF16),
        "land": ((4, 192, D), BF16),
        "land_z": ((4, nz - 1, D // 8, D), BF16),
        "fy": ((2, D, F), BF16),
        "fx": ((2, D // 2, F), BF16),
        "fz": ((2, nz - 1, D // 2 // nz, F), BF16),
        "fo": ((2, D, F), BF16),
        "gg": ((2, 8, D), F32),
        "gp": ((L, 3 * D), BF16),
        "g1": ((8, LANES), F32),
        "g2": ((8, LANES), F32),
        "gr": ((3 + ndp - 1, 8, LANES), F32),
    }
    n_sems = 40 + 6 * npair + ndp + (4 + npair) * (10 + 2 * (nz - 1)) + 5 * (nz - 1)
    names = list(ins) + list(outs) + list(scratch) + ["ls", "ss", "rs"]
    res = pl.pallas_call(
        functools.partial(layer_kernel, nz, names),
        out_shape=[jax.ShapeDtypeStruct(s, d) for s, d, _ in outs.values()],
        in_specs=[spec for _, spec in ins.values()],
        out_specs=[spec for _, _, spec in outs.values()],
        scratch_shapes=[pltpu.VMEM(s, d) for s, d in scratch.values()]
        + [
            pltpu.SemaphoreType.DMA((28,)),
            pltpu.SemaphoreType.DMA((n_sems,)),
            pltpu.SemaphoreType.DMA((n_sems,)),
        ],
        name="layer",
        compiler_params=pltpu.CompilerParams(
            collective_id=0, has_side_effects=True, vmem_limit_bytes=67043328
        ),
    )(*[a for a, _ in ins.values()])
    return hand_out(*res)


def hand_out_kernel(out, gt, up, down, grads, gains, *refs):
    o_out, o_gt, o_query, o_key, o_value, o_proj, o_up, o_down, o_attn, o_ffn = refs
    o_out[0] = out[...]
    o_gt[0] = gt[...]
    o_up[...] = up[0].astype(F32)
    o_down[...] = down[0].astype(F32).T
    o_proj[...] = grads[0].astype(F32)
    o_query[...] = grads[1].astype(F32)
    for p in range(grads.shape[2] // LANES):
        lanes = slice(p * LANES, (p + 1) * LANES)
        at = (p % 2) * 2 * LANES
        o_key[:, lanes] = grads[2 + p // 2, :, at : at + LANES].astype(F32)
        o_value[:, lanes] = grads[2 + p // 2, :, at + LANES : at + 2 * LANES].astype(F32)
    for j in range(4):
        lanes = slice(j * LANES, (j + 1) * LANES)
        o_ffn[:, lanes] = gains[j : j + 1, :]
        o_attn[:, lanes] = gains[4 + j : 5 + j, :]


def hand_out(out, gt, fo, grads, gains):
    (L, D), steps = out.shape, 4
    lr, dr = L // steps, D // steps
    tall = pl.BlockSpec((1, lr, D), lambda i: (0, i, 0))
    flat = pl.BlockSpec((dr, D), lambda i: (i, 0))
    row = pl.BlockSpec((1, D), lambda i: (0, 0))
    f32 = lambda *shape: jax.ShapeDtypeStruct(shape, F32)
    res = pl.pallas_call(
        hand_out_kernel,
        grid=(steps,),
        in_specs=[
            pl.BlockSpec((lr, D), lambda i: (i, 0)),
            pl.BlockSpec((lr, D), lambda i: (i, 0)),
            pl.BlockSpec((1, dr, D), lambda i: (0, i, 0)),
            pl.BlockSpec((1, D, dr), lambda i: (1, 0, i)),
            pl.BlockSpec((4, dr, D), lambda i: (0, i, 0)),
            pl.BlockSpec((8, LANES), lambda i: (0, 0)),
        ],
        out_specs=[tall, tall, flat, flat, flat, flat, flat, flat, row, row],
        out_shape=[jax.ShapeDtypeStruct((1, L, D), BF16), f32(1, L, D)]
        + [f32(D, D)] * 6 + [f32(1, D)] * 2,
        name="hand_out",
    )(out, gt, fo, fo, grads, gains)
    return (*res[:8], res[8][0], res[9][0])


def solution(mesh):
    whole = P()
    in_specs = (
        P("dp", "tp", None), P("dp", "tp"), P("dp", "tp", None), whole, whole, whole, whole,
        P(None, "tp"), P("tp", None), whole, whole, whole,
    )
    out_specs = (
        P("dp", "tp", None), P("dp", "tp", None), whole, whole, whole, whole,
        P(None, "tp"), P("tp", None), whole, whole,
    )
    return jax.shard_map(layer, mesh=mesh, in_specs=in_specs, out_specs=out_specs, check_vma=False)
```

```python
import functools
import math
from types import SimpleNamespace

import jax
import jax.numpy as jnp
from jax import lax
from jax.experimental import pallas as pl
from jax.experimental.pallas import tpu as pltpu
from jax.sharding import PartitionSpec as P

MESH = pl.DeviceIdType.MESH
F32 = jnp.float32
BF16 = jnp.bfloat16
NORM_EPS = 1e-05
GELU_SCALE = 0.7978845608028654
GELU_CUBIC = 0.044715
LANES = 128
(
    PROJECT, BASIS_BLOCKS, KEY_SIDE, PROJECT_QUERY, QUERY_SIDE, ALL_MASKS,
    ATTEND, MIDDLE, TRANSPOSES, BACK_MIDDLE, STATE_BACK, OUT_GRADS,
    BACK_QUERY, QUERY_GRADS, BACK_KEY, LAST_QUERY, LAST_GRADS, BACK_FIRST,
    TAIL,
) = range(19)
FFN_TILE, FFN_GRADS = 19, 23
(
    ENTER, W_UP, W_DOWN, STATES, STATE_GRADS, FFN_ACROSS,
    FFN_UP, FFN_DOWN, SUM_O, SUM_Q, SUM_Q3, GAINS,
    SUM_K,
) = range(13)
PLAN = (
    (PROJECT, 1, ENTER),
    (KEY_SIDE, 3, W_DOWN),
    (PROJECT_QUERY, 0, W_UP),
    (QUERY_SIDE, 3, STATES),
    (QUERY_SIDE, 11, STATES),
    (QUERY_SIDE, 15, W_DOWN),
    (ATTEND, 3, STATES),
    (ATTEND, 7, STATES),
    (MIDDLE, 3, W_UP),
    (MIDDLE, 3, W_DOWN),
    (FFN_TILE + 3, 3, FFN_ACROSS),
    (BACK_MIDDLE, 3, FFN_UP),
    (OUT_GRADS, 0, SUM_O),
    (OUT_GRADS, 0, FFN_DOWN),
    (BACK_QUERY, 3, STATE_GRADS),
    (BACK_QUERY, 3, SUM_O),
    (BACK_QUERY, 7, STATE_GRADS),
    (BACK_QUERY, 11, STATE_GRADS),
    (BACK_QUERY, 11, FFN_UP),
    (BACK_QUERY, 11, STATE_GRADS),
    (QUERY_GRADS, 0, SUM_Q),
    (BACK_KEY, 3, SUM_O),
    (BACK_KEY, 3, FFN_DOWN),
    (BACK_KEY, 3, SUM_K),
    (BACK_KEY, 3, SUM_Q),
    (BACK_KEY, 5, SUM_K),
    (BACK_KEY, 7, SUM_O),
    (BACK_KEY, 7, SUM_K + 1),
    (BACK_KEY, 9, SUM_K + 1),
    (BACK_KEY, 9, FFN_UP),
    (BACK_KEY, 11, SUM_K + 2),
    (BACK_KEY, 11, SUM_Q),
    (BACK_KEY, 13, SUM_K + 2),
    (BACK_KEY, 13, SUM_K),
    (BACK_KEY, 15, FFN_DOWN),
    (BACK_KEY, 15, SUM_K + 1),
    (BACK_KEY, 15, SUM_K + 3),
    (BACK_KEY, 15, SUM_Q),
    (LAST_QUERY, 3, SUM_O),
    (LAST_QUERY, 3, SUM_K + 3),
    (LAST_QUERY, 3, SUM_K + 2),
    (LAST_GRADS, 0, SUM_Q3),
    (BACK_FIRST, 1, SUM_Q3),
    (TAIL, 0, FFN_UP),
    (TAIL, 0, SUM_K),
    (TAIL, 0, FFN_DOWN),
    (TAIL, 0, SUM_K + 1),
    (TAIL, 0, GAINS),
    (TAIL, 0, SUM_Q),
    (TAIL, 0, SUM_K + 3),
    (TAIL, 0, SUM_O),
    (TAIL, 0, SUM_Q3),
    (TAIL, 0, SUM_K + 2),
    (TAIL, 0, SUM_K),
    (TAIL, 0, SUM_K + 1),
    (TAIL, 0, GAINS),
    (TAIL, 0, FFN_UP),
    (TAIL, 0, SUM_Q),
    (TAIL, 0, SUM_K + 3),
    (TAIL, 0, SUM_O),
    (TAIL, 0, SUM_Q3),
    (TAIL, 0, SUM_K + 2),
    (TAIL, 0, SUM_Q),
    (TAIL, 0, SUM_K),
    (TAIL, 0, SUM_K),
    (TAIL, 0, SUM_K + 1),
    (TAIL, 0, SUM_K + 3),
    (TAIL, 0, SUM_Q3),
    (TAIL, 0, SUM_O),
    (TAIL, 0, SUM_K + 1),
    (TAIL, 0, SUM_Q),
    (TAIL, 0, SUM_O),
    (TAIL, 0, SUM_K + 2),
    (TAIL, 0, SUM_Q),
    (TAIL, 0, SUM_K + 2),
    (TAIL, 0, SUM_K + 3),
    (TAIL, 0, SUM_Q3),
    (TAIL, 0, SUM_K + 3),
    (TAIL, 0, SUM_Q3),
)
UNROLL = {
    PROJECT: 2,
    MIDDLE: 2,
    BACK_MIDDLE: 2,
    BACK_FIRST: 2,
    BACK_KEY: 2,
    FFN_TILE: 2,
    KEY_SIDE: 4,
    QUERY_SIDE: 4,
    ATTEND: 4,
    STATE_BACK: 4,
    BACK_QUERY: 4,
    LAST_QUERY: 4,
}
STAGES = (("c", "y", "x"), ("c", "x", "y"), ("c", "xy"))
T = 256


def dot(a, b):
    return jnp.dot(a, b, preferred_element_type=F32)


def dot_t(a, b):
    return lax.dot_general(a, b, (((1,), (1,)), ((), ())), preferred_element_type=F32)


def dot_c(a, b):
    return lax.dot_general(a, b, (((0,), (0,)), ((), ())), preferred_element_type=F32)


def rows_at(start, size):
    return pl.ds(pl.multiple_of(start, 16), size)


def cat(parts, axis):
    return jnp.concatenate(parts, axis=axis)


def lane_groups():
    lane = lax.broadcasted_iota(jnp.int32, (1, 2 * LANES), 1)
    first = lax.rem(lane, LANES) < 64
    one = jnp.where(first, 1.0, 0.0)
    return one.astype(BF16), (1.0 - one).astype(BF16)


def layer_kernel(nz, names, *refs):
    r = SimpleNamespace(**dict(zip(names, refs)))
    L, D = r.tok.shape
    nt = L // T
    npair = r.basis_in.shape[0] // 2
    M = r.basis_in.shape[2]
    c4 = 64.0**-0.25
    exp_scale = c4 * math.log2(math.e)

    dp, tp = lax.axis_index("dp"), lax.axis_index("tp")
    ndp = 2 * nz
    core, ybit = lax.rem(tp, 2), lax.div(tp, 2)
    xbit, zi = lax.rem(dp, 2), lax.div(dp, 2)
    tp_core, tp_y, tp_far = tp + 1 - 2 * core, lax.rem(tp + 2, 4), 3 - tp
    dev_core, dev_y, dev_far = (dp, tp_core), (dp, tp_y), (dp, tp_far)
    dev_x = (dp + 1 - 2 * xbit, tp)

    def z_at(k):
        return lax.rem(zi + k, nz)

    def dev_z(k):
        return (z_at(k) * 2 + xbit, tp)

    plan, steps = {}, {}
    for place, i, chunk in PLAN:
        plan.setdefault((place, i), []).append(chunk)

    def advance(place, i):
        for chunk in plan.pop((place, i), ()):
            steps[chunk].pop(0)()

    def loop(name, n, body, tasks=(), before=None):
        u = UNROLL.get(FFN_TILE if FFN_TILE <= name < FFN_GRADS else name, 1)

        def step(i, _):
            if before is not None:
                pl.when(lax.rem(i * u, nt) == 0)(lambda: before(lax.div(i * u, nt)))
            for k in range(u):
                body(i * u + k)
            for when, task in tasks:
                pl.when(when(i * u + u - 1))(functools.partial(task, i * u + u - 1))
            for k in range(n):
                if (name, k) in plan:
                    pl.when(i == k // u)(functools.partial(advance, name, k))
            return 0

        lax.fori_loop(0, n // u, step, 0)

    def once(name, body):
        body()
        advance(name, 0)

    used = [0]

    def sems(n):
        first = used[0]
        used[0] += n
        return first

    def remote(src, dst, idx, dev):
        return pltpu.make_async_remote_copy(
            src_ref=src, dst_ref=dst, send_sem=r.ss.at[idx], recv_sem=r.rs.at[idx],
            device_id=dev, device_id_type=MESH,
        )

    loads = {
        name: pltpu.make_async_copy(getattr(r, name + "_in"), getattr(r, name), r.ls.at[14 + k])
        for k, name in enumerate(("tok", "wk", "wv", "wq", "wo", "go"))
    }
    own_up = pltpu.make_async_copy(r.wup, r.wu.at[tp], r.ls.at[0])
    own_down = pltpu.make_async_copy(r.wdn, r.wd.at[tp], r.ls.at[1])
    own_seg = pltpu.make_async_copy(r.seg, r.sg.at[tp], r.ls.at[2])
    basis_copies = [
        pltpu.make_async_copy(
            r.basis_in.at[h], r.bb.at[h // 2, pl.ds((h % 2) * 64, 64), pl.ds((h % 2) * M, M)], r.ls.at[20 + h]
        )
        for h in range(2 * npair)
    ]
    own_seg.start()
    for copy in list(loads.values()) + basis_copies:
        copy.start()
    own_up.start()
    own_down.start()

    barrier = pltpu.get_barrier_semaphore()
    for k in (1, 2, 3):
        pl.semaphore_signal(barrier, inc=1, device_id=(dp, lax.rem(tp + k, 4)), device_id_type=MESH)
    for k in range(1, ndp):
        pl.semaphore_signal(barrier, inc=1, device_id=(lax.rem(dp + k, ndp), tp), device_id_type=MESH)


    seg_base = sems(3)
    seg_copies = [
        remote(r.seg, r.sg.at[tp], seg_base + k - 1, (dp, lax.rem(tp + k, 4))) for k in (1, 2, 3)
    ]

    up_base, down_base = sems(5), sems(4 + nz - 1)
    pr = r.wdn.shape[0] // ndp
    up_core = remote(r.wup, r.wu.at[tp], up_base, dev_core)
    hd = r.wup.shape[0] // 2
    up_y = [
        remote(r.wup.at[pl.ds(g * hd, hd)], r.wu.at[tp, pl.ds(g * hd, hd)], up_base + 1 + g, dev_y)
        for g in range(2)
    ]
    up_on = [
        remote(r.wu.at[tp_y, pl.ds(g * hd, hd)], r.wu.at[tp_y, pl.ds(g * hd, hd)], up_base + 3 + g, dev_core)
        for g in range(2)
    ]
    down_core = remote(r.wdn, r.wd.at[tp], down_base, dev_core)
    down_piece = rows_at((xbit * nz + zi) * pr, pr)
    down_plane = rows_at(xbit * nz * pr, nz * pr)
    down_y = remote(r.wdn.at[down_piece], r.wd.at[tp, down_piece], down_base + 1, dev_y)
    down_z = [
        remote(r.wd.at[tp_y, down_piece], r.wd.at[tp_y, down_piece], down_base + 3 + k, dev_z(k))
        for k in range(1, nz)
    ]
    down_x = remote(r.wd.at[tp_y, down_plane], r.wd.at[tp_y, down_plane], down_base + 2, dev_x)
    down_on = remote(r.wd.at[tp_y], r.wd.at[tp_y], down_base + 3, dev_core)
    w_sends = [up_core, down_core, down_y, down_x, down_on] + up_y + up_on + down_z

    def start_all(*copies):
        for copy in copies:
            copy.start()

    def chain(name, *tasks):
        steps[name] = list(tasks)

    def then(waits, *starts):
        def task():
            for copy in waits:
                copy.wait_recv()
            start_all(*starts)

        return task

    chain(W_UP, then(up_y[:1], up_on[0]), then(up_y[1:], up_on[1]))
    chain(W_DOWN, then([down_y], *down_z), then(down_z, down_x), then([down_x], down_on))

    def enter():
        pl.semaphore_wait(barrier, 3 + ndp - 1)
        start_all(*seg_copies, down_y, up_y[0], up_core, down_core)

    steps[ENTER] = [enter]

    def basis_blocks():
        zero, one = jnp.zeros((64, M), BF16), jnp.ones((64, M), BF16)
        for p in range(npair):
            for h in range(2):
                lanes = slice(h * M, (h + 1) * M)
                r.bb[p, (1 - h) * 64 : (2 - h) * 64, lanes] = zero
                r.bb[p, LANES:, lanes] = cat([one, zero, one, zero] if h == 0 else [zero, one, zero, one], 0)
        for copy in basis_copies:
            copy.wait()

    once(BASIS_BLOCKS, basis_blocks)
    low, high = lane_groups()

    def project(t):
        rows = rows_at(t * T, T)
        x = r.tok[rows, :].astype(F32)
        mean = jnp.mean(x, axis=-1, keepdims=True)
        cen = x - mean
        inv = lax.rsqrt(jnp.mean(cen * cen, axis=-1, keepdims=True) + NORM_EPS)
        hid = ((cen * inv) * r.ga[...]).astype(BF16)
        r.hf[rows, :] = hid
        k = dot(hid, r.wk[...]).astype(BF16)
        v = dot(hid, r.wv[...]).astype(BF16)
        for p in range(npair):
            lanes = slice(p * LANES, (p + 1) * LANES)
            r.k[p, rows, :] = k[:, lanes]
            r.vp[p, rows, :LANES] = v[:, lanes]
            r.vp[p, rows, LANES:] = jnp.ones((T, LANES), BF16)

    loads["tok"].wait()
    loads["wk"].wait()
    loads["wv"].wait()
    loop(PROJECT, nt, project)

    own_seg.wait()
    for copy in seg_copies:
        copy.wait_recv()
    row_max, row_min = [], []
    for j in range(4):
        ids = r.sg[j].astype(F32)
        row_max.append(jnp.max(ids, axis=1, keepdims=True))
        row_min.append(jnp.min(ids, axis=1, keepdims=True))
    in_seg = jnp.full((1, 1), -1.0, F32)
    for j in range(4):
        in_seg = jnp.maximum(in_seg, jnp.where(j < tp, row_max[j], -1.0))
    mine = r.seg[...].astype(F32)
    ends = [jnp.max(mine[:, c * T : (c + 1) * T], axis=1, keepdims=True) for c in range(nt)]
    befores = [in_seg] + ends[:-1]
    keeps = [(befores[c] == ends[c]).astype(F32) for c in range(nt)]
    wide = lambda v: jnp.broadcast_to(v, (1, M))
    flag = jnp.ones((1, 1), F32)
    for c in range(nt):
        r.sc[c] = wide(keeps[c])
        r.sc[nt + c] = wide(flag)
        flag = flag * keeps[c]
    flag = jnp.ones((1, 1), F32)
    for c in reversed(range(nt)):
        r.sc[2 * nt + c] = wide(flag)
        flag = flag * keeps[c]
    for j in range(4):
        r.sc[3 * nt + j] = wide(jnp.where(j < tp, (row_max[j] == in_seg).astype(F32), 0.0))
        r.sc[3 * nt + 4 + j] = wide(jnp.where(j > tp, (row_min[j] == ends[-1]).astype(F32), 0.0))
    row_id = lax.broadcasted_iota(jnp.int32, (T, T), 0)
    col_id = lax.broadcasted_iota(jnp.int32, (T, T), 1)
    for c in range(nt):
        along = mine[:, c * T : (c + 1) * T]
        down = jnp.broadcast_to(along, (LANES, T)).T
        rows = slice(c * T, (c + 1) * T)
        use = (down == befores[c]).astype(F32).astype(BF16)
        tail = (down == ends[c]).astype(F32).astype(BF16)
        r.use[rows, :] = use
        r.tail[rows, :] = tail

    def masks(c):
        along = mine[:, c * T : (c + 1) * T]
        down = jnp.broadcast_to(along, (LANES, T)).T
        same = (cat([down, down], 1) == along).astype(F32)
        mask = (same * (row_id >= col_id).astype(F32)).astype(BF16)
        mask_t = (same * (row_id <= col_id).astype(F32)).astype(BF16)
        r.mask[c] = mask
        r.maskt[c] = mask_t

    def twice(v):
        return cat([v, v], 1)

    def features(u, p):
        wide_u = u.astype(F32)
        square = wide_u * wide_u * (-1.0 / (16.0 * c4))
        hi = square.astype(BF16)
        lo = (square - hi.astype(F32)).astype(BF16)
        expo = dot(cat([u, hi], 1), r.bb[p, : 2 * LANES]) + dot(lo, r.bb[p, 2 * LANES :])
        return jnp.exp2(expo * exp_scale).astype(BF16)

    def merge(u):
        return cat([u[:64, :M], u[64:128, M:], u[128:192, :M], u[192:, M:]], 0)

    def split(s):
        zero = jnp.zeros((64, M), s.dtype)
        first = cat([s[:64], zero, s[128:192], zero], 0)
        second = cat([zero, s[64:128], zero, s[192:]], 0)
        return cat([first, second], 1)

    def state_exchange(i, own, got):
        base = sems(3 * npair)

        def copies(p):
            at = base + p * 3
            return (
                remote(own.at[p], got.at[tp, p], at, dev_core),
                remote(own.at[p], got.at[tp, p], at + 1, dev_y),
                remote(got.at[tp_y, p], got.at[tp_y, p], at + 2, dev_core),
            )

        def pack(p, slot):
            state = r.sl[p * (nt + 1) + slot]
            own[p, :128, :] = state[:128].astype(BF16)
            own[p, 128:, :] = cat([state[128:136], state[192:200]], 0).astype(BF16)
            to_core, to_y, _ = copies(p)
            to_y.start()
            to_core.start()

        def relay(p):
            _, to_y, on = copies(p)
            to_y.wait_recv()
            on.start()

        def collect(p):
            to_core, to_y, on = copies(p)
            to_core.wait_recv()
            on.wait_recv()
            total = jnp.zeros((144, M), F32)
            for slot in (tp_core, tp_y, tp_far):
                total = total + got[slot, p].astype(F32) * r.sc[3 * nt + 4 * i + slot]
            r.tin[p, :128, :] = total[:128]
            r.tin[p, 128:192, :] = jnp.broadcast_to(total[128:129], (64, M))
            r.tin[p, 192:, :] = jnp.broadcast_to(total[136:137], (64, M))
            to_core.wait_send()
            to_y.wait_send()
            on.wait_send()

        return pack, [functools.partial(relay, p) for p in range(npair)], collect

    pack, steps[STATES], collect = state_exchange(0, r.own, r.got)

    def key_side(i):
        p, c = lax.div(i, nt), lax.rem(i, nt)
        rows = rows_at(c * T, T)
        phi = features(r.k[p, rows, :], p)
        r.phik[p, rows, :] = phi
        gain = merge(dot_c(r.vp[p, rows, :] * twice(r.tail[rows, :]), phi))

        @pl.when(c == 0)
        def _():
            r.sl[p * (nt + 1)] = jnp.zeros((M, M), F32)

        state = r.sc[c] * r.sl[p * (nt + 1) + c] + gain
        r.sl[p * (nt + 1) + c + 1] = state

    leaves = (lambda i: lax.rem(i, nt) == nt - 1), (lambda i: pack(lax.div(i, nt), nt))

    loop(KEY_SIDE, npair * nt, key_side, [leaves])

    up_y[1].start()

    def project_query(t):
        rows = rows_at(t * T, T)
        hid = r.hf[rows, :]
        r.ht[:, pl.ds(pl.multiple_of(t * T, LANES), T)] = hid.T
        q = dot(hid, r.wq[...]).astype(BF16)
        for p in range(npair):
            r.q[p, rows, :] = q[:, p * LANES : (p + 1) * LANES]

    loads["wq"].wait()
    loop(PROJECT_QUERY, nt, project_query)

    def query_side(i):
        p, c = lax.div(i, nt), lax.rem(i, nt)
        rows = rows_at(c * T, T)
        r.phiq[p, rows, :] = features(r.q[p, rows, :], p)

    loop(QUERY_SIDE, npair * nt, query_side)

    def all_masks():
        for c in range(nt):
            masks(c)

    once(ALL_MASKS, all_masks)

    def attend(i):
        p, c = lax.div(i, nt), lax.rem(i, nt)
        rows = rows_at(c * T, T)
        state = (r.sl[p * (nt + 1) + c] + r.sc[nt + c] * r.tin[p]).astype(BF16)
        state = split(state)
        r.st[i] = state
        phi_q, phi_k = r.phiq[p, rows, :], r.phik[p, rows, :]
        scores = cat([dot_t(phi_q[:, :M], phi_k[:, :M]), dot_t(phi_q[:, M:], phi_k[:, M:])], 1)
        scores = scores.astype(BF16) * twice(r.mask[c])
        vals = r.vp[p, rows, :]
        both = dot(scores, cat([vals * low, vals * high], 0))
        both = both + twice(r.use[rows, :].astype(F32)) * dot_t(phi_q, state)
        inv = 1.0 / both[:, LANES:]
        lanes = pl.ds(pl.multiple_of(p * LANES, LANES), LANES)
        r.inv[rows, lanes] = inv
        r.mix[rows, lanes] = (both[:, :LANES] * inv).astype(BF16)

    loop(ATTEND, npair * nt, attend, before=collect)

    def acc(t):
        return cat([r.sl[2 * t], r.sl[2 * t + 1]], 1)

    def add_acc(t, v):
        r.sl[2 * t] += v[:, :M]
        r.sl[2 * t + 1] += v[:, M:]

    def middle(t):
        rows = rows_at(t * T, T)
        res = r.tok[rows, :].astype(F32) + dot(r.mix[rows, :], r.wo[...])
        r.res[rows, :] = res
        mean = jnp.mean(res, axis=-1, keepdims=True)
        cen = res - mean
        inv = lax.rsqrt(jnp.mean(cen * cen, axis=-1, keepdims=True) + NORM_EPS)
        r.hf[rows, :] = ((cen * inv) * r.gf[...]).astype(BF16)
        r.sl[2 * t] = res[:, :M]
        r.sl[2 * t + 1] = res[:, M:]
        r.sl[2 * nt + 2 * t] = jnp.zeros((T, M), F32)
        r.sl[2 * nt + 2 * t + 1] = jnp.zeros((T, M), F32)

    loads["wo"].wait()
    loop(MIDDLE, nt, middle)
    loads["go"].wait()
    own_up.wait()
    own_down.wait()
    up_core.wait_recv()
    down_core.wait_recv()
    for copy in up_on:
        copy.wait_recv()
    down_on.wait_recv()
    def transposes():
        for t in range(nt):
            rows = slice(t * T, (t + 1) * T)
            r.hft[:, rows] = r.hf[rows, :].T
            r.got_t[:, rows] = r.go[rows, :].T

    once(TRANSPOSES, transposes)

    def add_rows(dst, start, src, n):
        step = min(n, 128)

        def one(b, _):
            at = rows_at(start + b * step, step)
            dst[at, :] = dst[at, :] + src[rows_at(b * step, step), :]
            return 0

        lax.fori_loop(0, n // step, one, 0)

    bits = {"c": core, "x": xbit, "y": ybit}

    def flips(axes):
        out = [""]
        for axis in axes:
            out = out + [f + axis for f in out]
        return out[1:]

    def device(flip):
        to = {"": tp, "c": tp_core, "y": tp_y, "cy": tp_far}["".join(a for a in "cy" if a in flip)]
        return (dp + 1 - 2 * xbit if "x" in flip else dp, to)

    def place(axes, flip):
        index = 0
        for axis in axes:
            index = index * 2 + (1 - bits[axis] if axis in flip else bits[axis])
        return index

    def sum_chain(name, buf, res, stages, recvs, recv_z, out, starts=True, extra=None):
        start, n, to, back, spans = 0, buf.shape[0], [], [], []
        count = sum(len(flips(axes)) for axes in stages)
        base = sems(2 * count + 2 * (nz - 1))
        for axes, recv in zip(stages, recvs):
            n = n // 2 ** len(axes)
            others = flips(axes)
            to.append([])
            back.append([])
            here = start + place(axes, "") * n
            kept = rows_at(here, n)
            for flip, landing in zip(others, recv):
                there = rows_at(start + place(axes, flip) * n, n)
                to[-1].append(remote(buf.at[there], landing, base, device(flip)))
                back[-1].append(remote(res.at[kept], res.at[kept], base + 1, device(flip)))
                base = base + 2
            start = here
            spans.append((start, n))
        base = base - 1
        cut = n // nz if (n // nz) % 16 == 0 else n
        share = cut != n
        piece = lambda z: rows_at(start + (z * cut if share else 0), cut)
        to_z = [
            remote(buf.at[piece(z_at(k))], recv_z.at[k - 1, :cut], base + k, dev_z(k))
            for k in range(1, nz)
        ]
        own = piece(zi)
        back_z = [
            remote(res.at[own], res.at[own], base + nz - 1 + k, dev_z(k)) for k in range(1, nz)
        ] if share else []

        def part_sum(j):
            for copy in to[j]:
                copy.wait_recv()
            for landing in recvs[j]:
                add_rows(buf, spans[j][0], landing, spans[j][1])
            if extra is not None:
                extra(spans[j])
            start_all(*(to_z if j + 1 == len(to) else to[j + 1]))

        def sum_z():
            for copy in to_z:
                copy.wait_recv()
            total = buf[own, :].astype(F32)
            for k in range(1, nz):
                total = total + recv_z[k - 1, :cut].astype(F32)
            res[own, :] = total.astype(BF16)
            start_all(*back_z)

        handed = [back_z] + back[::-1]
        follow = back[::-1] + [[out]]
        first = [functools.partial(start_all, *to[0])] if starts else []
        chain(
            name, *first, *[functools.partial(part_sum, j) for j in range(len(to))], sum_z,
            *[then(a, *b) for a, b in zip(handed, follow)],
        )
        for group in to + [to_z, back_z] + back:
            last_sends.extend(group)
        outs.append(out)
        return to[0]

    f_base = sems(5)
    f_c0 = remote(r.ct.at[0], r.fc.at[0], f_base, dev_core)
    f_c1 = remote(r.ct.at[2], r.fc.at[1], f_base + 1, dev_core)
    f_part = rows_at(xbit * (D // 2), D // 2)
    f_other = rows_at((1 - xbit) * (D // 2), D // 2)
    f_y = remote(r.ct.at[1, 0], r.fy.at[0], f_base + 2, dev_y)
    f_x = remote(r.ct.at[1, 1, f_other], r.fy.at[1, D // 2 :], f_base + 3, dev_x)
    f_xy = remote(r.ct.at[1, 1, f_part], r.fy.at[1, : D // 2], f_base + 4, dev_y)
    f_outs = [pltpu.make_async_copy(r.fo.at[g], r.fo_out.at[g], r.ls.at[3 + g]) for g in range(2)]
    last_sends, outs = [f_y, f_x, f_xy], []

    def across_up():
        f_y.wait_recv()
        add_rows(r.ct.at[3, 0], 0, r.fy.at[0], D)
        start_all(*f0)

    def plane_down():
        f_x.wait_recv()
        add_rows(r.ct.at[1, 1], xbit * (D // 2), r.fy.at[1, D // 2 :], D // 2)
        f_xy.start()

    def across_down(span):
        f_xy.wait_recv()
        add_rows(r.ct.at[3, 1], span[0], r.fy.at[1, : D // 2], span[1])

    f0 = sum_chain(
        FFN_UP, r.ct.at[3, 0], r.fo.at[0], ["x"], [[r.fx.at[0]]], r.fz.at[0], f_outs[0], False
    )
    f1 = sum_chain(
        FFN_DOWN, r.ct.at[3, 1], r.fo.at[1], ["x"], [[r.fx.at[1]]], r.fz.at[1], f_outs[1], False, across_down
    )
    steps[FFN_UP].insert(0, across_up)
    chain(FFN_ACROSS, plane_down)

    def ffn(k, s, out):
        def tile(t):
            rows = rows_at(t * T, T)
            for h in range(2):
                lanes = slice(h * (D // 2), (h + 1) * (D // 2))
                up = dot(r.hf[rows, :], r.wu[s, :, lanes])
                grad_act = dot_t(r.go[rows, :], r.wd[s, lanes, :])
                cubic = (GELU_SCALE * GELU_CUBIC) * (up * up)
                tang = jnp.tanh(up * (GELU_SCALE + cubic))
                half_up, half_t = 0.5 * up, 0.5 + 0.5 * tang
                slope = half_t + half_up * (1.0 - tang * tang) * (GELU_SCALE + 3.0 * cubic)
                r.gp[rows, lanes] = (up * half_t).astype(BF16)
                r.gp[rows, slice(D + lanes.start, D + lanes.stop)] = (grad_act * slope).astype(BF16)
            add_acc(t, dot(r.gp[rows, :D], r.wd[s]))
            add_acc(nt + t, dot_t(r.gp[rows, D : 2 * D], r.wu[s]))

        loop(FFN_TILE + k, nt, tile)

        def grads(t):
            rows = rows_at(t * T, T)
            out[0, rows, :] = dot(r.hft[rows, :], r.gp[:, D : 2 * D]).astype(BF16)
            out[1, rows, :] = dot(r.got_t[rows, :], r.gp[:, :D]).astype(BF16)

        loop(FFN_GRADS + k, D // T, grads)

    ffn(0, tp_far, r.ct.at[0])
    f_c0.start()
    ffn(1, tp_y, r.ct.at[1])
    f_c0.wait_recv()
    add_rows(r.ct.at[1, 1], 0, r.fc.at[0, 1], D)
    f_x.start()
    add_rows(r.ct.at[1, 0], 0, r.fc.at[0, 0], D)
    f_y.start()
    ffn(2, tp_core, r.ct.at[2])
    f_c1.start()
    ffn(3, tp, r.ct.at[3])
    f_c1.wait_recv()
    add_rows(r.ct.at[3, 1], 0, r.fc.at[1, 1], D)
    start_all(*f1)
    add_rows(r.ct.at[3, 0], 0, r.fc.at[1, 0], D)

    ones_row = lax.broadcasted_iota(jnp.int32, (2 * LANES, LANES), 0)
    ones_col = lax.broadcasted_iota(jnp.int32, (2 * LANES, LANES), 1)
    head_ones = (lax.div(lax.rem(ones_row, LANES), 64) == lax.div(ones_col, 64)).astype(F32).astype(BF16)
    r.gg[...] = jnp.zeros((2, 8, D), F32)

    def gn_at(c):
        return rows_at(lax.rem(c, 2) * T, T), pl.ds(pl.multiple_of(lax.div(c, 2) * T, T), T)

    def gn_of(p, c):
        at, wide_at = gn_at(c)
        return r.wd[p, at, wide_at]

    def fold(v):
        return jnp.sum(v.reshape(T // 8, 8, D), axis=0)

    for copy in w_sends:
        copy.wait_send()

    def back_middle(t):
        rows = rows_at(t * T, T)
        r.hf[rows, :] = acc(t).astype(BF16)
        res = r.res[rows, :]
        mean = jnp.mean(res, axis=-1, keepdims=True)
        cen = res - mean
        inv = lax.rsqrt(jnp.mean(cen * cen, axis=-1, keepdims=True) + NORM_EPS)
        n = cen * inv
        gh = acc(nt + t)
        r.gg[0] += fold(gh * n)
        sc = gh * r.gf[...]
        centre = jnp.mean(sc, axis=-1, keepdims=True)
        inner = jnp.mean(sc * n, axis=-1, keepdims=True)
        gres = r.go[rows, :].astype(F32) + inv * (sc - centre - n * inner)
        r.res[rows, :] = gres
        gattn = gres.astype(BF16)
        r.gp[rows, 2 * D :] = gattn
        gmi = dot_t(gattn, r.wo[...]) * r.inv[rows, :]
        w = gmi * r.mix[rows, :].astype(F32) * (-1.0)
        hi = w.astype(BF16)
        lo = (w - hi.astype(F32)).astype(BF16)
        gnum = gmi.astype(BF16)
        for p in range(npair):
            lanes = slice(p * LANES, (p + 1) * LANES)
            gden = dot(cat([hi[:, lanes], lo[:, lanes]], 1), head_ones).astype(BF16)
            at, wide_at = gn_at(t)
            r.wd[p, at, wide_at] = cat([gnum[:, lanes], gden * jnp.asarray(1.0 / 64.0, BF16)], 1)

    loop(BACK_MIDDLE, nt, back_middle)
    out_copy = pltpu.make_async_copy(r.hf, r.out, r.ls.at[13])
    out_copy.start()

    bpack, steps[STATE_GRADS], bcollect = state_exchange(1, r.own, r.bgot)

    def state_back(i):
        p, c = lax.div(i, nt), nt - 1 - lax.rem(i, nt)
        rows = rows_at(c * T, T)

        @pl.when(c == nt - 1)
        def _():
            r.sl[p * (nt + 1) + nt] = jnp.zeros((M, M), F32)

        gain = merge(dot_c(gn_of(p, c) * twice(r.use[rows, :]), r.phiq[p, rows, :]))
        state = r.sc[c] * r.sl[p * (nt + 1) + c + 1] + gain
        r.sl[p * (nt + 1) + c] = state

    bleaves = (lambda i: lax.rem(i, nt) == nt - 1), (lambda i: bpack(lax.div(i, nt), 0))

    loop(STATE_BACK, npair * nt, state_back, [bleaves])

    half = D // 2
    parts = [
        (SUM_O, 0, 0, 0, D), (SUM_Q, 1, 1, 0, D - LANES), (SUM_Q3, 2, 1, D - LANES, LANES)
    ]
    parts = parts + [(SUM_K + p, 2, 2 + p // 2, (p % 2) * half, half) for p in range(npair)]
    for i, (name, kind, g, lane, n) in enumerate(parts):
        lanes = slice(lane, lane + n)
        core_land = r.fc.at[0, g, :half, lanes] if g < 2 else r.fc.at[0, g - 2, half:, lanes]
        stages = STAGES[kind]
        recvs, at = [[core_land]], 0
        rows = D // 2
        for axes in stages[1:]:
            rows = rows // 2 ** len(axes)
            recvs.append([r.land.at[g, pl.ds(at + k * rows, rows), lanes] for k in range(2 ** len(axes) - 1)])
            at = at + rows * (2 ** len(axes) - 1)
        rz = r.land_z.at[g, :, :, lanes]
        source = r.ct.at[0 if g < 2 else 2, g % 2, :, lanes]
        sum_chain(
            name, source, r.wu.at[g, :, lanes], stages, recvs, rz,
            pltpu.make_async_copy(r.wu.at[g, :, lanes], r.grads.at[g, :, lanes], r.ls.at[5 + i]),
        )

    f_c0.wait_send()
    f_c1.wait_send()
    def out_grads():
        for t in range(D // T):
            rows = slice(t * T, (t + 1) * T)
            r.ct[0, 0, rows, :] = dot_c(r.mix[:, rows], r.gp[:, 2 * D :]).astype(BF16)

    once(OUT_GRADS, out_grads)

    def back_query(i):
        p, c = lax.div(i, nt), lax.rem(i, nt)
        rows = rows_at(c * T, T)
        vals, gn = r.vp[p, rows, :], gn_of(p, c)
        phi_q, phi_k = r.phiq[p, rows, :], r.phik[p, rows, :]
        g = dot_t(gn, cat([vals * low, vals * high], 0)).astype(BF16) * twice(r.mask[c])
        used = gn * twice(r.use[rows, :])
        gphi = cat([dot(g[:, :M], phi_k[:, :M]), dot(g[:, M:], phi_k[:, M:])], 1)
        gphi = gphi + dot(used, r.st[i])
        t = (gphi * phi_q.astype(F32)).astype(BF16)
        o = dot_t(t, r.bb[p, : 2 * LANES])
        gq = c4 * o[:, :LANES] - r.q[p, rows, :].astype(F32) * (o[:, LANES:] * 0.125)
        r.gp[rows, pl.ds(pl.multiple_of(p * LANES, LANES), LANES)] = gq.astype(BF16)

    loop(BACK_QUERY, (npair - 1) * nt, back_query)
    def query_grads(lanes):
        for t in range(D // T):
            rows = slice(t * T, (t + 1) * T)
            r.ct[0, 1, rows, lanes] = dot(r.ht[rows, :], r.gp[:, lanes]).astype(BF16)

    once(QUERY_GRADS, lambda: query_grads(slice(0, D - LANES)))

    def pair_grads(i):
        p = lax.div(i, nt)
        kv = cat(
            [r.gp[:, pl.ds(pl.multiple_of(o * D + p * LANES, LANES), LANES)] for o in (1, 2)], 1
        )
        wide_at = pl.ds(pl.multiple_of(lax.rem(p, 2) * half, half), half)
        for t in range(D // T):
            rows = slice(t * T, (t + 1) * T)
            r.ct[2, lax.div(p, 2), rows, wide_at] = dot(r.ht[rows, :], kv).astype(BF16)

    def back_key(i):
        p, c = lax.div(i, nt), lax.rem(i, nt)
        rows = rows_at(c * T, T)
        dstate = split((r.sl[p * (nt + 1) + c + 1] + r.sc[2 * nt + c] * r.tin[p]).astype(BF16))
        vals, gn = r.vp[p, rows, :], gn_of(p, c)
        phi_q, phi_k = r.phiq[p, rows, :], r.phik[p, rows, :]
        mask = twice(r.maskt[c])
        gt = cat([dot_t(vals * low, gn), dot_t(vals * high, gn)], 1).astype(BF16) * mask
        st = cat([dot_t(phi_k[:, :M], phi_q[:, :M]), dot_t(phi_k[:, M:], phi_q[:, M:])], 1)
        st = st.astype(BF16) * mask
        tail = r.tail[rows, :]
        left = vals * twice(tail)
        gphi = cat(
            [
                dot(cat([gt[:, m], left], 1), cat([phi_q[:, m], dstate[:, m]], 0))
                for m in (slice(0, M), slice(M, 2 * M))
            ],
            1,
        )
        gnum = gn[:, :LANES]
        gv = dot(st, cat([gnum * low[:, :LANES], gnum * high[:, :LANES]], 0))
        gv = gv + tail.astype(F32) * dot_t(phi_k, dstate[:LANES])
        t = (gphi * phi_k.astype(F32)).astype(BF16)
        o = dot_t(t, r.bb[p, : 2 * LANES])
        gk = c4 * o[:, :LANES] - r.k[p, rows, :].astype(F32) * (o[:, LANES:] * 0.125)
        r.gp[rows, pl.ds(pl.multiple_of(D + p * LANES, LANES), LANES)] = gk.astype(BF16)
        r.gp[rows, pl.ds(pl.multiple_of(2 * D + p * LANES, LANES), LANES)] = gv.astype(BF16)

    loop(BACK_KEY, npair * nt, back_key, [((lambda i: lax.rem(i, nt) == nt - 1), pair_grads)], bcollect)

    loop(LAST_QUERY, nt, lambda c: back_query((npair - 1) * nt + c))
    once(LAST_GRADS, lambda: query_grads(slice(D - LANES, D)))

    def back_first(t):
        rows = rows_at(t * T, T)
        gh = dot_t(r.gp[rows, :D], r.wq[...])
        gh = gh + dot_t(r.gp[rows, D : 2 * D], r.wk[...])
        gh = gh + dot_t(r.gp[rows, 2 * D :], r.wv[...])
        x = r.tok[rows, :].astype(F32)
        mean = jnp.mean(x, axis=-1, keepdims=True)
        cen = x - mean
        inv = lax.rsqrt(jnp.mean(cen * cen, axis=-1, keepdims=True) + NORM_EPS)
        n = cen * inv
        r.gg[1] += fold(gh * n)
        sc = gh * r.ga[...]
        centre = jnp.mean(sc, axis=-1, keepdims=True)
        inner = jnp.mean(sc * n, axis=-1, keepdims=True)
        r.res[rows, :] += inv * (sc - centre - n * inner)

    loop(BACK_FIRST, nt, back_first)
    gt_copy = pltpu.make_async_copy(r.res, r.gt, r.ls.at[3 + 9])
    gt_copy.start()

    g_base = sems(3 + ndp - 1)
    sums = [jnp.sum(r.gg[k], axis=0, keepdims=True) for k in range(2)]
    r.g1[...] = cat([v[:, j : j + LANES] for v in sums for j in range(0, D, LANES)], 0)
    g_tp = [remote(r.g1, r.gr.at[k - 1], g_base + k - 1, (dp, lax.rem(tp + k, 4))) for k in (1, 2, 3)]
    g_dp = [
        remote(r.g2, r.gr.at[2 + k], g_base + 2 + k, (lax.rem(dp + k, ndp), tp)) for k in range(1, ndp)
    ]
    start_all(*g_tp)

    def gains_tp():
        for copy in g_tp:
            copy.wait_recv()
        r.g2[...] = r.g1[...] + r.gr[0] + r.gr[1] + r.gr[2]
        start_all(*g_dp)

    def gains_dp():
        total = r.g2[...]
        for k in range(1, ndp):
            g_dp[k - 1].wait_recv()
            total = total + r.gr[2 + k]
        r.gout[...] = total

    chain(GAINS, gains_tp, gains_dp)
    advance(TAIL, 0)
    assert not plan and not any(steps.values())

    for copy in seg_copies + last_sends + g_tp + g_dp:
        copy.wait_send()
    for copy in outs + [out_copy, gt_copy]:
        copy.wait()
    assert used[0] <= r.ss.shape[0]


def layer(tokens, segment_ids, grad_out, w_query, w_key, w_value, w_out, w_up, w_down, gain_attn,
          gain_ffn, feature_basis):
    _, L, D = tokens.shape
    H, DH, M = feature_basis.shape
    F = w_up.shape[1]
    npair, nt = H // 2, L // T
    ndp = lax.axis_size("dp")
    nz = ndp // 2
    assert lax.axis_size("tp") == 4 and F == D and DH == 64 and M == T

    vmem, hbm = pl.BlockSpec(memory_space=pltpu.VMEM), pl.BlockSpec(memory_space=pl.ANY)
    ins = {
        "seg": (segment_ids, vmem),
        "tok_in": (tokens[0], hbm),
        "go_in": (grad_out[0], hbm),
        "wq_in": (w_query, hbm),
        "wk_in": (w_key, hbm),
        "wv_in": (w_value, hbm),
        "wo_in": (w_out, hbm),
        "wup": (w_up, hbm),
        "wdn": (w_down, hbm),
        "ga": (gain_attn[None], vmem),
        "gf": (gain_ffn[None], vmem),
        "basis_in": (feature_basis, hbm),
    }
    outs = {
        "out": ((L, D), BF16, hbm),
        "gt": ((L, D), F32, hbm),
        "fo_out": ((2, D, F), BF16, hbm),
        "grads": ((4, D, D), BF16, hbm),
        "gout": ((8, LANES), F32, vmem),
    }

    scratch = {
        "tok": ((L, D), BF16),
        "wk": ((D, D), BF16),
        "wv": ((D, D), BF16),
        "wq": ((D, D), BF16),
        "wo": ((D, D), BF16),
        "go": ((L, D), BF16),
        "sg": ((4, 1, L), jnp.int32),
        "wu": ((4, D, F), BF16),
        "wd": ((4, F, D), BF16),
        "bb": ((npair, 3 * LANES, 2 * M), BF16),
        "ht": ((D, L), BF16),
        "q": ((npair, L, LANES), BF16),
        "k": ((npair, L, LANES), BF16),
        "vp": ((npair, L, 2 * LANES), BF16),
        "sc": ((3 * nt + 8, 1, M), F32),
        "use": ((L, LANES), BF16),
        "tail": ((L, LANES), BF16),
        "mask": ((nt, T, M), BF16),
        "maskt": ((nt, T, M), BF16),
        "phik": ((npair, L, 2 * M), BF16),
        "phiq": ((npair, L, 2 * M), BF16),
        "sl": ((npair * (nt + 1), M, M), F32),
        "own": ((npair, 144, M), BF16),
        "got": ((4, npair, 144, M), BF16),
        "bgot": ((4, npair, 144, M), BF16),
        "tin": ((npair, M, M), F32),
        "st": ((npair * nt, M, 2 * M), BF16),
        "inv": ((L, D), F32),
        "mix": ((L, D), BF16),
        "res": ((L, D), F32),
        "hf": ((L, D), BF16),
        "hft": ((D, L), BF16),
        "got_t": ((D, L), BF16),
        "ct": ((4, 2, D, F), BF16),
        "fc": ((2, 2, D, F), BF16),
        "land": ((4, 192, D), BF16),
        "land_z": ((4, nz - 1, D // 8, D), BF16),
        "fy": ((2, D, F), BF16),
        "fx": ((2, D // 2, F), BF16),
        "fz": ((2, nz - 1, D // 2 // nz, F), BF16),
        "fo": ((2, D, F), BF16),
        "gg": ((2, 8, D), F32),
        "gp": ((L, 3 * D), BF16),
        "g1": ((8, LANES), F32),
        "g2": ((8, LANES), F32),
        "gr": ((3 + ndp - 1, 8, LANES), F32),
    }
    n_sems = 40 + 6 * npair + ndp + (4 + npair) * (10 + 2 * (nz - 1)) + 5 * (nz - 1)
    names = list(ins) + list(outs) + list(scratch) + ["ls", "ss", "rs"]
    res = pl.pallas_call(
        functools.partial(layer_kernel, nz, names),
        out_shape=[jax.ShapeDtypeStruct(s, d) for s, d, _ in outs.values()],
        in_specs=[spec for _, spec in ins.values()],
        out_specs=[spec for _, _, spec in outs.values()],
        scratch_shapes=[pltpu.VMEM(s, d) for s, d in scratch.values()]
        + [
            pltpu.SemaphoreType.DMA((28,)),
            pltpu.SemaphoreType.DMA((n_sems,)),
            pltpu.SemaphoreType.DMA((n_sems,)),
        ],
        name="layer",
        compiler_params=pltpu.CompilerParams(
            collective_id=0, has_side_effects=True, vmem_limit_bytes=67043328
        ),
    )(*[a for a, _ in ins.values()])
    return hand_out(*res)


def hand_out_kernel(out, gt, up, down, grads, gains, *refs):
    o_out, o_gt, o_query, o_key, o_value, o_proj, o_up, o_down, o_attn, o_ffn = refs
    o_out[0] = out[...]
    o_gt[0] = gt[...]
    o_up[...] = up[0].astype(F32)
    o_down[...] = down[0].astype(F32).T
    o_proj[...] = grads[0].astype(F32)
    o_query[...] = grads[1].astype(F32)
    for p in range(grads.shape[2] // LANES):
        lanes = slice(p * LANES, (p + 1) * LANES)
        at = (p % 2) * 2 * LANES
        o_key[:, lanes] = grads[2 + p // 2, :, at : at + LANES].astype(F32)
        o_value[:, lanes] = grads[2 + p // 2, :, at + LANES : at + 2 * LANES].astype(F32)
    for j in range(4):
        lanes = slice(j * LANES, (j + 1) * LANES)
        o_ffn[:, lanes] = gains[j : j + 1, :]
        o_attn[:, lanes] = gains[4 + j : 5 + j, :]


def hand_out(out, gt, fo, grads, gains):
    (L, D), steps = out.shape, 2
    lr, dr = L // steps, D // steps
    tall = pl.BlockSpec((1, lr, D), lambda i: (0, i, 0))
    flat = pl.BlockSpec((dr, D), lambda i: (i, 0))
    row = pl.BlockSpec((1, D), lambda i: (0, 0))
    f32 = lambda *shape: jax.ShapeDtypeStruct(shape, F32)
    res = pl.pallas_call(
        hand_out_kernel,
        grid=(steps,),
        in_specs=[
            pl.BlockSpec((lr, D), lambda i: (i, 0)),
            pl.BlockSpec((lr, D), lambda i: (i, 0)),
            pl.BlockSpec((1, dr, D), lambda i: (0, i, 0)),
            pl.BlockSpec((1, D, dr), lambda i: (1, 0, i)),
            pl.BlockSpec((4, dr, D), lambda i: (0, i, 0)),
            pl.BlockSpec((8, LANES), lambda i: (0, 0)),
        ],
        out_specs=[tall, tall, flat, flat, flat, flat, flat, flat, row, row],
        out_shape=[jax.ShapeDtypeStruct((1, L, D), BF16), f32(1, L, D)]
        + [f32(D, D)] * 6 + [f32(1, D)] * 2,
        name="hand_out", compiler_params=pltpu.CompilerParams(vmem_limit_bytes=60000000),
    )(out, gt, fo, fo, grads, gains)
    return (*res[:8], res[8][0], res[9][0])


def solution(mesh):
    whole = P()
    in_specs = (
        P("dp", "tp", None), P("dp", "tp"), P("dp", "tp", None), whole, whole, whole, whole,
        P(None, "tp"), P("tp", None), whole, whole, whole,
    )
    out_specs = (
        P("dp", "tp", None), P("dp", "tp", None), whole, whole, whole, whole,
        P(None, "tp"), P("tp", None), whole, whole,
    )
    return jax.shard_map(layer, mesh=mesh, in_specs=in_specs, out_specs=out_specs, check_vma=False)
```

```python
import functools
import math
from types import SimpleNamespace

import jax
import jax.numpy as jnp
from jax import lax
from jax.experimental import pallas as pl
from jax.experimental.pallas import tpu as pltpu
from jax.sharding import PartitionSpec as P

MESH = pl.DeviceIdType.MESH
F32 = jnp.float32
BF16 = jnp.bfloat16
NORM_EPS = 1e-05
GELU_SCALE = 0.7978845608028654
GELU_CUBIC = 0.044715
LANES = 128
(
    PROJECT, BASIS_BLOCKS, KEY_SIDE, PROJECT_QUERY, QUERY_SIDE, ALL_MASKS,
    ATTEND, MIDDLE, TRANSPOSES, BACK_MIDDLE, STATE_BACK, OUT_GRADS,
    BACK_QUERY, QUERY_GRADS, BACK_KEY, LAST_QUERY, LAST_GRADS, BACK_FIRST,
    TAIL,
) = range(19)
FFN_TILE, FFN_GRADS = 19, 23
(
    W_UP, W_DOWN, STATES, STATE_GRADS, FFN_ACROSS,
    FFN_UP, FFN_DOWN, SUM_O, SUM_Q, SUM_Q3, GAINS,
    SUM_K,
) = range(12)
PLAN = (
    (KEY_SIDE, 3, W_DOWN),
    (PROJECT_QUERY, 0, W_UP),
    (QUERY_SIDE, 3, STATES),
    (QUERY_SIDE, 11, STATES),
    (QUERY_SIDE, 15, W_DOWN),
    (ALL_MASKS, 0, STATES),
    (ATTEND, 3, STATES),
    (MIDDLE, 1, W_UP),
    (MIDDLE, 3, W_DOWN),
    (FFN_TILE + 3, 3, FFN_ACROSS),
    (BACK_MIDDLE, 3, FFN_UP),
    (OUT_GRADS, 0, FFN_DOWN),
    (OUT_GRADS, 0, SUM_O),
    (BACK_QUERY, 3, STATE_GRADS),
    (BACK_QUERY, 3, SUM_O),
    (BACK_QUERY, 7, STATE_GRADS),
    (BACK_QUERY, 11, STATE_GRADS),
    (BACK_QUERY, 11, FFN_UP),
    (BACK_QUERY, 11, STATE_GRADS),
    (QUERY_GRADS, 0, SUM_Q),
    (BACK_KEY, 3, FFN_DOWN),
    (BACK_KEY, 3, SUM_K),
    (BACK_KEY, 3, SUM_Q),
    (BACK_KEY, 3, SUM_O),
    (BACK_KEY, 5, SUM_K),
    (BACK_KEY, 7, SUM_K + 1),
    (BACK_KEY, 9, FFN_UP),
    (BACK_KEY, 9, SUM_K + 1),
    (BACK_KEY, 9, SUM_Q),
    (BACK_KEY, 11, SUM_K + 2),
    (BACK_KEY, 11, SUM_O),
    (BACK_KEY, 13, SUM_K + 2),
    (BACK_KEY, 13, SUM_K),
    (BACK_KEY, 15, FFN_DOWN),
    (BACK_KEY, 15, SUM_K + 1),
    (BACK_KEY, 15, SUM_K + 3),
    (BACK_KEY, 15, SUM_Q),
    (LAST_QUERY, 3, SUM_K + 3),
    (LAST_GRADS, 0, SUM_Q3),
    (LAST_GRADS, 0, SUM_K + 2),
    (BACK_FIRST, 1, SUM_Q3),
    (BACK_FIRST, 3, FFN_UP),
    (TAIL, 0, SUM_O),
    (TAIL, 0, SUM_K),
    (TAIL, 0, FFN_DOWN),
    (TAIL, 0, SUM_K + 1),
    (TAIL, 0, GAINS),
    (TAIL, 0, SUM_Q),
    (TAIL, 0, SUM_K + 2),
    (TAIL, 0, SUM_K + 3),
    (TAIL, 0, SUM_Q3),
    (TAIL, 0, SUM_O),
    (TAIL, 0, SUM_K),
    (TAIL, 0, SUM_K + 1),
    (TAIL, 0, GAINS),
    (TAIL, 0, FFN_UP),
    (TAIL, 0, SUM_Q),
    (TAIL, 0, SUM_K + 2),
    (TAIL, 0, SUM_O),
    (TAIL, 0, SUM_K + 3),
    (TAIL, 0, SUM_Q3),
    (TAIL, 0, SUM_Q),
    (TAIL, 0, SUM_K),
    (TAIL, 0, SUM_K),
    (TAIL, 0, SUM_K + 1),
    (TAIL, 0, SUM_K + 3),
    (TAIL, 0, SUM_Q3),
    (TAIL, 0, SUM_K + 2),
    (TAIL, 0, SUM_K + 1),
    (TAIL, 0, SUM_O),
    (TAIL, 0, SUM_Q),
    (TAIL, 0, SUM_K + 2),
    (TAIL, 0, SUM_O),
    (TAIL, 0, SUM_Q),
    (TAIL, 0, SUM_K + 3),
    (TAIL, 0, SUM_Q3),
    (TAIL, 0, SUM_K + 3),
    (TAIL, 0, SUM_Q3),
)
UNROLL = {
    PROJECT: 2,
    MIDDLE: 2,
    BACK_MIDDLE: 2,
    BACK_FIRST: 2,
    BACK_KEY: 2,
    FFN_TILE: 2,
    KEY_SIDE: 4,
    QUERY_SIDE: 4,
    ATTEND: 4,
    STATE_BACK: 4,
    BACK_QUERY: 4,
    LAST_QUERY: 4,
}
STAGES = (("c", "y", "x"), ("c", "x", "y"), ("c", "xy"))
T = 256


def dot(a, b):
    return jnp.dot(a, b, preferred_element_type=F32)


def dot_t(a, b):
    return lax.dot_general(a, b, (((1,), (1,)), ((), ())), preferred_element_type=F32)


def dot_c(a, b):
    return lax.dot_general(a, b, (((0,), (0,)), ((), ())), preferred_element_type=F32)


def rows_at(start, size):
    return pl.ds(pl.multiple_of(start, 16), size)


def cat(parts, axis):
    return jnp.concatenate(parts, axis=axis)


def lane_groups():
    lane = lax.broadcasted_iota(jnp.int32, (1, 2 * LANES), 1)
    first = lax.rem(lane, LANES) < 64
    one = jnp.where(first, 1.0, 0.0)
    return one.astype(BF16), (1.0 - one).astype(BF16)


def layer_kernel(nz, names, *refs):
    r = SimpleNamespace(**dict(zip(names, refs)))
    L, D = r.tok.shape
    nt = L // T
    npair = r.basis_in.shape[0] // 2
    M = r.basis_in.shape[2]
    c4 = 64.0**-0.25
    exp_scale = c4 * math.log2(math.e)

    dp, tp = lax.axis_index("dp"), lax.axis_index("tp")
    ndp = 2 * nz
    core, ybit = lax.rem(tp, 2), lax.div(tp, 2)
    xbit, zi = lax.rem(dp, 2), lax.div(dp, 2)
    tp_core, tp_y, tp_far = tp + 1 - 2 * core, lax.rem(tp + 2, 4), 3 - tp
    dev_core, dev_y, dev_far = (dp, tp_core), (dp, tp_y), (dp, tp_far)
    dev_x = (dp + 1 - 2 * xbit, tp)

    def z_at(k):
        return lax.rem(zi + k, nz)

    def dev_z(k):
        return (z_at(k) * 2 + xbit, tp)

    plan, steps = {}, {}
    for place, i, chunk in PLAN:
        plan.setdefault((place, i), []).append(chunk)

    def advance(place, i):
        for chunk in plan.pop((place, i), ()):
            steps[chunk].pop(0)()

    def loop(name, n, body, tasks=(), before=None):
        u = UNROLL.get(FFN_TILE if FFN_TILE <= name < FFN_GRADS else name, 1)

        def step(i, _):
            if before is not None:
                pl.when(lax.rem(i * u, nt) == 0)(lambda: before(lax.div(i * u, nt)))
            for k in range(u):
                body(i * u + k)
            for when, task in tasks:
                pl.when(when(i * u + u - 1))(functools.partial(task, i * u + u - 1))
            for k in range(n):
                if (name, k) in plan:
                    pl.when(i == k // u)(functools.partial(advance, name, k))
            return 0

        lax.fori_loop(0, n // u, step, 0)

    def once(name, body):
        body()
        advance(name, 0)

    used = [0]

    def sems(n):
        first = used[0]
        used[0] += n
        return first

    def remote(src, dst, idx, dev):
        return pltpu.make_async_remote_copy(
            src_ref=src, dst_ref=dst, send_sem=r.ss.at[idx], recv_sem=r.rs.at[idx],
            device_id=dev, device_id_type=MESH,
        )

    loads = {
        name: pltpu.make_async_copy(getattr(r, name + "_in"), getattr(r, name), r.ls.at[14 + k])
        for k, name in enumerate(("tok", "wk", "wv", "wq", "wo", "go"))
    }
    own_up = pltpu.make_async_copy(r.wup, r.wu.at[tp], r.ls.at[0])
    own_down = pltpu.make_async_copy(r.wdn, r.wd.at[tp], r.ls.at[1])
    own_seg = pltpu.make_async_copy(r.seg, r.sg.at[tp], r.ls.at[2])
    basis_copies = [
        pltpu.make_async_copy(
            r.basis_in.at[h], r.bb.at[h // 2, pl.ds((h % 2) * 64, 64), pl.ds((h % 2) * M, M)], r.ls.at[20 + h]
        )
        for h in range(2 * npair)
    ]
    own_seg.start()
    for copy in list(loads.values()) + basis_copies:
        copy.start()
    own_up.start()
    own_down.start()

    barrier = pltpu.get_barrier_semaphore()
    for k in (1, 2, 3):
        pl.semaphore_signal(barrier, inc=1, device_id=(dp, lax.rem(tp + k, 4)), device_id_type=MESH)
    for k in range(1, ndp):
        pl.semaphore_signal(barrier, inc=1, device_id=(lax.rem(dp + k, ndp), tp), device_id_type=MESH)


    seg_base = sems(3)
    seg_copies = [
        remote(r.seg, r.sg.at[tp], seg_base + k - 1, (dp, lax.rem(tp + k, 4))) for k in (1, 2, 3)
    ]

    up_base, down_base = sems(5), sems(4 + nz - 1)
    pr = r.wdn.shape[0] // ndp
    up_core = remote(r.wup, r.wu.at[tp], up_base, dev_core)
    hd = r.wup.shape[0] // 2
    up_y = [
        remote(r.wup.at[pl.ds(g * hd, hd)], r.wu.at[tp, pl.ds(g * hd, hd)], up_base + 1 + g, dev_y)
        for g in range(2)
    ]
    up_on = [
        remote(r.wu.at[tp_y, pl.ds(g * hd, hd)], r.wu.at[tp_y, pl.ds(g * hd, hd)], up_base + 3 + g, dev_core)
        for g in range(2)
    ]
    down_core = remote(r.wdn, r.wd.at[tp], down_base, dev_core)
    down_piece = rows_at((xbit * nz + zi) * pr, pr)
    down_plane = rows_at(xbit * nz * pr, nz * pr)
    down_y = remote(r.wdn.at[down_piece], r.wd.at[tp, down_piece], down_base + 1, dev_y)
    down_z = [
        remote(r.wd.at[tp_y, down_piece], r.wd.at[tp_y, down_piece], down_base + 3 + k, dev_z(k))
        for k in range(1, nz)
    ]
    down_x = remote(r.wd.at[tp_y, down_plane], r.wd.at[tp_y, down_plane], down_base + 2, dev_x)
    down_on = remote(r.wd.at[tp_y], r.wd.at[tp_y], down_base + 3, dev_core)
    w_sends = [up_core, down_core, down_y, down_x, down_on] + up_y + up_on + down_z

    def start_all(*copies):
        for copy in copies:
            copy.start()

    def chain(name, *tasks):
        steps[name] = list(tasks)

    def then(waits, *starts):
        def task():
            for copy in waits:
                copy.wait_recv()
            start_all(*starts)

        return task

    chain(W_UP, then(up_y[:1], up_on[0]), then(up_y[1:], up_on[1]))
    chain(W_DOWN, then([down_y], *down_z), then(down_z, down_x), then([down_x], down_on))

    def enter():
        pl.semaphore_wait(barrier, 3 + ndp - 1)
        start_all(*seg_copies, down_y, up_y[0], up_core, down_core)

    enter()

    def basis_blocks():
        zero, one = jnp.zeros((64, M), BF16), jnp.ones((64, M), BF16)
        for p in range(npair):
            for h in range(2):
                lanes = slice(h * M, (h + 1) * M)
                r.bb[p, (1 - h) * 64 : (2 - h) * 64, lanes] = zero
                r.bb[p, LANES:, lanes] = cat([one, zero, one, zero] if h == 0 else [zero, one, zero, one], 0)
        for copy in basis_copies:
            copy.wait()

    once(BASIS_BLOCKS, basis_blocks)
    low, high = lane_groups()

    def project(t):
        rows = rows_at(t * T, T)
        x = r.tok[rows, :].astype(F32)
        mean = jnp.mean(x, axis=-1, keepdims=True)
        cen = x - mean
        inv = lax.rsqrt(jnp.mean(cen * cen, axis=-1, keepdims=True) + NORM_EPS)
        hid = ((cen * inv) * r.ga[...]).astype(BF16)
        r.hf[rows, :] = hid
        k = dot(hid, r.wk[...]).astype(BF16)
        v = dot(hid, r.wv[...]).astype(BF16)
        for p in range(npair):
            lanes = slice(p * LANES, (p + 1) * LANES)
            r.k[p, rows, :] = k[:, lanes]
            r.vp[p, rows, :LANES] = v[:, lanes]
            r.vp[p, rows, LANES:] = jnp.ones((T, LANES), BF16)

    loads["tok"].wait()
    loads["wk"].wait()
    loads["wv"].wait()
    loop(PROJECT, nt, project)

    own_seg.wait()
    for copy in seg_copies:
        copy.wait_recv()
    row_max, row_min = [], []
    for j in range(4):
        ids = r.sg[j].astype(F32)
        row_max.append(jnp.max(ids, axis=1, keepdims=True))
        row_min.append(jnp.min(ids, axis=1, keepdims=True))
    in_seg = jnp.full((1, 1), -1.0, F32)
    for j in range(4):
        in_seg = jnp.maximum(in_seg, jnp.where(j < tp, row_max[j], -1.0))
    mine = r.seg[...].astype(F32)
    ends = [jnp.max(mine[:, c * T : (c + 1) * T], axis=1, keepdims=True) for c in range(nt)]
    befores = [in_seg] + ends[:-1]
    keeps = [(befores[c] == ends[c]).astype(F32) for c in range(nt)]
    wide = lambda v: jnp.broadcast_to(v, (1, M))
    flag = jnp.ones((1, 1), F32)
    for c in range(nt):
        r.sc[c] = wide(keeps[c])
        r.sc[nt + c] = wide(flag)
        flag = flag * keeps[c]
    flag = jnp.ones((1, 1), F32)
    for c in reversed(range(nt)):
        r.sc[2 * nt + c] = wide(flag)
        flag = flag * keeps[c]
    for j in range(4):
        r.sc[3 * nt + j] = wide(jnp.where(j < tp, (row_max[j] == in_seg).astype(F32), 0.0))
        r.sc[3 * nt + 4 + j] = wide(jnp.where(j > tp, (row_min[j] == ends[-1]).astype(F32), 0.0))
    row_id = lax.broadcasted_iota(jnp.int32, (T, T), 0)
    col_id = lax.broadcasted_iota(jnp.int32, (T, T), 1)
    for c in range(nt):
        along = mine[:, c * T : (c + 1) * T]
        down = jnp.broadcast_to(along, (LANES, T)).T
        rows = slice(c * T, (c + 1) * T)
        use = (down == befores[c]).astype(F32).astype(BF16)
        tail = (down == ends[c]).astype(F32).astype(BF16)
        r.use[rows, :] = use
        r.tail[rows, :] = tail

    def masks(c):
        along = mine[:, c * T : (c + 1) * T]
        down = jnp.broadcast_to(along, (LANES, T)).T
        same = (cat([down, down], 1) == along).astype(F32)
        mask = (same * (row_id >= col_id).astype(F32)).astype(BF16)
        mask_t = (same * (row_id <= col_id).astype(F32)).astype(BF16)
        r.mask[c] = mask
        r.maskt[c] = mask_t

    def twice(v):
        return cat([v, v], 1)

    def features(u, p):
        wide_u = u.astype(F32)
        square = wide_u * wide_u * (-1.0 / (16.0 * c4))
        hi = square.astype(BF16)
        lo = (square - hi.astype(F32)).astype(BF16)
        expo = dot(cat([u, hi], 1), r.bb[p, : 2 * LANES]) + dot(lo, r.bb[p, 2 * LANES :])
        return jnp.exp2(expo * exp_scale).astype(BF16)

    def merge(u):
        return cat([u[:64, :M], u[64:128, M:], u[128:192, :M], u[192:, M:]], 0)

    def split(s):
        zero = jnp.zeros((64, M), s.dtype)
        first = cat([s[:64], zero, s[128:192], zero], 0)
        second = cat([zero, s[64:128], zero, s[192:]], 0)
        return cat([first, second], 1)

    def state_exchange(i, own, got):
        base = sems(3 * npair)

        def copies(p):
            at = base + p * 3
            return (
                remote(own.at[p], got.at[tp, p], at, dev_core),
                remote(own.at[p], got.at[tp, p], at + 1, dev_y),
                remote(got.at[tp_y, p], got.at[tp_y, p], at + 2, dev_core),
            )

        def pack(p, slot):
            state = r.sl[p * (nt + 1) + slot]
            own[p, :128, :] = state[:128].astype(BF16)
            own[p, 128:, :] = cat([state[128:136], state[192:200]], 0).astype(BF16)
            to_core, to_y, _ = copies(p)
            to_y.start()
            to_core.start()

        def relay(p):
            _, to_y, on = copies(p)
            to_y.wait_recv()
            on.start()

        def collect(p):
            to_core, to_y, on = copies(p)
            to_core.wait_recv()
            on.wait_recv()
            total = jnp.zeros((144, M), F32)
            for slot in (tp_core, tp_y, tp_far):
                total = total + got[slot, p].astype(F32) * r.sc[3 * nt + 4 * i + slot]
            r.tin[p, :128, :] = total[:128]
            r.tin[p, 128:192, :] = jnp.broadcast_to(total[128:129], (64, M))
            r.tin[p, 192:, :] = jnp.broadcast_to(total[136:137], (64, M))
            to_core.wait_send()
            to_y.wait_send()
            on.wait_send()

        return pack, [functools.partial(relay, p) for p in range(npair)], collect

    pack, steps[STATES], collect = state_exchange(0, r.own, r.got)

    def key_side(i):
        p, c = lax.div(i, nt), lax.rem(i, nt)
        rows = rows_at(c * T, T)
        phi = features(r.k[p, rows, :], p)
        r.phik[p, rows, :] = phi
        gain = merge(dot_c(r.vp[p, rows, :] * twice(r.tail[rows, :]), phi))

        @pl.when(c == 0)
        def _():
            r.sl[p * (nt + 1)] = jnp.zeros((M, M), F32)

        state = r.sc[c] * r.sl[p * (nt + 1) + c] + gain
        r.sl[p * (nt + 1) + c + 1] = state

    leaves = (lambda i: lax.rem(i, nt) == nt - 1), (lambda i: pack(lax.div(i, nt), nt))

    loop(KEY_SIDE, npair * nt, key_side, [leaves])

    up_y[1].start()

    def project_query(t):
        rows = rows_at(t * T, T)
        hid = r.hf[rows, :]
        r.ht[:, pl.ds(pl.multiple_of(t * T, LANES), T)] = hid.T
        q = dot(hid, r.wq[...]).astype(BF16)
        for p in range(npair):
            r.q[p, rows, :] = q[:, p * LANES : (p + 1) * LANES]

    loads["wq"].wait()
    loop(PROJECT_QUERY, nt, project_query)

    def query_side(i):
        p, c = lax.div(i, nt), lax.rem(i, nt)
        rows = rows_at(c * T, T)
        r.phiq[p, rows, :] = features(r.q[p, rows, :], p)

    loop(QUERY_SIDE, npair * nt, query_side)

    def all_masks():
        for c in range(nt):
            masks(c)

    once(ALL_MASKS, all_masks)

    def attend(i):
        p, c = lax.div(i, nt), lax.rem(i, nt)
        rows = rows_at(c * T, T)
        state = (r.sl[p * (nt + 1) + c] + r.sc[nt + c] * r.tin[p]).astype(BF16)
        state = split(state)
        r.st[i] = state
        phi_q, phi_k = r.phiq[p, rows, :], r.phik[p, rows, :]
        scores = cat([dot_t(phi_q[:, :M], phi_k[:, :M]), dot_t(phi_q[:, M:], phi_k[:, M:])], 1)
        scores = scores.astype(BF16) * twice(r.mask[c])
        vals = r.vp[p, rows, :]
        both = dot(scores, cat([vals * low, vals * high], 0))
        both = both + twice(r.use[rows, :].astype(F32)) * dot_t(phi_q, state)
        inv = 1.0 / both[:, LANES:]
        lanes = pl.ds(pl.multiple_of(p * LANES, LANES), LANES)
        r.inv[rows, lanes] = inv
        r.mix[rows, lanes] = (both[:, :LANES] * inv).astype(BF16)

    loop(ATTEND, npair * nt, attend, before=collect)

    def acc(t):
        return cat([r.sl[2 * t], r.sl[2 * t + 1]], 1)

    def add_acc(t, v):
        r.sl[2 * t] += v[:, :M]
        r.sl[2 * t + 1] += v[:, M:]

    def middle(t):
        rows = rows_at(t * T, T)
        res = r.tok[rows, :].astype(F32) + dot(r.mix[rows, :], r.wo[...])
        r.res[rows, :] = res
        mean = jnp.mean(res, axis=-1, keepdims=True)
        cen = res - mean
        inv = lax.rsqrt(jnp.mean(cen * cen, axis=-1, keepdims=True) + NORM_EPS)
        r.hf[rows, :] = ((cen * inv) * r.gf[...]).astype(BF16)
        r.sl[2 * t] = res[:, :M]
        r.sl[2 * t + 1] = res[:, M:]
        r.sl[2 * nt + 2 * t] = jnp.zeros((T, M), F32)
        r.sl[2 * nt + 2 * t + 1] = jnp.zeros((T, M), F32)

    loads["wo"].wait()
    loop(MIDDLE, nt, middle)
    loads["go"].wait()
    own_up.wait()
    own_down.wait()
    up_core.wait_recv()
    down_core.wait_recv()
    for copy in up_on:
        copy.wait_recv()
    down_on.wait_recv()
    def transposes():
        for t in range(nt):
            rows = slice(t * T, (t + 1) * T)
            r.hft[:, rows] = r.hf[rows, :].T
            r.got_t[:, rows] = r.go[rows, :].T

    once(TRANSPOSES, transposes)

    def add_rows(dst, start, src, n):
        step = min(n, 128)

        def one(b, _):
            at = rows_at(start + b * step, step)
            dst[at, :] = dst[at, :] + src[rows_at(b * step, step), :]
            return 0

        lax.fori_loop(0, n // step, one, 0)

    bits = {"c": core, "x": xbit, "y": ybit}

    def flips(axes):
        out = [""]
        for axis in axes:
            out = out + [f + axis for f in out]
        return out[1:]

    def device(flip):
        to = {"": tp, "c": tp_core, "y": tp_y, "cy": tp_far}["".join(a for a in "cy" if a in flip)]
        return (dp + 1 - 2 * xbit if "x" in flip else dp, to)

    def place(axes, flip):
        index = 0
        for axis in axes:
            index = index * 2 + (1 - bits[axis] if axis in flip else bits[axis])
        return index

    def sum_chain(name, buf, res, stages, recvs, recv_z, out, starts=True, extra=None):
        start, n, to, back, spans = 0, buf.shape[0], [], [], []
        count = sum(len(flips(axes)) for axes in stages)
        base = sems(2 * count + 2 * (nz - 1))
        for axes, recv in zip(stages, recvs):
            n = n // 2 ** len(axes)
            others = flips(axes)
            to.append([])
            back.append([])
            here = start + place(axes, "") * n
            kept = rows_at(here, n)
            for flip, landing in zip(others, recv):
                there = rows_at(start + place(axes, flip) * n, n)
                to[-1].append(remote(buf.at[there], landing, base, device(flip)))
                back[-1].append(remote(res.at[kept], res.at[kept], base + 1, device(flip)))
                base = base + 2
            start = here
            spans.append((start, n))
        base = base - 1
        cut = n // nz if (n // nz) % 16 == 0 else n
        share = cut != n
        piece = lambda z: rows_at(start + (z * cut if share else 0), cut)
        to_z = [
            remote(buf.at[piece(z_at(k))], recv_z.at[k - 1, :cut], base + k, dev_z(k))
            for k in range(1, nz)
        ]
        own = piece(zi)
        back_z = [
            remote(res.at[own], res.at[own], base + nz - 1 + k, dev_z(k)) for k in range(1, nz)
        ] if share else []

        def part_sum(j):
            for copy in to[j]:
                copy.wait_recv()
            for landing in recvs[j]:
                add_rows(buf, spans[j][0], landing, spans[j][1])
            if extra is not None:
                extra(spans[j])
            start_all(*(to_z if j + 1 == len(to) else to[j + 1]))

        def sum_z():
            for copy in to_z:
                copy.wait_recv()
            total = buf[own, :].astype(F32)
            for k in range(1, nz):
                total = total + recv_z[k - 1, :cut].astype(F32)
            res[own, :] = total.astype(BF16)
            start_all(*back_z)

        handed = [back_z] + back[::-1]
        follow = back[::-1] + [[out]]
        first = [functools.partial(start_all, *to[0])] if starts else []
        chain(
            name, *first, *[functools.partial(part_sum, j) for j in range(len(to))], sum_z,
            *[then(a, *b) for a, b in zip(handed, follow)],
        )
        for group in to + [to_z, back_z] + back:
            last_sends.extend(group)
        outs.append(out)
        return to[0]

    f_base = sems(5)
    f_c0 = remote(r.ct.at[0], r.fc.at[0], f_base, dev_core)
    f_c1 = remote(r.ct.at[2], r.fc.at[1], f_base + 1, dev_core)
    f_part = rows_at(xbit * (D // 2), D // 2)
    f_other = rows_at((1 - xbit) * (D // 2), D // 2)
    f_y = remote(r.ct.at[1, 0], r.fy.at[0], f_base + 2, dev_y)
    f_x = remote(r.ct.at[1, 1, f_other], r.fy.at[1, D // 2 :], f_base + 3, dev_x)
    f_xy = remote(r.ct.at[1, 1, f_part], r.fy.at[1, : D // 2], f_base + 4, dev_y)
    f_outs = [pltpu.make_async_copy(r.fo.at[g], r.fo_out.at[g], r.ls.at[3 + g]) for g in range(2)]
    last_sends, outs = [f_y, f_x, f_xy], []

    def across_up():
        f_y.wait_recv()
        add_rows(r.ct.at[3, 0], 0, r.fy.at[0], D)
        start_all(*f0)

    def plane_down():
        f_x.wait_recv()
        add_rows(r.ct.at[1, 1], xbit * (D // 2), r.fy.at[1, D // 2 :], D // 2)
        f_xy.start()

    def across_down(span):
        f_xy.wait_recv()
        add_rows(r.ct.at[3, 1], span[0], r.fy.at[1, : D // 2], span[1])

    f0 = sum_chain(
        FFN_UP, r.ct.at[3, 0], r.fo.at[0], ["x"], [[r.fx.at[0]]], r.fz.at[0], f_outs[0], False
    )
    f1 = sum_chain(
        FFN_DOWN, r.ct.at[3, 1], r.fo.at[1], ["x"], [[r.fx.at[1]]], r.fz.at[1], f_outs[1], False, across_down
    )
    steps[FFN_UP].insert(0, across_up)
    chain(FFN_ACROSS, plane_down)

    def ffn(k, s, out):
        def tile(t):
            rows = rows_at(t * T, T)
            for h in range(2):
                lanes = slice(h * (D // 2), (h + 1) * (D // 2))
                up = dot(r.hf[rows, :], r.wu[s, :, lanes])
                grad_act = dot_t(r.go[rows, :], r.wd[s, lanes, :])
                cubic = (GELU_SCALE * GELU_CUBIC) * (up * up)
                tang = jnp.tanh(up * (GELU_SCALE + cubic))
                half_up, half_t = 0.5 * up, 0.5 + 0.5 * tang
                slope = half_t + half_up * (1.0 - tang * tang) * (GELU_SCALE + 3.0 * cubic)
                r.gp[rows, lanes] = (up * half_t).astype(BF16)
                r.gp[rows, slice(D + lanes.start, D + lanes.stop)] = (grad_act * slope).astype(BF16)
            add_acc(t, dot(r.gp[rows, :D], r.wd[s]))
            add_acc(nt + t, dot_t(r.gp[rows, D : 2 * D], r.wu[s]))

        loop(FFN_TILE + k, nt, tile)

        def grads(t):
            rows = rows_at(t * T, T)
            out[0, rows, :] = dot(r.hft[rows, :], r.gp[:, D : 2 * D]).astype(BF16)
            out[1, rows, :] = dot(r.got_t[rows, :], r.gp[:, :D]).astype(BF16)

        loop(FFN_GRADS + k, D // T, grads)

    ffn(0, tp_far, r.ct.at[0])
    f_c0.start()
    ffn(1, tp_y, r.ct.at[1])
    f_c0.wait_recv()
    add_rows(r.ct.at[1, 1], 0, r.fc.at[0, 1], D)
    f_x.start()
    add_rows(r.ct.at[1, 0], 0, r.fc.at[0, 0], D)
    f_y.start()
    ffn(2, tp_core, r.ct.at[2])
    f_c1.start()
    ffn(3, tp, r.ct.at[3])
    f_c1.wait_recv()
    add_rows(r.ct.at[3, 1], 0, r.fc.at[1, 1], D)
    start_all(*f1)
    add_rows(r.ct.at[3, 0], 0, r.fc.at[1, 0], D)

    ones_row = lax.broadcasted_iota(jnp.int32, (2 * LANES, LANES), 0)
    ones_col = lax.broadcasted_iota(jnp.int32, (2 * LANES, LANES), 1)
    head_ones = (lax.div(lax.rem(ones_row, LANES), 64) == lax.div(ones_col, 64)).astype(F32).astype(BF16)
    r.gg[...] = jnp.zeros((2, 8, D), F32)

    def gn_at(c):
        return rows_at(lax.rem(c, 2) * T, T), pl.ds(pl.multiple_of(lax.div(c, 2) * T, T), T)

    def gn_of(p, c):
        at, wide_at = gn_at(c)
        return r.wd[p, at, wide_at]

    def fold(v):
        return jnp.sum(v.reshape(T // 8, 8, D), axis=0)

    for copy in w_sends:
        copy.wait_send()

    def back_middle(t):
        rows = rows_at(t * T, T)
        r.hf[rows, :] = acc(t).astype(BF16)
        res = r.res[rows, :]
        mean = jnp.mean(res, axis=-1, keepdims=True)
        cen = res - mean
        inv = lax.rsqrt(jnp.mean(cen * cen, axis=-1, keepdims=True) + NORM_EPS)
        n = cen * inv
        gh = acc(nt + t)
        r.gg[0] += fold(gh * n)
        sc = gh * r.gf[...]
        centre = jnp.mean(sc, axis=-1, keepdims=True)
        inner = jnp.mean(sc * n, axis=-1, keepdims=True)
        gres = r.go[rows, :].astype(F32) + inv * (sc - centre - n * inner)
        r.res[rows, :] = gres
        gattn = gres.astype(BF16)
        r.gp[rows, 2 * D :] = gattn
        gmi = dot_t(gattn, r.wo[...]) * r.inv[rows, :]
        w = gmi * r.mix[rows, :].astype(F32) * (-1.0)
        hi = w.astype(BF16)
        lo = (w - hi.astype(F32)).astype(BF16)
        gnum = gmi.astype(BF16)
        for p in range(npair):
            lanes = slice(p * LANES, (p + 1) * LANES)
            gden = dot(cat([hi[:, lanes], lo[:, lanes]], 1), head_ones).astype(BF16)
            at, wide_at = gn_at(t)
            r.wd[p, at, wide_at] = cat([gnum[:, lanes], gden * jnp.asarray(1.0 / 64.0, BF16)], 1)

    loop(BACK_MIDDLE, nt, back_middle)
    out_copy = pltpu.make_async_copy(r.hf, r.out, r.ls.at[13])
    out_copy.start()

    bpack, steps[STATE_GRADS], bcollect = state_exchange(1, r.own, r.bgot)

    def state_back(i):
        p, c = lax.div(i, nt), nt - 1 - lax.rem(i, nt)
        rows = rows_at(c * T, T)

        @pl.when(c == nt - 1)
        def _():
            r.sl[p * (nt + 1) + nt] = jnp.zeros((M, M), F32)

        gain = merge(dot_c(gn_of(p, c) * twice(r.use[rows, :]), r.phiq[p, rows, :]))
        state = r.sc[c] * r.sl[p * (nt + 1) + c + 1] + gain
        r.sl[p * (nt + 1) + c] = state

    bleaves = (lambda i: lax.rem(i, nt) == nt - 1), (lambda i: bpack(lax.div(i, nt), 0))

    loop(STATE_BACK, npair * nt, state_back, [bleaves])

    half = D // 2
    parts = [
        (SUM_O, 0, 0, 0, D), (SUM_Q, 1, 1, 0, D - LANES), (SUM_Q3, 2, 1, D - LANES, LANES)
    ]
    parts = parts + [(SUM_K + p, 2, 2 + p // 2, (p % 2) * half, half) for p in range(npair)]
    for i, (name, kind, g, lane, n) in enumerate(parts):
        lanes = slice(lane, lane + n)
        core_land = r.fc.at[0, g, :half, lanes] if g < 2 else r.fc.at[0, g - 2, half:, lanes]
        stages = STAGES[kind]
        recvs, at = [[core_land]], 0
        rows = D // 2
        for axes in stages[1:]:
            rows = rows // 2 ** len(axes)
            recvs.append([r.land.at[g, pl.ds(at + k * rows, rows), lanes] for k in range(2 ** len(axes) - 1)])
            at = at + rows * (2 ** len(axes) - 1)
        rz = r.land_z.at[g, :, :, lanes]
        source = r.ct.at[0 if g < 2 else 2, g % 2, :, lanes]
        sum_chain(
            name, source, r.wu.at[g, :, lanes], stages, recvs, rz,
            pltpu.make_async_copy(r.wu.at[g, :, lanes], r.grads.at[g, :, lanes], r.ls.at[5 + i]),
        )

    f_c0.wait_send()
    f_c1.wait_send()
    def out_grads():
        for t in range(D // T):
            rows = slice(t * T, (t + 1) * T)
            r.ct[0, 0, rows, :] = dot_c(r.mix[:, rows], r.gp[:, 2 * D :]).astype(BF16)

    once(OUT_GRADS, out_grads)

    def back_query(i):
        p, c = lax.div(i, nt), lax.rem(i, nt)
        rows = rows_at(c * T, T)
        vals, gn = r.vp[p, rows, :], gn_of(p, c)
        phi_q, phi_k = r.phiq[p, rows, :], r.phik[p, rows, :]
        g = dot_t(gn, cat([vals * low, vals * high], 0)).astype(BF16) * twice(r.mask[c])
        used = gn * twice(r.use[rows, :])
        gphi = cat([dot(g[:, :M], phi_k[:, :M]), dot(g[:, M:], phi_k[:, M:])], 1)
        gphi = gphi + dot(used, r.st[i])
        t = (gphi * phi_q.astype(F32)).astype(BF16)
        o = dot_t(t, r.bb[p, : 2 * LANES])
        gq = c4 * o[:, :LANES] - r.q[p, rows, :].astype(F32) * (o[:, LANES:] * 0.125)
        r.gp[rows, pl.ds(pl.multiple_of(p * LANES, LANES), LANES)] = gq.astype(BF16)

    loop(BACK_QUERY, (npair - 1) * nt, back_query)
    def query_grads(lanes):
        for t in range(D // T):
            rows = slice(t * T, (t + 1) * T)
            r.ct[0, 1, rows, lanes] = dot(r.ht[rows, :], r.gp[:, lanes]).astype(BF16)

    once(QUERY_GRADS, lambda: query_grads(slice(0, D - LANES)))

    def pair_grads(i):
        p = lax.div(i, nt)
        kv = cat(
            [r.gp[:, pl.ds(pl.multiple_of(o * D + p * LANES, LANES), LANES)] for o in (1, 2)], 1
        )
        wide_at = pl.ds(pl.multiple_of(lax.rem(p, 2) * half, half), half)
        for t in range(D // T):
            rows = slice(t * T, (t + 1) * T)
            r.ct[2, lax.div(p, 2), rows, wide_at] = dot(r.ht[rows, :], kv).astype(BF16)

    def back_key(i):
        p, c = lax.div(i, nt), lax.rem(i, nt)
        rows = rows_at(c * T, T)
        dstate = split((r.sl[p * (nt + 1) + c + 1] + r.sc[2 * nt + c] * r.tin[p]).astype(BF16))
        vals, gn = r.vp[p, rows, :], gn_of(p, c)
        phi_q, phi_k = r.phiq[p, rows, :], r.phik[p, rows, :]
        mask = twice(r.maskt[c])
        gt = cat([dot_t(vals * low, gn), dot_t(vals * high, gn)], 1).astype(BF16) * mask
        st = cat([dot_t(phi_k[:, :M], phi_q[:, :M]), dot_t(phi_k[:, M:], phi_q[:, M:])], 1)
        st = st.astype(BF16) * mask
        tail = r.tail[rows, :]
        left = vals * twice(tail)
        gphi = cat(
            [
                dot(cat([gt[:, m], left], 1), cat([phi_q[:, m], dstate[:, m]], 0))
                for m in (slice(0, M), slice(M, 2 * M))
            ],
            1,
        )
        gnum = gn[:, :LANES]
        gv = dot(st, cat([gnum * low[:, :LANES], gnum * high[:, :LANES]], 0))
        gv = gv + tail.astype(F32) * dot_t(phi_k, dstate[:LANES])
        t = (gphi * phi_k.astype(F32)).astype(BF16)
        o = dot_t(t, r.bb[p, : 2 * LANES])
        gk = c4 * o[:, :LANES] - r.k[p, rows, :].astype(F32) * (o[:, LANES:] * 0.125)
        r.gp[rows, pl.ds(pl.multiple_of(D + p * LANES, LANES), LANES)] = gk.astype(BF16)
        r.gp[rows, pl.ds(pl.multiple_of(2 * D + p * LANES, LANES), LANES)] = gv.astype(BF16)

    loop(BACK_KEY, npair * nt, back_key, [((lambda i: lax.rem(i, nt) == nt - 1), pair_grads)], bcollect)

    loop(LAST_QUERY, nt, lambda c: back_query((npair - 1) * nt + c))
    once(LAST_GRADS, lambda: query_grads(slice(D - LANES, D)))

    def back_first(t):
        rows = rows_at(t * T, T)
        gh = dot_t(r.gp[rows, :D], r.wq[...])
        gh = gh + dot_t(r.gp[rows, D : 2 * D], r.wk[...])
        gh = gh + dot_t(r.gp[rows, 2 * D :], r.wv[...])
        x = r.tok[rows, :].astype(F32)
        mean = jnp.mean(x, axis=-1, keepdims=True)
        cen = x - mean
        inv = lax.rsqrt(jnp.mean(cen * cen, axis=-1, keepdims=True) + NORM_EPS)
        n = cen * inv
        r.gg[1] += fold(gh * n)
        sc = gh * r.ga[...]
        centre = jnp.mean(sc, axis=-1, keepdims=True)
        inner = jnp.mean(sc * n, axis=-1, keepdims=True)
        r.res[rows, :] += inv * (sc - centre - n * inner)

    loop(BACK_FIRST, nt, back_first)
    gt_copy = pltpu.make_async_copy(r.res, r.gt, r.ls.at[3 + 9])
    gt_copy.start()

    g_base = sems(3 + ndp - 1)
    sums = [jnp.sum(r.gg[k], axis=0, keepdims=True) for k in range(2)]
    r.g1[...] = cat([v[:, j : j + LANES] for v in sums for j in range(0, D, LANES)], 0)
    g_tp = [remote(r.g1, r.gr.at[k - 1], g_base + k - 1, (dp, lax.rem(tp + k, 4))) for k in (1, 2, 3)]
    g_dp = [
        remote(r.g2, r.gr.at[2 + k], g_base + 2 + k, (lax.rem(dp + k, ndp), tp)) for k in range(1, ndp)
    ]
    start_all(*g_tp)

    def gains_tp():
        for copy in g_tp:
            copy.wait_recv()
        r.g2[...] = r.g1[...] + r.gr[0] + r.gr[1] + r.gr[2]
        start_all(*g_dp)

    def gains_dp():
        total = r.g2[...]
        for k in range(1, ndp):
            g_dp[k - 1].wait_recv()
            total = total + r.gr[2 + k]
        r.gout[...] = total

    chain(GAINS, gains_tp, gains_dp)
    advance(TAIL, 0)
    assert not plan and not any(steps.values())

    for copy in seg_copies + last_sends + g_tp + g_dp:
        copy.wait_send()
    for copy in outs + [out_copy, gt_copy]:
        copy.wait()
    assert used[0] <= r.ss.shape[0]


def layer(tokens, segment_ids, grad_out, w_query, w_key, w_value, w_out, w_up, w_down, gain_attn,
          gain_ffn, feature_basis):
    _, L, D = tokens.shape
    H, DH, M = feature_basis.shape
    F = w_up.shape[1]
    npair, nt = H // 2, L // T
    ndp = lax.axis_size("dp")
    nz = ndp // 2
    assert lax.axis_size("tp") == 4 and F == D and DH == 64 and M == T

    vmem, hbm = pl.BlockSpec(memory_space=pltpu.VMEM), pl.BlockSpec(memory_space=pl.ANY)
    ins = {
        "seg": (segment_ids, vmem),
        "tok_in": (tokens[0], hbm),
        "go_in": (grad_out[0], hbm),
        "wq_in": (w_query, hbm),
        "wk_in": (w_key, hbm),
        "wv_in": (w_value, hbm),
        "wo_in": (w_out, hbm),
        "wup": (w_up, hbm),
        "wdn": (w_down, hbm),
        "ga": (gain_attn[None], vmem),
        "gf": (gain_ffn[None], vmem),
        "basis_in": (feature_basis, hbm),
    }
    outs = {
        "out": ((L, D), BF16, hbm),
        "gt": ((L, D), F32, hbm),
        "fo_out": ((2, D, F), BF16, hbm),
        "grads": ((4, D, D), BF16, hbm),
        "gout": ((8, LANES), F32, vmem),
    }

    scratch = {
        "tok": ((L, D), BF16),
        "wk": ((D, D), BF16),
        "wv": ((D, D), BF16),
        "wq": ((D, D), BF16),
        "wo": ((D, D), BF16),
        "go": ((L, D), BF16),
        "sg": ((4, 1, L), jnp.int32),
        "wu": ((4, D, F), BF16),
        "wd": ((4, F, D), BF16),
        "bb": ((npair, 3 * LANES, 2 * M), BF16),
        "ht": ((D, L), BF16),
        "q": ((npair, L, LANES), BF16),
        "k": ((npair, L, LANES), BF16),
        "vp": ((npair, L, 2 * LANES), BF16),
        "sc": ((3 * nt + 8, 1, M), F32),
        "use": ((L, LANES), BF16),
        "tail": ((L, LANES), BF16),
        "mask": ((nt, T, M), BF16),
        "maskt": ((nt, T, M), BF16),
        "phik": ((npair, L, 2 * M), BF16),
        "phiq": ((npair, L, 2 * M), BF16),
        "sl": ((npair * (nt + 1), M, M), F32),
        "own": ((npair, 144, M), BF16),
        "got": ((4, npair, 144, M), BF16),
        "bgot": ((4, npair, 144, M), BF16),
        "tin": ((npair, M, M), F32),
        "st": ((npair * nt, M, 2 * M), BF16),
        "inv": ((L, D), F32),
        "mix": ((L, D), BF16),
        "res": ((L, D), F32),
        "hf": ((L, D), BF16),
        "hft": ((D, L), BF16),
        "got_t": ((D, L), BF16),
        "ct": ((4, 2, D, F), BF16),
        "fc": ((2, 2, D, F), BF16),
        "land": ((4, 192, D), BF16),
        "land_z": ((4, nz - 1, D // 8, D), BF16),
        "fy": ((2, D, F), BF16),
        "fx": ((2, D // 2, F), BF16),
        "fz": ((2, nz - 1, D // 2 // nz, F), BF16),
        "fo": ((2, D, F), BF16),
        "gg": ((2, 8, D), F32),
        "gp": ((L, 3 * D), BF16),
        "g1": ((8, LANES), F32),
        "g2": ((8, LANES), F32),
        "gr": ((3 + ndp - 1, 8, LANES), F32),
    }
    n_sems = 40 + 6 * npair + ndp + (4 + npair) * (10 + 2 * (nz - 1)) + 5 * (nz - 1)
    names = list(ins) + list(outs) + list(scratch) + ["ls", "ss", "rs"]
    res = pl.pallas_call(
        functools.partial(layer_kernel, nz, names),
        out_shape=[jax.ShapeDtypeStruct(s, d) for s, d, _ in outs.values()],
        in_specs=[spec for _, spec in ins.values()],
        out_specs=[spec for _, _, spec in outs.values()],
        scratch_shapes=[pltpu.VMEM(s, d) for s, d in scratch.values()]
        + [
            pltpu.SemaphoreType.DMA((28,)),
            pltpu.SemaphoreType.DMA((n_sems,)),
            pltpu.SemaphoreType.DMA((n_sems,)),
        ],
        name="layer",
        compiler_params=pltpu.CompilerParams(
            collective_id=0, has_side_effects=True, vmem_limit_bytes=67043328
        ),
    )(*[a for a, _ in ins.values()])
    return hand_out(*res)


def hand_out_kernel(out, gt, up, down, grads, gains, *refs):
    o_out, o_gt, o_query, o_key, o_value, o_proj, o_up, o_down, o_attn, o_ffn = refs
    o_out[0] = out[...]
    o_gt[0] = gt[...]
    o_up[...] = up[0].astype(F32)
    o_down[...] = down[0].astype(F32).T
    o_proj[...] = grads[0].astype(F32)
    o_query[...] = grads[1].astype(F32)
    for p in range(grads.shape[2] // LANES):
        lanes = slice(p * LANES, (p + 1) * LANES)
        at = (p % 2) * 2 * LANES
        o_key[:, lanes] = grads[2 + p // 2, :, at : at + LANES].astype(F32)
        o_value[:, lanes] = grads[2 + p // 2, :, at + LANES : at + 2 * LANES].astype(F32)
    for j in range(4):
        lanes = slice(j * LANES, (j + 1) * LANES)
        o_ffn[:, lanes] = gains[j : j + 1, :]
        o_attn[:, lanes] = gains[4 + j : 5 + j, :]


def hand_out(out, gt, fo, grads, gains):
    (L, D), steps = out.shape, 2
    lr, dr = L // steps, D // steps
    tall = pl.BlockSpec((1, lr, D), lambda i: (0, i, 0))
    flat = pl.BlockSpec((dr, D), lambda i: (i, 0))
    row = pl.BlockSpec((1, D), lambda i: (0, 0))
    f32 = lambda *shape: jax.ShapeDtypeStruct(shape, F32)
    res = pl.pallas_call(
        hand_out_kernel,
        grid=(steps,),
        in_specs=[
            pl.BlockSpec((lr, D), lambda i: (i, 0)),
            pl.BlockSpec((lr, D), lambda i: (i, 0)),
            pl.BlockSpec((1, dr, D), lambda i: (0, i, 0)),
            pl.BlockSpec((1, D, dr), lambda i: (1, 0, i)),
            pl.BlockSpec((4, dr, D), lambda i: (0, i, 0)),
            pl.BlockSpec((8, LANES), lambda i: (0, 0)),
        ],
        out_specs=[tall, tall, flat, flat, flat, flat, flat, flat, row, row],
        out_shape=[jax.ShapeDtypeStruct((1, L, D), BF16), f32(1, L, D)]
        + [f32(D, D)] * 6 + [f32(1, D)] * 2,
        name="hand_out", compiler_params=pltpu.CompilerParams(vmem_limit_bytes=60000000),
    )(out, gt, fo, fo, grads, gains)
    return (*res[:8], res[8][0], res[9][0])


def solution(mesh):
    whole = P()
    in_specs = (
        P("dp", "tp", None), P("dp", "tp"), P("dp", "tp", None), whole, whole, whole, whole,
        P(None, "tp"), P("tp", None), whole, whole, whole,
    )
    out_specs = (
        P("dp", "tp", None), P("dp", "tp", None), whole, whole, whole, whole,
        P(None, "tp"), P("tp", None), whole, whole,
    )
    return jax.shard_map(layer, mesh=mesh, in_specs=in_specs, out_specs=out_specs, check_vma=False)
```

```python
import functools
import math
from types import SimpleNamespace

import jax
import jax.numpy as jnp
from jax import lax
from jax.experimental import pallas as pl
from jax.experimental.pallas import tpu as pltpu
from jax.sharding import PartitionSpec as P

MESH = pl.DeviceIdType.MESH
F32 = jnp.float32
BF16 = jnp.bfloat16
NORM_EPS = 1e-05
GELU_SCALE = 0.7978845608028654
GELU_CUBIC = 0.044715
LANES = 128
(
    PROJECT, BASIS_BLOCKS, KEY_SIDE, PROJECT_QUERY, QUERY_SIDE, ALL_MASKS,
    ATTEND, MIDDLE, TRANSPOSES, BACK_MIDDLE, STATE_BACK, OUT_GRADS,
    BACK_QUERY, QUERY_GRADS, BACK_KEY, LAST_QUERY, LAST_GRADS, BACK_FIRST,
    TAIL,
) = range(19)
FFN_TILE, FFN_GRADS = 19, 23
(
    W_UP, W_DOWN, STATES, STATE_GRADS, FFN_ACROSS,
    FFN_UP, FFN_DOWN, SUM_O, SUM_Q, SUM_Q3, GAINS,
    SUM_K,
) = range(12)
PLAN = (
    (KEY_SIDE, 3, W_DOWN),
    (PROJECT_QUERY, 0, W_UP),
    (QUERY_SIDE, 3, STATES),
    (QUERY_SIDE, 11, STATES),
    (QUERY_SIDE, 15, W_DOWN),
    (QUERY_SIDE, 15, STATES),
    (ATTEND, 3, STATES),
    (MIDDLE, 1, W_UP),
    (MIDDLE, 3, W_DOWN),
    (FFN_TILE + 3, 3, FFN_ACROSS),
    (BACK_MIDDLE, 3, FFN_UP),
    (OUT_GRADS, 0, SUM_O),
    (OUT_GRADS, 0, FFN_DOWN),
    (BACK_QUERY, 3, STATE_GRADS),
    (BACK_QUERY, 3, SUM_O),
    (BACK_QUERY, 7, STATE_GRADS),
    (BACK_QUERY, 11, STATE_GRADS),
    (BACK_QUERY, 11, FFN_UP),
    (BACK_QUERY, 11, STATE_GRADS),
    (QUERY_GRADS, 0, SUM_Q),
    (BACK_KEY, 3, SUM_O),
    (BACK_KEY, 3, SUM_K),
    (BACK_KEY, 3, FFN_DOWN),
    (BACK_KEY, 3, SUM_Q),
    (BACK_KEY, 5, SUM_K),
    (BACK_KEY, 7, SUM_O),
    (BACK_KEY, 7, SUM_K + 1),
    (BACK_KEY, 9, FFN_UP),
    (BACK_KEY, 9, SUM_K + 1),
    (BACK_KEY, 11, SUM_K + 2),
    (BACK_KEY, 11, SUM_Q),
    (BACK_KEY, 13, SUM_K),
    (BACK_KEY, 13, SUM_K + 2),
    (BACK_KEY, 15, FFN_DOWN),
    (BACK_KEY, 15, SUM_K + 3),
    (BACK_KEY, 15, SUM_K + 1),
    (BACK_KEY, 15, SUM_Q),
    (LAST_QUERY, 3, SUM_O),
    (LAST_QUERY, 3, SUM_K + 3),
    (LAST_GRADS, 0, SUM_K + 2),
    (LAST_GRADS, 0, SUM_Q3),
    (BACK_FIRST, 1, SUM_Q3),
    (TAIL, 0, FFN_UP),
    (TAIL, 0, SUM_K),
    (TAIL, 0, FFN_DOWN),
    (TAIL, 0, SUM_K + 1),
    (TAIL, 0, GAINS),
    (TAIL, 0, SUM_Q),
    (TAIL, 0, SUM_K + 3),
    (TAIL, 0, SUM_O),
    (TAIL, 0, SUM_Q3),
    (TAIL, 0, SUM_K + 2),
    (TAIL, 0, SUM_K),
    (TAIL, 0, SUM_K + 1),
    (TAIL, 0, GAINS),
    (TAIL, 0, FFN_UP),
    (TAIL, 0, SUM_Q),
    (TAIL, 0, SUM_K + 3),
    (TAIL, 0, SUM_O),
    (TAIL, 0, SUM_Q3),
    (TAIL, 0, SUM_K + 2),
    (TAIL, 0, SUM_Q),
    (TAIL, 0, SUM_K),
    (TAIL, 0, SUM_K),
    (TAIL, 0, SUM_K + 1),
    (TAIL, 0, SUM_K + 3),
    (TAIL, 0, SUM_Q3),
    (TAIL, 0, SUM_O),
    (TAIL, 0, SUM_K + 1),
    (TAIL, 0, SUM_Q),
    (TAIL, 0, SUM_O),
    (TAIL, 0, SUM_K + 2),
    (TAIL, 0, SUM_Q),
    (TAIL, 0, SUM_K + 2),
    (TAIL, 0, SUM_K + 3),
    (TAIL, 0, SUM_Q3),
    (TAIL, 0, SUM_K + 3),
    (TAIL, 0, SUM_Q3),
)
UNROLL = {
    PROJECT: 2,
    MIDDLE: 2,
    BACK_MIDDLE: 2,
    BACK_FIRST: 2,
    BACK_KEY: 2,
    FFN_TILE: 2,
    KEY_SIDE: 4,
    QUERY_SIDE: 4,
    ATTEND: 4,
    STATE_BACK: 4,
    BACK_QUERY: 4,
    LAST_QUERY: 4,
}
STAGES = (("c", "y", "x"), ("c", "x", "y"), ("c", "xy"))
T = 256


def dot(a, b):
    return jnp.dot(a, b, preferred_element_type=F32)


def dot_t(a, b):
    return lax.dot_general(a, b, (((1,), (1,)), ((), ())), preferred_element_type=F32)


def dot_c(a, b):
    return lax.dot_general(a, b, (((0,), (0,)), ((), ())), preferred_element_type=F32)


def rows_at(start, size):
    return pl.ds(pl.multiple_of(start, 16), size)


def cat(parts, axis):
    return jnp.concatenate(parts, axis=axis)


def lane_groups():
    lane = lax.broadcasted_iota(jnp.int32, (1, 2 * LANES), 1)
    first = lax.rem(lane, LANES) < 64
    one = jnp.where(first, 1.0, 0.0)
    return one.astype(BF16), (1.0 - one).astype(BF16)


def layer_kernel(nz, names, *refs):
    r = SimpleNamespace(**dict(zip(names, refs)))
    L, D = r.tok.shape
    nt = L // T
    npair = r.basis_in.shape[0] // 2
    M = r.basis_in.shape[2]
    c4 = 64.0**-0.25
    exp_scale = c4 * math.log2(math.e)

    dp, tp = lax.axis_index("dp"), lax.axis_index("tp")
    ndp = 2 * nz
    core, ybit = lax.rem(tp, 2), lax.div(tp, 2)
    xbit, zi = lax.rem(dp, 2), lax.div(dp, 2)
    tp_core, tp_y, tp_far = tp + 1 - 2 * core, lax.rem(tp + 2, 4), 3 - tp
    dev_core, dev_y, dev_far = (dp, tp_core), (dp, tp_y), (dp, tp_far)
    dev_x = (dp + 1 - 2 * xbit, tp)

    def z_at(k):
        return lax.rem(zi + k, nz)

    def dev_z(k):
        return (z_at(k) * 2 + xbit, tp)

    plan, steps = {}, {}
    for place, i, chunk in PLAN:
        plan.setdefault((place, i), []).append(chunk)

    def advance(place, i):
        for chunk in plan.pop((place, i), ()):
            steps[chunk].pop(0)()

    def loop(name, n, body, tasks=(), before=None):
        u = UNROLL.get(FFN_TILE if FFN_TILE <= name < FFN_GRADS else name, 1)

        def step(i, _):
            if before is not None:
                pl.when(lax.rem(i * u, nt) == 0)(lambda: before(lax.div(i * u, nt)))
            for k in range(u):
                body(i * u + k)
            for when, task in tasks:
                pl.when(when(i * u + u - 1))(functools.partial(task, i * u + u - 1))
            for k in range(n):
                if (name, k) in plan:
                    pl.when(i == k // u)(functools.partial(advance, name, k))
            return 0

        lax.fori_loop(0, n // u, step, 0)

    def once(name, body):
        body()
        advance(name, 0)

    used = [0]

    def sems(n):
        first = used[0]
        used[0] += n
        return first

    def remote(src, dst, idx, dev):
        return pltpu.make_async_remote_copy(
            src_ref=src, dst_ref=dst, send_sem=r.ss.at[idx], recv_sem=r.rs.at[idx],
            device_id=dev, device_id_type=MESH,
        )

    loads = {
        name: pltpu.make_async_copy(getattr(r, name + "_in"), getattr(r, name), r.ls.at[14 + k])
        for k, name in enumerate(("tok", "wk", "wv", "wq", "wo", "go"))
    }
    own_up = pltpu.make_async_copy(r.wup, r.wu.at[tp], r.ls.at[0])
    own_down = pltpu.make_async_copy(r.wdn, r.wd.at[tp], r.ls.at[1])
    own_seg = pltpu.make_async_copy(r.seg, r.sg.at[tp], r.ls.at[2])
    basis_copies = [
        pltpu.make_async_copy(
            r.basis_in.at[h], r.bb.at[h // 2, pl.ds((h % 2) * 64, 64), pl.ds((h % 2) * M, M)], r.ls.at[20 + h]
        )
        for h in range(2 * npair)
    ]
    own_seg.start()
    for copy in list(loads.values()) + basis_copies:
        copy.start()
    own_up.start()
    own_down.start()

    barrier = pltpu.get_barrier_semaphore()
    for k in (1, 2, 3):
        pl.semaphore_signal(barrier, inc=1, device_id=(dp, lax.rem(tp + k, 4)), device_id_type=MESH)
    for k in range(1, ndp):
        pl.semaphore_signal(barrier, inc=1, device_id=(lax.rem(dp + k, ndp), tp), device_id_type=MESH)


    seg_base = sems(3)
    seg_copies = [
        remote(r.seg, r.sg.at[tp], seg_base + k - 1, (dp, lax.rem(tp + k, 4))) for k in (1, 2, 3)
    ]

    up_base, down_base = sems(5), sems(4 + nz - 1)
    pr = r.wdn.shape[0] // ndp
    up_core = remote(r.wup, r.wu.at[tp], up_base, dev_core)
    hd = r.wup.shape[0] // 2
    up_y = [
        remote(r.wup.at[pl.ds(g * hd, hd)], r.wu.at[tp, pl.ds(g * hd, hd)], up_base + 1 + g, dev_y)
        for g in range(2)
    ]
    up_on = [
        remote(r.wu.at[tp_y, pl.ds(g * hd, hd)], r.wu.at[tp_y, pl.ds(g * hd, hd)], up_base + 3 + g, dev_core)
        for g in range(2)
    ]
    down_core = remote(r.wdn, r.wd.at[tp], down_base, dev_core)
    down_piece = rows_at((xbit * nz + zi) * pr, pr)
    down_plane = rows_at(xbit * nz * pr, nz * pr)
    down_y = remote(r.wdn.at[down_piece], r.wd.at[tp, down_piece], down_base + 1, dev_y)
    down_z = [
        remote(r.wd.at[tp_y, down_piece], r.wd.at[tp_y, down_piece], down_base + 3 + k, dev_z(k))
        for k in range(1, nz)
    ]
    down_x = remote(r.wd.at[tp_y, down_plane], r.wd.at[tp_y, down_plane], down_base + 2, dev_x)
    down_on = remote(r.wd.at[tp_y], r.wd.at[tp_y], down_base + 3, dev_core)
    w_sends = [up_core, down_core, down_y, down_x, down_on] + up_y + up_on + down_z

    def start_all(*copies):
        for copy in copies:
            copy.start()

    def chain(name, *tasks):
        steps[name] = list(tasks)

    def then(waits, *starts):
        def task():
            for copy in waits:
                copy.wait_recv()
            start_all(*starts)

        return task

    chain(W_UP, then(up_y[:1], up_on[0]), then(up_y[1:], up_on[1]))
    chain(W_DOWN, then([down_y], *down_z), then(down_z, down_x), then([down_x], down_on))

    def enter():
        pl.semaphore_wait(barrier, 3 + ndp - 1)
        start_all(*seg_copies, down_y, up_y[0], up_core, down_core)

    enter()

    def basis_blocks():
        zero, one = jnp.zeros((64, M), BF16), jnp.ones((64, M), BF16)
        for p in range(npair):
            for h in range(2):
                lanes = slice(h * M, (h + 1) * M)
                r.bb[p, (1 - h) * 64 : (2 - h) * 64, lanes] = zero
                r.bb[p, LANES:, lanes] = cat([one, zero, one, zero] if h == 0 else [zero, one, zero, one], 0)
        for copy in basis_copies:
            copy.wait()

    once(BASIS_BLOCKS, basis_blocks)
    low, high = lane_groups()

    def project(t):
        rows = rows_at(t * T, T)
        x = r.tok[rows, :].astype(F32)
        mean = jnp.mean(x, axis=-1, keepdims=True)
        cen = x - mean
        inv = lax.rsqrt(jnp.mean(cen * cen, axis=-1, keepdims=True) + NORM_EPS)
        hid = ((cen * inv) * r.ga[...]).astype(BF16)
        r.hf[rows, :] = hid
        k = dot(hid, r.wk[...]).astype(BF16)
        v = dot(hid, r.wv[...]).astype(BF16)
        for p in range(npair):
            lanes = slice(p * LANES, (p + 1) * LANES)
            r.k[p, rows, :] = k[:, lanes]
            r.vp[p, rows, :LANES] = v[:, lanes]
            r.vp[p, rows, LANES:] = jnp.ones((T, LANES), BF16)

    loads["tok"].wait()
    loads["wk"].wait()
    loads["wv"].wait()
    loop(PROJECT, nt, project)

    own_seg.wait()
    for copy in seg_copies:
        copy.wait_recv()
    row_max, row_min = [], []
    for j in range(4):
        ids = r.sg[j].astype(F32)
        row_max.append(jnp.max(ids, axis=1, keepdims=True))
        row_min.append(jnp.min(ids, axis=1, keepdims=True))
    in_seg = jnp.full((1, 1), -1.0, F32)
    for j in range(4):
        in_seg = jnp.maximum(in_seg, jnp.where(j < tp, row_max[j], -1.0))
    mine = r.seg[...].astype(F32)
    ends = [jnp.max(mine[:, c * T : (c + 1) * T], axis=1, keepdims=True) for c in range(nt)]
    befores = [in_seg] + ends[:-1]
    keeps = [(befores[c] == ends[c]).astype(F32) for c in range(nt)]
    wide = lambda v: jnp.broadcast_to(v, (1, M))
    flag = jnp.ones((1, 1), F32)
    for c in range(nt):
        r.sc[c] = wide(keeps[c])
        r.sc[nt + c] = wide(flag)
        flag = flag * keeps[c]
    flag = jnp.ones((1, 1), F32)
    for c in reversed(range(nt)):
        r.sc[2 * nt + c] = wide(flag)
        flag = flag * keeps[c]
    for j in range(4):
        r.sc[3 * nt + j] = wide(jnp.where(j < tp, (row_max[j] == in_seg).astype(F32), 0.0))
        r.sc[3 * nt + 4 + j] = wide(jnp.where(j > tp, (row_min[j] == ends[-1]).astype(F32), 0.0))
    row_id = lax.broadcasted_iota(jnp.int32, (T, T), 0)
    col_id = lax.broadcasted_iota(jnp.int32, (T, T), 1)
    for c in range(nt):
        along = mine[:, c * T : (c + 1) * T]
        down = jnp.broadcast_to(along, (LANES, T)).T
        rows = slice(c * T, (c + 1) * T)
        use = (down == befores[c]).astype(F32).astype(BF16)
        tail = (down == ends[c]).astype(F32).astype(BF16)
        r.use[rows, :] = use
        r.tail[rows, :] = tail

    def masks(c):
        along = mine[:, c * T : (c + 1) * T]
        down = jnp.broadcast_to(along, (LANES, T)).T
        same = (cat([down, down], 1) == along).astype(F32)
        mask = (same * (row_id >= col_id).astype(F32)).astype(BF16)
        mask_t = (same * (row_id <= col_id).astype(F32)).astype(BF16)
        r.mask[c] = mask
        r.maskt[c] = mask_t

    def twice(v):
        return cat([v, v], 1)

    def features(u, p):
        wide_u = u.astype(F32)
        square = wide_u * wide_u * (-1.0 / (16.0 * c4))
        hi = square.astype(BF16)
        lo = (square - hi.astype(F32)).astype(BF16)
        expo = dot(cat([u, hi], 1), r.bb[p, : 2 * LANES]) + dot(lo, r.bb[p, 2 * LANES :])
        return jnp.exp2(expo * exp_scale).astype(BF16)

    def merge(u):
        return cat([u[:64, :M], u[64:128, M:], u[128:192, :M], u[192:, M:]], 0)

    def split(s):
        zero = jnp.zeros((64, M), s.dtype)
        first = cat([s[:64], zero, s[128:192], zero], 0)
        second = cat([zero, s[64:128], zero, s[192:]], 0)
        return cat([first, second], 1)

    def state_exchange(i, own, got):
        base = sems(3 * npair)

        def copies(p):
            at = base + p * 3
            return (
                remote(own.at[p], got.at[tp, p], at, dev_core),
                remote(own.at[p], got.at[tp, p], at + 1, dev_y),
                remote(got.at[tp_y, p], got.at[tp_y, p], at + 2, dev_core),
            )

        def pack(p, slot):
            state = r.sl[p * (nt + 1) + slot]
            own[p, :128, :] = state[:128].astype(BF16)
            own[p, 128:, :] = cat([state[128:136], state[192:200]], 0).astype(BF16)
            to_core, to_y, _ = copies(p)
            to_y.start()
            to_core.start()

        def relay(p):
            _, to_y, on = copies(p)
            to_y.wait_recv()
            on.start()

        def collect(p):
            to_core, to_y, on = copies(p)
            to_core.wait_recv()
            on.wait_recv()
            total = jnp.zeros((144, M), F32)
            for slot in (tp_core, tp_y, tp_far):
                total = total + got[slot, p].astype(F32) * r.sc[3 * nt + 4 * i + slot]
            r.tin[p, :128, :] = total[:128]
            r.tin[p, 128:192, :] = jnp.broadcast_to(total[128:129], (64, M))
            r.tin[p, 192:, :] = jnp.broadcast_to(total[136:137], (64, M))
            to_core.wait_send()
            to_y.wait_send()
            on.wait_send()

        return pack, [functools.partial(relay, p) for p in range(npair)], collect

    pack, steps[STATES], collect = state_exchange(0, r.own, r.got)

    def key_side(i):
        p, c = lax.div(i, nt), lax.rem(i, nt)
        rows = rows_at(c * T, T)
        phi = features(r.k[p, rows, :], p)
        r.phik[p, rows, :] = phi
        gain = merge(dot_c(r.vp[p, rows, :] * twice(r.tail[rows, :]), phi))

        @pl.when(c == 0)
        def _():
            r.sl[p * (nt + 1)] = jnp.zeros((M, M), F32)

        state = r.sc[c] * r.sl[p * (nt + 1) + c] + gain
        r.sl[p * (nt + 1) + c + 1] = state

    leaves = (lambda i: lax.rem(i, nt) == nt - 1), (lambda i: pack(lax.div(i, nt), nt))

    loop(KEY_SIDE, npair * nt, key_side, [leaves])

    up_y[1].start()

    def project_query(t):
        rows = rows_at(t * T, T)
        hid = r.hf[rows, :]
        r.ht[:, pl.ds(pl.multiple_of(t * T, LANES), T)] = hid.T
        q = dot(hid, r.wq[...]).astype(BF16)
        for p in range(npair):
            r.q[p, rows, :] = q[:, p * LANES : (p + 1) * LANES]

    loads["wq"].wait()
    loop(PROJECT_QUERY, nt, project_query)

    def query_side(i):
        p, c = lax.div(i, nt), lax.rem(i, nt)
        rows = rows_at(c * T, T)
        r.phiq[p, rows, :] = features(r.q[p, rows, :], p)

    loop(QUERY_SIDE, npair * nt, query_side)

    def all_masks():
        for c in range(nt):
            masks(c)

    once(ALL_MASKS, all_masks)

    def attend(i):
        p, c = lax.div(i, nt), lax.rem(i, nt)
        rows = rows_at(c * T, T)
        state = (r.sl[p * (nt + 1) + c] + r.sc[nt + c] * r.tin[p]).astype(BF16)
        state = split(state)
        r.st[i] = state
        phi_q, phi_k = r.phiq[p, rows, :], r.phik[p, rows, :]
        scores = cat([dot_t(phi_q[:, :M], phi_k[:, :M]), dot_t(phi_q[:, M:], phi_k[:, M:])], 1)
        scores = scores.astype(BF16) * twice(r.mask[c])
        vals = r.vp[p, rows, :]
        both = dot(scores, cat([vals * low, vals * high], 0))
        both = both + twice(r.use[rows, :].astype(F32)) * dot_t(phi_q, state)
        inv = 1.0 / both[:, LANES:]
        lanes = pl.ds(pl.multiple_of(p * LANES, LANES), LANES)
        r.inv[rows, lanes] = inv
        r.mix[rows, lanes] = (both[:, :LANES] * inv).astype(BF16)

    loop(ATTEND, npair * nt, attend, before=collect)

    def acc(t):
        return cat([r.sl[2 * t], r.sl[2 * t + 1]], 1)

    def add_acc(t, v):
        r.sl[2 * t] += v[:, :M]
        r.sl[2 * t + 1] += v[:, M:]

    def middle(t):
        rows = rows_at(t * T, T)
        res = r.tok[rows, :].astype(F32) + dot(r.mix[rows, :], r.wo[...])
        r.res[rows, :] = res
        mean = jnp.mean(res, axis=-1, keepdims=True)
        cen = res - mean
        inv = lax.rsqrt(jnp.mean(cen * cen, axis=-1, keepdims=True) + NORM_EPS)
        r.hf[rows, :] = ((cen * inv) * r.gf[...]).astype(BF16)
        r.sl[2 * t] = res[:, :M]
        r.sl[2 * t + 1] = res[:, M:]
        r.sl[2 * nt + 2 * t] = jnp.zeros((T, M), F32)
        r.sl[2 * nt + 2 * t + 1] = jnp.zeros((T, M), F32)

    loads["wo"].wait()
    loop(MIDDLE, nt, middle)
    loads["go"].wait()
    own_up.wait()
    own_down.wait()
    up_core.wait_recv()
    down_core.wait_recv()
    for copy in up_on:
        copy.wait_recv()
    down_on.wait_recv()
    def transposes():
        for t in range(nt):
            rows = slice(t * T, (t + 1) * T)
            r.hft[:, rows] = r.hf[rows, :].T
            r.got_t[:, rows] = r.go[rows, :].T

    once(TRANSPOSES, transposes)

    def add_rows(dst, start, src, n):
        step = min(n, 128)

        def one(b, _):
            at = rows_at(start + b * step, step)
            dst[at, :] = dst[at, :] + src[rows_at(b * step, step), :]
            return 0

        lax.fori_loop(0, n // step, one, 0)

    bits = {"c": core, "x": xbit, "y": ybit}

    def flips(axes):
        out = [""]
        for axis in axes:
            out = out + [f + axis for f in out]
        return out[1:]

    def device(flip):
        to = {"": tp, "c": tp_core, "y": tp_y, "cy": tp_far}["".join(a for a in "cy" if a in flip)]
        return (dp + 1 - 2 * xbit if "x" in flip else dp, to)

    def place(axes, flip):
        index = 0
        for axis in axes:
            index = index * 2 + (1 - bits[axis] if axis in flip else bits[axis])
        return index

    def sum_chain(name, buf, res, stages, recvs, recv_z, out, starts=True, extra=None):
        start, n, to, back, spans = 0, buf.shape[0], [], [], []
        count = sum(len(flips(axes)) for axes in stages)
        base = sems(2 * count + 2 * (nz - 1))
        for axes, recv in zip(stages, recvs):
            n = n // 2 ** len(axes)
            others = flips(axes)
            to.append([])
            back.append([])
            here = start + place(axes, "") * n
            kept = rows_at(here, n)
            for flip, landing in zip(others, recv):
                there = rows_at(start + place(axes, flip) * n, n)
                to[-1].append(remote(buf.at[there], landing, base, device(flip)))
                back[-1].append(remote(res.at[kept], res.at[kept], base + 1, device(flip)))
                base = base + 2
            start = here
            spans.append((start, n))
        base = base - 1
        cut = n // nz if (n // nz) % 16 == 0 else n
        share = cut != n
        piece = lambda z: rows_at(start + (z * cut if share else 0), cut)
        to_z = [
            remote(buf.at[piece(z_at(k))], recv_z.at[k - 1, :cut], base + k, dev_z(k))
            for k in range(1, nz)
        ]
        own = piece(zi)
        back_z = [
            remote(res.at[own], res.at[own], base + nz - 1 + k, dev_z(k)) for k in range(1, nz)
        ] if share else []

        def part_sum(j):
            for copy in to[j]:
                copy.wait_recv()
            for landing in recvs[j]:
                add_rows(buf, spans[j][0], landing, spans[j][1])
            if extra is not None:
                extra(spans[j])
            start_all(*(to_z if j + 1 == len(to) else to[j + 1]))

        def sum_z():
            for copy in to_z:
                copy.wait_recv()
            total = buf[own, :].astype(F32)
            for k in range(1, nz):
                total = total + recv_z[k - 1, :cut].astype(F32)
            res[own, :] = total.astype(BF16)
            start_all(*back_z)

        handed = [back_z] + back[::-1]
        follow = back[::-1] + [[out]]
        first = [functools.partial(start_all, *to[0])] if starts else []
        chain(
            name, *first, *[functools.partial(part_sum, j) for j in range(len(to))], sum_z,
            *[then(a, *b) for a, b in zip(handed, follow)],
        )
        for group in to + [to_z, back_z] + back:
            last_sends.extend(group)
        outs.append(out)
        return to[0]

    f_base = sems(5)
    f_c0 = remote(r.ct.at[0], r.fc.at[0], f_base, dev_core)
    f_c1 = remote(r.ct.at[2], r.fc.at[1], f_base + 1, dev_core)
    f_part = rows_at(xbit * (D // 2), D // 2)
    f_other = rows_at((1 - xbit) * (D // 2), D // 2)
    f_y = remote(r.ct.at[1, 0], r.fy.at[0], f_base + 2, dev_y)
    f_x = remote(r.ct.at[1, 1, f_other], r.fy.at[1, D // 2 :], f_base + 3, dev_x)
    f_xy = remote(r.ct.at[1, 1, f_part], r.fy.at[1, : D // 2], f_base + 4, dev_y)
    f_outs = [pltpu.make_async_copy(r.fo.at[g], r.fo_out.at[g], r.ls.at[3 + g]) for g in range(2)]
    last_sends, outs = [f_y, f_x, f_xy], []

    def across_up():
        f_y.wait_recv()
        add_rows(r.ct.at[3, 0], 0, r.fy.at[0], D)
        start_all(*f0)

    def plane_down():
        f_x.wait_recv()
        add_rows(r.ct.at[1, 1], xbit * (D // 2), r.fy.at[1, D // 2 :], D // 2)
        f_xy.start()

    def across_down(span):
        f_xy.wait_recv()
        add_rows(r.ct.at[3, 1], span[0], r.fy.at[1, : D // 2], span[1])

    f0 = sum_chain(
        FFN_UP, r.ct.at[3, 0], r.fo.at[0], ["x"], [[r.fx.at[0]]], r.fz.at[0], f_outs[0], False
    )
    f1 = sum_chain(
        FFN_DOWN, r.ct.at[3, 1], r.fo.at[1], ["x"], [[r.fx.at[1]]], r.fz.at[1], f_outs[1], False, across_down
    )
    steps[FFN_UP].insert(0, across_up)
    chain(FFN_ACROSS, plane_down)

    def ffn(k, s, out):
        def tile(t):
            rows = rows_at(t * T, T)
            for h in range(2):
                lanes = slice(h * (D // 2), (h + 1) * (D // 2))
                up = dot(r.hf[rows, :], r.wu[s, :, lanes])
                grad_act = dot_t(r.go[rows, :], r.wd[s, lanes, :])
                cubic = (GELU_SCALE * GELU_CUBIC) * (up * up)
                tang = jnp.tanh(up * (GELU_SCALE + cubic))
                half_up, half_t = 0.5 * up, 0.5 + 0.5 * tang
                slope = half_t + half_up * (1.0 - tang * tang) * (GELU_SCALE + 3.0 * cubic)
                r.gp[rows, lanes] = (up * half_t).astype(BF16)
                r.gp[rows, slice(D + lanes.start, D + lanes.stop)] = (grad_act * slope).astype(BF16)
            add_acc(t, dot(r.gp[rows, :D], r.wd[s]))
            add_acc(nt + t, dot_t(r.gp[rows, D : 2 * D], r.wu[s]))

        loop(FFN_TILE + k, nt, tile)

        def grads(t):
            rows = rows_at(t * T, T)
            out[0, rows, :] = dot(r.hft[rows, :], r.gp[:, D : 2 * D]).astype(BF16)
            out[1, rows, :] = dot(r.got_t[rows, :], r.gp[:, :D]).astype(BF16)

        loop(FFN_GRADS + k, D // T, grads)

    ffn(0, tp_far, r.ct.at[0])
    f_c0.start()
    ffn(1, tp_y, r.ct.at[1])
    f_c0.wait_recv()
    add_rows(r.ct.at[1, 1], 0, r.fc.at[0, 1], D)
    f_x.start()
    add_rows(r.ct.at[1, 0], 0, r.fc.at[0, 0], D)
    f_y.start()
    ffn(2, tp_core, r.ct.at[2])
    f_c1.start()
    ffn(3, tp, r.ct.at[3])
    f_c1.wait_recv()
    add_rows(r.ct.at[3, 1], 0, r.fc.at[1, 1], D)
    start_all(*f1)
    add_rows(r.ct.at[3, 0], 0, r.fc.at[1, 0], D)

    ones_row = lax.broadcasted_iota(jnp.int32, (2 * LANES, LANES), 0)
    ones_col = lax.broadcasted_iota(jnp.int32, (2 * LANES, LANES), 1)
    head_ones = (lax.div(lax.rem(ones_row, LANES), 64) == lax.div(ones_col, 64)).astype(F32).astype(BF16)
    r.gg[...] = jnp.zeros((2, 8, D), F32)

    def gn_at(c):
        return rows_at(lax.rem(c, 2) * T, T), pl.ds(pl.multiple_of(lax.div(c, 2) * T, T), T)

    def gn_of(p, c):
        at, wide_at = gn_at(c)
        return r.wd[p, at, wide_at]

    def fold(v):
        return jnp.sum(v.reshape(T // 8, 8, D), axis=0)

    for copy in w_sends:
        copy.wait_send()

    def back_middle(t):
        rows = rows_at(t * T, T)
        r.hf[rows, :] = acc(t).astype(BF16)
        res = r.res[rows, :]
        mean = jnp.mean(res, axis=-1, keepdims=True)
        cen = res - mean
        inv = lax.rsqrt(jnp.mean(cen * cen, axis=-1, keepdims=True) + NORM_EPS)
        n = cen * inv
        gh = acc(nt + t)
        r.gg[0] += fold(gh * n)
        sc = gh * r.gf[...]
        centre = jnp.mean(sc, axis=-1, keepdims=True)
        inner = jnp.mean(sc * n, axis=-1, keepdims=True)
        gres = r.go[rows, :].astype(F32) + inv * (sc - centre - n * inner)
        r.res[rows, :] = gres
        gattn = gres.astype(BF16)
        r.gp[rows, 2 * D :] = gattn
        gmi = dot_t(gattn, r.wo[...]) * r.inv[rows, :]
        w = gmi * r.mix[rows, :].astype(F32) * (-1.0)
        hi = w.astype(BF16)
        lo = (w - hi.astype(F32)).astype(BF16)
        gnum = gmi.astype(BF16)
        for p in range(npair):
            lanes = slice(p * LANES, (p + 1) * LANES)
            gden = dot(cat([hi[:, lanes], lo[:, lanes]], 1), head_ones).astype(BF16)
            at, wide_at = gn_at(t)
            r.wd[p, at, wide_at] = cat([gnum[:, lanes], gden * jnp.asarray(1.0 / 64.0, BF16)], 1)

    loop(BACK_MIDDLE, nt, back_middle)
    out_copy = pltpu.make_async_copy(r.hf, r.out, r.ls.at[13])
    out_copy.start()

    bpack, steps[STATE_GRADS], bcollect = state_exchange(1, r.own, r.bgot)

    def state_back(i):
        p, c = lax.div(i, nt), nt - 1 - lax.rem(i, nt)
        rows = rows_at(c * T, T)

        @pl.when(c == nt - 1)
        def _():
            r.sl[p * (nt + 1) + nt] = jnp.zeros((M, M), F32)

        gain = merge(dot_c(gn_of(p, c) * twice(r.use[rows, :]), r.phiq[p, rows, :]))
        state = r.sc[c] * r.sl[p * (nt + 1) + c + 1] + gain
        r.sl[p * (nt + 1) + c] = state

    bleaves = (lambda i: lax.rem(i, nt) == nt - 1), (lambda i: bpack(lax.div(i, nt), 0))

    loop(STATE_BACK, npair * nt, state_back, [bleaves])

    half = D // 2
    parts = [
        (SUM_O, 0, 0, 0, D), (SUM_Q, 1, 1, 0, D - LANES), (SUM_Q3, 2, 1, D - LANES, LANES)
    ]
    parts = parts + [(SUM_K + p, 2, 2 + p // 2, (p % 2) * half, half) for p in range(npair)]
    for i, (name, kind, g, lane, n) in enumerate(parts):
        lanes = slice(lane, lane + n)
        core_land = r.fc.at[0, g, :half, lanes] if g < 2 else r.fc.at[0, g - 2, half:, lanes]
        stages = STAGES[kind]
        recvs, at = [[core_land]], 0
        rows = D // 2
        for axes in stages[1:]:
            rows = rows // 2 ** len(axes)
            recvs.append([r.land.at[g, pl.ds(at + k * rows, rows), lanes] for k in range(2 ** len(axes) - 1)])
            at = at + rows * (2 ** len(axes) - 1)
        rz = r.land_z.at[g, :, :, lanes]
        source = r.ct.at[0 if g < 2 else 2, g % 2, :, lanes]
        sum_chain(
            name, source, r.wu.at[g, :, lanes], stages, recvs, rz,
            pltpu.make_async_copy(r.wu.at[g, :, lanes], r.grads.at[g, :, lanes], r.ls.at[5 + i]),
        )

    f_c0.wait_send()
    f_c1.wait_send()
    def out_grads():
        for t in range(D // T):
            rows = slice(t * T, (t + 1) * T)
            r.ct[0, 0, rows, :] = dot_c(r.mix[:, rows], r.gp[:, 2 * D :]).astype(BF16)

    once(OUT_GRADS, out_grads)

    def back_query(i):
        p, c = lax.div(i, nt), lax.rem(i, nt)
        rows = rows_at(c * T, T)
        vals, gn = r.vp[p, rows, :], gn_of(p, c)
        phi_q, phi_k = r.phiq[p, rows, :], r.phik[p, rows, :]
        g = dot_t(gn, cat([vals * low, vals * high], 0)).astype(BF16) * twice(r.mask[c])
        used = gn * twice(r.use[rows, :])
        gphi = cat([dot(g[:, :M], phi_k[:, :M]), dot(g[:, M:], phi_k[:, M:])], 1)
        gphi = gphi + dot(used, r.st[i])
        t = (gphi * phi_q.astype(F32)).astype(BF16)
        o = dot_t(t, r.bb[p, : 2 * LANES])
        gq = c4 * o[:, :LANES] - r.q[p, rows, :].astype(F32) * (o[:, LANES:] * 0.125)
        r.gp[rows, pl.ds(pl.multiple_of(p * LANES, LANES), LANES)] = gq.astype(BF16)

    loop(BACK_QUERY, (npair - 1) * nt, back_query)
    def query_grads(lanes):
        for t in range(D // T):
            rows = slice(t * T, (t + 1) * T)
            r.ct[0, 1, rows, lanes] = dot(r.ht[rows, :], r.gp[:, lanes]).astype(BF16)

    once(QUERY_GRADS, lambda: query_grads(slice(0, D - LANES)))

    def pair_grads(i):
        p = lax.div(i, nt)
        kv = cat(
            [r.gp[:, pl.ds(pl.multiple_of(o * D + p * LANES, LANES), LANES)] for o in (1, 2)], 1
        )
        wide_at = pl.ds(pl.multiple_of(lax.rem(p, 2) * half, half), half)
        for t in range(D // T):
            rows = slice(t * T, (t + 1) * T)
            r.ct[2, lax.div(p, 2), rows, wide_at] = dot(r.ht[rows, :], kv).astype(BF16)

    def back_key(i):
        p, c = lax.div(i, nt), lax.rem(i, nt)
        rows = rows_at(c * T, T)
        dstate = split((r.sl[p * (nt + 1) + c + 1] + r.sc[2 * nt + c] * r.tin[p]).astype(BF16))
        vals, gn = r.vp[p, rows, :], gn_of(p, c)
        phi_q, phi_k = r.phiq[p, rows, :], r.phik[p, rows, :]
        mask = twice(r.maskt[c])
        gt = cat([dot_t(vals * low, gn), dot_t(vals * high, gn)], 1).astype(BF16) * mask
        st = cat([dot_t(phi_k[:, :M], phi_q[:, :M]), dot_t(phi_k[:, M:], phi_q[:, M:])], 1)
        st = st.astype(BF16) * mask
        tail = r.tail[rows, :]
        left = vals * twice(tail)
        gphi = cat(
            [
                dot(cat([gt[:, m], left], 1), cat([phi_q[:, m], dstate[:, m]], 0))
                for m in (slice(0, M), slice(M, 2 * M))
            ],
            1,
        )
        gnum = gn[:, :LANES]
        gv = dot(st, cat([gnum * low[:, :LANES], gnum * high[:, :LANES]], 0))
        gv = gv + tail.astype(F32) * dot_t(phi_k, dstate[:LANES])
        t = (gphi * phi_k.astype(F32)).astype(BF16)
        o = dot_t(t, r.bb[p, : 2 * LANES])
        gk = c4 * o[:, :LANES] - r.k[p, rows, :].astype(F32) * (o[:, LANES:] * 0.125)
        r.gp[rows, pl.ds(pl.multiple_of(D + p * LANES, LANES), LANES)] = gk.astype(BF16)
        r.gp[rows, pl.ds(pl.multiple_of(2 * D + p * LANES, LANES), LANES)] = gv.astype(BF16)

    loop(BACK_KEY, npair * nt, back_key, [((lambda i: lax.rem(i, nt) == nt - 1), pair_grads)], bcollect)

    loop(LAST_QUERY, nt, lambda c: back_query((npair - 1) * nt + c))
    once(LAST_GRADS, lambda: query_grads(slice(D - LANES, D)))

    def back_first(t):
        rows = rows_at(t * T, T)
        gh = dot_t(r.gp[rows, :D], r.wq[...])
        gh = gh + dot_t(r.gp[rows, D : 2 * D], r.wk[...])
        gh = gh + dot_t(r.gp[rows, 2 * D :], r.wv[...])
        x = r.tok[rows, :].astype(F32)
        mean = jnp.mean(x, axis=-1, keepdims=True)
        cen = x - mean
        inv = lax.rsqrt(jnp.mean(cen * cen, axis=-1, keepdims=True) + NORM_EPS)
        n = cen * inv
        r.gg[1] += fold(gh * n)
        sc = gh * r.ga[...]
        centre = jnp.mean(sc, axis=-1, keepdims=True)
        inner = jnp.mean(sc * n, axis=-1, keepdims=True)
        r.res[rows, :] += inv * (sc - centre - n * inner)

    loop(BACK_FIRST, nt, back_first)
    gt_copy = pltpu.make_async_copy(r.res, r.gt, r.ls.at[3 + 9])
    gt_copy.start()

    g_base = sems(3 + ndp - 1)
    sums = [jnp.sum(r.gg[k], axis=0, keepdims=True) for k in range(2)]
    r.g1[...] = cat([v[:, j : j + LANES] for v in sums for j in range(0, D, LANES)], 0)
    g_tp = [remote(r.g1, r.gr.at[k - 1], g_base + k - 1, (dp, lax.rem(tp + k, 4))) for k in (1, 2, 3)]
    g_dp = [
        remote(r.g2, r.gr.at[2 + k], g_base + 2 + k, (lax.rem(dp + k, ndp), tp)) for k in range(1, ndp)
    ]
    start_all(*g_tp)

    def gains_tp():
        for copy in g_tp:
            copy.wait_recv()
        r.g2[...] = r.g1[...] + r.gr[0] + r.gr[1] + r.gr[2]
        start_all(*g_dp)

    def gains_dp():
        total = r.g2[...]
        for k in range(1, ndp):
            g_dp[k - 1].wait_recv()
            total = total + r.gr[2 + k]
        r.gout[...] = total

    chain(GAINS, gains_tp, gains_dp)
    advance(TAIL, 0)
    assert not plan and not any(steps.values())

    for copy in seg_copies + last_sends + g_tp + g_dp:
        copy.wait_send()
    for copy in outs + [out_copy, gt_copy]:
        copy.wait()
    assert used[0] <= r.ss.shape[0]


def layer(tokens, segment_ids, grad_out, w_query, w_key, w_value, w_out, w_up, w_down, gain_attn,
          gain_ffn, feature_basis):
    _, L, D = tokens.shape
    H, DH, M = feature_basis.shape
    F = w_up.shape[1]
    npair, nt = H // 2, L // T
    ndp = lax.axis_size("dp")
    nz = ndp // 2
    assert lax.axis_size("tp") == 4 and F == D and DH == 64 and M == T

    vmem, hbm = pl.BlockSpec(memory_space=pltpu.VMEM), pl.BlockSpec(memory_space=pl.ANY)
    ins = {
        "seg": (segment_ids, vmem),
        "tok_in": (tokens[0], hbm),
        "go_in": (grad_out[0], hbm),
        "wq_in": (w_query, hbm),
        "wk_in": (w_key, hbm),
        "wv_in": (w_value, hbm),
        "wo_in": (w_out, hbm),
        "wup": (w_up, hbm),
        "wdn": (w_down, hbm),
        "ga": (gain_attn[None], vmem),
        "gf": (gain_ffn[None], vmem),
        "basis_in": (feature_basis, hbm),
    }
    outs = {
        "out": ((L, D), BF16, hbm),
        "gt": ((L, D), F32, hbm),
        "fo_out": ((2, D, F), BF16, hbm),
        "grads": ((4, D, D), BF16, hbm),
        "gout": ((8, LANES), F32, vmem),
    }

    scratch = {
        "tok": ((L, D), BF16),
        "wk": ((D, D), BF16),
        "wv": ((D, D), BF16),
        "wq": ((D, D), BF16),
        "wo": ((D, D), BF16),
        "go": ((L, D), BF16),
        "sg": ((4, 1, L), jnp.int32),
        "wu": ((4, D, F), BF16),
        "wd": ((4, F, D), BF16),
        "bb": ((npair, 3 * LANES, 2 * M), BF16),
        "ht": ((D, L), BF16),
        "q": ((npair, L, LANES), BF16),
        "k": ((npair, L, LANES), BF16),
        "vp": ((npair, L, 2 * LANES), BF16),
        "sc": ((3 * nt + 8, 1, M), F32),
        "use": ((L, LANES), BF16),
        "tail": ((L, LANES), BF16),
        "mask": ((nt, T, M), BF16),
        "maskt": ((nt, T, M), BF16),
        "phik": ((npair, L, 2 * M), BF16),
        "phiq": ((npair, L, 2 * M), BF16),
        "sl": ((npair * (nt + 1), M, M), F32),
        "own": ((npair, 144, M), BF16),
        "got": ((4, npair, 144, M), BF16),
        "bgot": ((4, npair, 144, M), BF16),
        "tin": ((npair, M, M), F32),
        "st": ((npair * nt, M, 2 * M), BF16),
        "inv": ((L, D), F32),
        "mix": ((L, D), BF16),
        "res": ((L, D), F32),
        "hf": ((L, D), BF16),
        "hft": ((D, L), BF16),
        "got_t": ((D, L), BF16),
        "ct": ((4, 2, D, F), BF16),
        "fc": ((2, 2, D, F), BF16),
        "land": ((4, 192, D), BF16),
        "land_z": ((4, nz - 1, D // 8, D), BF16),
        "fy": ((2, D, F), BF16),
        "fx": ((2, D // 2, F), BF16),
        "fz": ((2, nz - 1, D // 2 // nz, F), BF16),
        "fo": ((2, D, F), BF16),
        "gg": ((2, 8, D), F32),
        "gp": ((L, 3 * D), BF16),
        "g1": ((8, LANES), F32),
        "g2": ((8, LANES), F32),
        "gr": ((3 + ndp - 1, 8, LANES), F32),
    }
    n_sems = 40 + 6 * npair + ndp + (4 + npair) * (10 + 2 * (nz - 1)) + 5 * (nz - 1)
    names = list(ins) + list(outs) + list(scratch) + ["ls", "ss", "rs"]
    res = pl.pallas_call(
        functools.partial(layer_kernel, nz, names),
        out_shape=[jax.ShapeDtypeStruct(s, d) for s, d, _ in outs.values()],
        in_specs=[spec for _, spec in ins.values()],
        out_specs=[spec for _, _, spec in outs.values()],
        scratch_shapes=[pltpu.VMEM(s, d) for s, d in scratch.values()]
        + [
            pltpu.SemaphoreType.DMA((28,)),
            pltpu.SemaphoreType.DMA((n_sems,)),
            pltpu.SemaphoreType.DMA((n_sems,)),
        ],
        name="layer",
        compiler_params=pltpu.CompilerParams(
            collective_id=0, has_side_effects=True, vmem_limit_bytes=67043328
        ),
    )(*[a for a, _ in ins.values()])
    return hand_out(*res)


def hand_out_kernel(out, gt, up, down, grads, gains, *refs):
    o_out, o_gt, o_query, o_key, o_value, o_proj, o_up, o_down, o_attn, o_ffn = refs
    o_out[0] = out[...]
    o_gt[0] = gt[...]
    o_up[...] = up[0].astype(F32)
    o_down[...] = down[0].astype(F32).T
    o_proj[...] = grads[0].astype(F32)
    o_query[...] = grads[1].astype(F32)
    for p in range(grads.shape[2] // LANES):
        lanes = slice(p * LANES, (p + 1) * LANES)
        at = (p % 2) * 2 * LANES
        o_key[:, lanes] = grads[2 + p // 2, :, at : at + LANES].astype(F32)
        o_value[:, lanes] = grads[2 + p // 2, :, at + LANES : at + 2 * LANES].astype(F32)
    for j in range(4):
        lanes = slice(j * LANES, (j + 1) * LANES)
        o_ffn[:, lanes] = gains[j : j + 1, :]
        o_attn[:, lanes] = gains[4 + j : 5 + j, :]


def hand_out(out, gt, fo, grads, gains):
    (L, D), steps = out.shape, 2
    lr, dr = L // steps, D // steps
    tall = pl.BlockSpec((1, lr, D), lambda i: (0, i, 0))
    flat = pl.BlockSpec((dr, D), lambda i: (i, 0))
    row = pl.BlockSpec((1, D), lambda i: (0, 0))
    f32 = lambda *shape: jax.ShapeDtypeStruct(shape, F32)
    res = pl.pallas_call(
        hand_out_kernel,
        grid=(steps,),
        in_specs=[
            pl.BlockSpec((lr, D), lambda i: (i, 0)),
            pl.BlockSpec((lr, D), lambda i: (i, 0)),
            pl.BlockSpec((1, dr, D), lambda i: (0, i, 0)),
            pl.BlockSpec((1, D, dr), lambda i: (1, 0, i)),
            pl.BlockSpec((4, dr, D), lambda i: (0, i, 0)),
            pl.BlockSpec((8, LANES), lambda i: (0, 0)),
        ],
        out_specs=[tall, tall, flat, flat, flat, flat, flat, flat, row, row],
        out_shape=[jax.ShapeDtypeStruct((1, L, D), BF16), f32(1, L, D)]
        + [f32(D, D)] * 6 + [f32(1, D)] * 2,
        name="hand_out", compiler_params=pltpu.CompilerParams(vmem_limit_bytes=60000000),
    )(out, gt, fo, fo, grads, gains)
    return (*res[:8], res[8][0], res[9][0])


def solution(mesh):
    whole = P()
    in_specs = (
        P("dp", "tp", None), P("dp", "tp"), P("dp", "tp", None), whole, whole, whole, whole,
        P(None, "tp"), P("tp", None), whole, whole, whole,
    )
    out_specs = (
        P("dp", "tp", None), P("dp", "tp", None), whole, whole, whole, whole,
        P(None, "tp"), P("tp", None), whole, whole,
    )
    return jax.shard_map(layer, mesh=mesh, in_specs=in_specs, out_specs=out_specs, check_vma=False)
```
